32 devices in a mesh: fsdp: 8 (over z, y), seq: 4 (over x, core).
Axes of the slice: x: 2, y: 2, z: 4, core: 2. Of those that a mesh axis runs over, the one named last changes fastest.
Arguments:
- tokens: bfloat16 [16, 1024, 1024], P('fsdp', 'seq'), may hold values from -6 to 6
- first_gain: float32 [1024], replicated, may hold values from 0.5 to 1.5
- first_shift: float32 [1024], replicated, may hold values from -1 to 1
- attention_weight: bfloat16 [1024, 3072], P('fsdp', 'seq'), may hold values from -0.25 to 0.25
- attention_bias: float32 [3072], replicated, may hold values from -1.5 to 1.5
- output_weight: bfloat16 [1024, 1024], P('fsdp', 'seq'), may hold values from -1.5 to 1.5
- output_bias: float32 [1024], replicated, may hold values from -1 to 1
- second_gain: float32 [1024], replicated, may hold values from 0.5 to 1.5
- second_shift: float32 [1024], replicated, may hold values from -1 to 1
- expand_weight: bfloat16 [1024, 4096], P('fsdp', 'seq'), may hold values from -0.1875 to 0.1875
- expand_bias: float32 [4096], replicated, may hold values from -1 to 1
- contract_weight: bfloat16 [4096, 1024], P('fsdp', 'seq'), may hold values from -0.1875 to 0.1875
- contract_bias: float32 [1024], replicated, may hold values from -1 to 1
- cotangent: bfloat16 [16, 1024, 1024], P('fsdp', 'seq'), may hold values from -6 to 6
- threshold: float32 [1], replicated, may hold values from 3 to 6
Outputs:
- block_output: bfloat16 [16, 1024, 1024], P('fsdp', 'seq')
- input_grad: float32 [16, 1024, 1024], P('fsdp', 'seq')
- grad_first_gain: float32 [1024], replicated
- grad_first_shift: float32 [1024], replicated
- grad_attention_weight: float32 [1024, 3072], P('fsdp', 'seq')
- grad_attention_bias: float32 [3072], replicated
- grad_output_weight: float32 [1024, 1024], P('fsdp', 'seq')
- grad_output_bias: float32 [1024], replicated
- grad_second_gain: float32 [1024], replicated
- grad_second_shift: float32 [1024], replicated
- grad_expand_weight: float32 [1024, 4096], P('fsdp', 'seq')
- grad_expand_bias: float32 [4096], replicated
- grad_contract_weight: float32 [4096, 1024], P('fsdp', 'seq')
- grad_contract_bias: float32 [1024], replicated
- head_peak: float32 [16], P('seq')
- clipped_weight: float32 [1024, 3072], P('fsdp', 'seq')
- clipped_bias: float32 [3072], P('seq')
The draws below stay inside these ranges and needn't reach their ends.
All inputs are finite; a program needn't handle non-finite values.
Results may differ from the reference program's by a relative error of at most 0.018.
Values may be sent and summed in bfloat16 or wider, within the bound.
No kernel may reach another device: no remote copies, remote signals or barrier semaphores. Data moves between devices by JAX's collectives and lax.ppermute only.
A program may use at most 320 MiB of HBM per device.

```python
import jax
import jax.numpy as jnp
from jax import lax

D = 1024
H = 16
HD = 64
FF = 4096
LEN = 1024
SEQS = 16


def shard_levels(stream_key, dims, shards, low, high):
    loudness, own = 1.0, jax.random.fold_in(stream_key, 6)
    for axis_at, blocks in shards:
        heights = jnp.exp(jax.random.uniform(jax.random.fold_in(own, axis_at), (blocks,), jnp.float32, low / len(shards), high / len(shards)))
        loudness = loudness * jnp.repeat(heights, dims[axis_at] // blocks).reshape([-1 if axis == axis_at else 1 for axis in range(len(dims))])
    return loudness


def gaussian(rng, shape, width, limit, cuts=(), kind=jnp.bfloat16):
    loudness = shard_levels(rng, shape, cuts, -0.22, 0.18) if cuts else 1.0
    array = jax.random.normal(rng, shape, jnp.float32) * width * loudness
    return jnp.minimum(jnp.maximum(array, -limit), limit).astype(kind)


def setup_inputs(seed: int = 0) -> dict:
    seeds = jax.random.split(jax.random.key(seed), 16)
    tokens = gaussian(seeds[0], (SEQS, LEN, D), 1.0, 6.0, ((0, 8), (1, 4)))
    first_gain = jnp.clip(1.0 + 0.1 * jax.random.normal(seeds[1], (D,), jnp.float32), 0.5, 1.5)
    first_shift = gaussian(seeds[2], (D,), 0.2, 1.0, (), jnp.float32)
    attention_weight = gaussian(seeds[3], (D, 3 * D), (D // 2) ** -0.5, 0.25, ((0, 8), (1, 4)))
    attention_bias = gaussian(seeds[4], (3 * D,), 0.3, 1.5, (), jnp.float32)
    output_weight = gaussian(seeds[5], (D, D), (D // 64) ** -0.5, 1.5, ((0, 8), (1, 4)))
    output_bias = gaussian(seeds[6], (D,), 0.2, 1.0, (), jnp.float32)
    second_gain = jnp.clip(1.0 + 0.1 * jax.random.normal(seeds[7], (D,), jnp.float32), 0.5, 1.5)
    second_shift = gaussian(seeds[8], (D,), 0.2, 1.0, (), jnp.float32)
    expand_weight = gaussian(seeds[9], (D, FF), D ** -0.5, 0.1875, ((0, 8), (1, 4)))
    expand_bias = gaussian(seeds[10], (FF,), 0.2, 1.0, (), jnp.float32)
    contract_weight = gaussian(seeds[11], (FF, D), (FF // 4) ** -0.5, 0.1875, ((0, 8), (1, 4)))
    contract_bias = gaussian(seeds[12], (D,), 0.2, 1.0, (), jnp.float32)
    cotangent = gaussian(seeds[13], (SEQS, LEN, D), 1.0, 6.0, ((0, 8), (1, 4)))
    threshold = jnp.clip(jax.random.uniform(seeds[14], (1,), jnp.float32, 3.0, 6.0), 3.0, 6.0)
    return dict(tokens=tokens, first_gain=first_gain, first_shift=first_shift, attention_weight=attention_weight, attention_bias=attention_bias, output_weight=output_weight, output_bias=output_bias, second_gain=second_gain, second_shift=second_shift, expand_weight=expand_weight, expand_bias=expand_bias, contract_weight=contract_weight, contract_bias=contract_bias, cotangent=cotangent, threshold=threshold)


@jax.custom_vjp
def low(v):
    return lax.optimization_barrier(v.astype(jnp.bfloat16)).astype(jnp.float32)

@jax.custom_vjp
def low_back(v):
    return v

def low_keep(v):
    return (low(v), None)

def low_pass(kept, grad):
    return (grad,)

def back_keep(v):
    return (v, None)

def back_low(kept, grad):
    return (low(grad),)
low.defvjp(low_keep, low_pass)
low_back.defvjp(back_keep, back_low)
precise = lax.Precision.HIGHEST

def layer_norm(values, gain, shift):
    centered = values - lax.optimization_barrier(jnp.mean(values, axis=-1, keepdims=True))
    variance = lax.optimization_barrier(jnp.mean(centered * centered, axis=-1, keepdims=True))
    return centered * lax.rsqrt(variance + 1e-05) * gain + shift

def project(values, matrix):
    return jnp.einsum('std,de->ste', values, matrix, precision=precise)

def attend_sequence(packed):
    queries, keys_all, values_all = packed
    logits = jnp.einsum('qhd,khd->hqk', queries, keys_all, precision=precise) * HD ** (-0.5)
    logits = low_back(logits)
    length = logits.shape[-1]
    causal_mask = jnp.arange(length)[None, :] <= jnp.arange(length)[:, None]
    logits = jnp.where(causal_mask[None], logits, -jnp.inf)
    peak_value = lax.optimization_barrier(jnp.max(logits, axis=(1, 2)))
    probabilities = low(jax.nn.softmax(logits, axis=-1))
    attended = jnp.einsum('hqk,khd->qhd', probabilities, values_all, precision=precise)
    return (attended, peak_value)

def forward(tokens, first_gain, first_shift, attention_weight, attention_bias, output_weight, output_bias, second_gain, second_shift, expand_weight, expand_bias, contract_weight, contract_bias):
    normed_first = low(layer_norm(tokens, first_gain, first_shift))
    mixed = low_back(low(project(normed_first, attention_weight) + attention_bias))
    grouped = mixed.reshape(SEQS, LEN, H, 3, HD)
    attended, peaks = lax.map(jax.checkpoint(attend_sequence), (grouped[:, :, :, 0], grouped[:, :, :, 1], grouped[:, :, :, 2]))
    attended = low_back(low(attended)).reshape(SEQS, LEN, D)
    residual = tokens + low_back(project(attended, output_weight) + output_bias)
    normed_second = low(layer_norm(residual, second_gain, second_shift))
    hidden = low_back(project(normed_second, expand_weight) + expand_bias)
    active = low(jax.nn.gelu(hidden, approximate=True))
    result = residual + project(active, contract_weight) + contract_bias
    return (result, lax.optimization_barrier(jnp.max(peaks, axis=0)))

def reference(tokens, first_gain, first_shift, attention_weight, attention_bias, output_weight, output_bias, second_gain, second_shift, expand_weight, expand_bias, contract_weight, contract_bias, cotangent, threshold):
    result, pullback, head_peak = jax.vjp(forward, tokens.astype(jnp.float32), first_gain.astype(jnp.float32), first_shift.astype(jnp.float32), attention_weight.astype(jnp.float32), attention_bias.astype(jnp.float32), output_weight.astype(jnp.float32), output_bias.astype(jnp.float32), second_gain.astype(jnp.float32), second_shift.astype(jnp.float32), expand_weight.astype(jnp.float32), expand_bias.astype(jnp.float32), contract_weight.astype(jnp.float32), contract_bias.astype(jnp.float32), has_aux=True)
    grads = pullback(cotangent.astype(jnp.float32))
    factor = jnp.sqrt(threshold[0] / jnp.maximum(head_peak, threshold[0]))
    multiplier = jnp.stack([factor, factor, jnp.ones_like(factor)], axis=1)
    clipped_weight = (attention_weight.astype(jnp.float32).reshape(D, H, 3, HD) * multiplier[None, :, :, None]).reshape(D, 3 * D)
    clipped_bias = (attention_bias.astype(jnp.float32).reshape(H, 3, HD) * multiplier[:, :, None]).reshape(3 * D)
    return (result.astype(jnp.bfloat16), grads[0], grads[1], grads[2], grads[3], grads[4], grads[5], grads[6], grads[7], grads[8], grads[9], grads[10], grads[11], grads[12], head_peak, clipped_weight, clipped_bias)
```

```python
import functools
import math

import jax
import jax.numpy as jnp
from jax import lax
from jax.experimental import pallas as pl
from jax.experimental.pallas import tpu as pltpu
from jax.sharding import PartitionSpec as P

HEAD = 64
LOG2E = math.log2(math.e)
BF = jnp.bfloat16
F32 = jnp.float32


def swap(value, axis, size, bit):
    return lax.ppermute(value, axis, [(i, i ^ bit) for i in range(size)])


def bits_of(size):
    return [1 << p for p in range(size.bit_length() - 1)]


def gather_slots(value, axis, size):
    slots = {0: value}
    for bit in reversed(bits_of(size)):
        for k in list(slots):
            slots[k | bit] = swap(slots[k], axis, size, bit)
    return [slots[k] for k in range(size)]


def scatter_slots(partial, axis, size):
    for bit in bits_of(size):
        pairs = partial.reshape(-1, 2, *partial.shape[1:])
        came = swap(pairs[:, 1].astype(BF), axis, size, bit)
        partial = pairs[:, 0] + came.astype(F32)
    return partial[0]


def gather_rows(value, index, axis, size):
    value = value[None]
    for bit in reversed(bits_of(size)):
        came = swap(value, axis, size, bit)
        value = jnp.where(
            (index & bit) != 0,
            jnp.stack([came, value], axis=1),
            jnp.stack([value, came], axis=1),
        ).reshape(-1, *value.shape[1:])
    return value


def scatter_rows(value, index, axis, size):
    for bit in bits_of(size):
        pairs = value.reshape(-1, 2, *value.shape[1:])
        own = ((index & bit) != 0).astype(jnp.int32)
        sent = lax.dynamic_index_in_dim(pairs, 1 - own, 1, keepdims=False).astype(BF)
        kept = lax.dynamic_index_in_dim(pairs, own, 1, keepdims=False).astype(F32)
        value = kept + swap(sent, axis, size, bit).astype(F32)
    return value[0]


def exchange_slots(slots, axis, size):
    return [slots[0]] + [swap(slots[k], axis, size, k) for k in range(1, size)]


def all_sum(value, axes):
    for axis, size in axes:
        for bit in bits_of(size):
            value = value + swap(value, axis, size, bit)
    return value


def dot(a, b, dims):
    return lax.dot_general(a, b, (dims, ((), ())), preferred_element_type=F32)


def head_mask(width, head):
    lanes = lax.broadcasted_iota(jnp.int32, (1, width), 1)
    return (lanes // HEAD) == head


def causal(tile):
    keys = lax.broadcasted_iota(jnp.int32, (tile, tile), 0)
    queries = lax.broadcasted_iota(jnp.int32, (tile, tile), 1)
    return keys <= queries


def forward_kernel(slots, tile, width, at_ref, q_ref, k_ref, v_ref, o_ref, lse_ref, peak_ref, k_s, vt_s):
    here = at_ref[0]
    scale = HEAD**-0.5
    factor = scale * LOG2E
    heads = width // HEAD
    for i in range(slots):
        rows = slice(i * tile, (i + 1) * tile)
        k_s[rows, :] = k_ref[i ^ here]
        vt_s[:, rows] = v_ref[i ^ here].T

    def scores(q, start, stop, masked):
        found = dot(k_s[start:stop], q, ((1,), (1,)))
        if masked:
            edge = jnp.where(causal(tile), found[stop - start - tile :], -jnp.inf)
            if stop - start == tile:
                return edge
            return jnp.concatenate([found[: stop - start - tile], edge], axis=0)
        return found

    peaks = [None] * heads
    for i in range(slots):
        q_tile = q_ref[i ^ here]
        outs = []
        for h in range(heads):
            q = jnp.where(head_mask(width, h), q_tile, jnp.zeros_like(q_tile))
            top = total = acc = None
            limit = (i + 1) * tile
            step = min(limit, 4 * tile)
            for start in range(0, limit, step):
                stop = min(start + step, limit)
                found = scores(q, start, stop, stop == limit)
                high = jnp.max(found, axis=0, keepdims=True)
                new_top = high if top is None else jnp.maximum(top, high)
                grown = jnp.exp2((found - new_top) * factor)
                part = jnp.sum(grown, axis=0, keepdims=True)
                mixed = dot(
                    vt_s[h * HEAD : (h + 1) * HEAD, start:stop], grown.astype(BF), ((1,), (0,))
                )
                if top is None:
                    total, acc = part, mixed
                else:
                    shrink = jnp.exp2((top - new_top) * factor)
                    total = total * shrink + part
                    acc = acc * shrink + mixed
                top = new_top
            outs.append(acc / total)
            lse_ref[h : h + 1, i * tile : (i + 1) * tile] = top * factor + jnp.log2(total)
            peaks[h] = top if peaks[h] is None else jnp.maximum(peaks[h], top)
        joined = outs[0] if heads == 1 else jnp.concatenate(outs, axis=0)
        o_ref[i ^ here] = joined.T.astype(BF)
    for h in range(heads):
        peak_ref[h : h + 1, :] = peaks[h] * scale


def backward_kernel(
    slots, tile, width, at_ref, q_ref, k_ref, v_ref, o_ref, g_ref, lse_ref, dq_ref, dk_ref, dv_ref,
    k_s, v_s, kt_s, dk_s, dv_s,
):
    here = at_ref[0]
    scale = HEAD**-0.5
    factor = scale * LOG2E
    heads = width // HEAD
    for i in range(slots):
        rows = slice(i * tile, (i + 1) * tile)
        k_s[rows, :] = k_ref[i ^ here]
        v_s[rows, :] = v_ref[i ^ here]
        kt_s[:, rows] = k_ref[i ^ here].T
    for i in reversed(range(slots)):
        q_tile = q_ref[i ^ here]
        g_tile = g_ref[i ^ here]
        inner = (g_tile.astype(F32) * o_ref[i ^ here].astype(F32)).T
        outs = []
        limit = (i + 1) * tile
        for h in range(heads):
            mask = head_mask(width, h)
            q = jnp.where(mask, q_tile, jnp.zeros_like(q_tile))
            g = jnp.where(mask, g_tile, jnp.zeros_like(g_tile))
            delta = jnp.sum(inner[h * HEAD : (h + 1) * HEAD], axis=0, keepdims=True)
            lse = lse_ref[h : h + 1, i * tile : (i + 1) * tile]
            acc = None
            step = min(limit, 4 * tile)
            for start in range(0, limit, step):
                stop = min(start + step, limit)
                found = dot(k_s[start:stop], q, ((1,), (1,)))
                probs = jnp.exp2(found * factor - lse)
                if stop == limit:
                    edge = jnp.where(causal(tile), probs[stop - start - tile :], 0.0)
                    if stop - start == tile:
                        probs = edge
                    else:
                        probs = jnp.concatenate([probs[: stop - start - tile], edge], axis=0)
                spread = dot(v_s[start:stop], g, ((1,), (1,)))
                logit_cot = (probs * (spread - delta)).astype(BF)
                dv_part = dot(probs.astype(BF), g, ((1,), (0,)))
                dk_part = dot(logit_cot, q, ((1,), (0,)))
                if i == slots - 1 and h == 0:
                    dv_s[start:stop] = dv_part
                    dk_s[start:stop] = dk_part
                else:
                    dv_s[start:stop] += dv_part
                    dk_s[start:stop] += dk_part
                dq_part = dot(kt_s[h * HEAD : (h + 1) * HEAD, start:stop], logit_cot, ((1,), (0,)))
                acc = dq_part if acc is None else acc + dq_part
            outs.append(acc)
        joined = outs[0] if heads == 1 else jnp.concatenate(outs, axis=0)
        dq_ref[i ^ here] = (joined.T * scale).astype(BF)
    for i in range(slots):
        rows = slice(i * tile, (i + 1) * tile)
        dk_ref[i ^ here] = (dk_s[rows] * scale).astype(BF)
        dv_ref[i ^ here] = dv_s[rows].astype(BF)


def part_specs(mixed, width, groups):
    slots, tile, columns = mixed.shape
    every = columns // 3
    if width % 128 == 0:
        return [mixed] * 3, [
            pl.BlockSpec((slots, tile, width), lambda g, at, j=j: (0, 0, j * groups + g))
            for j in range(3)
        ]
    pieces = [mixed[..., j * every : (j + 1) * every] for j in range(3)]
    return pieces, [pl.BlockSpec((slots, tile, width), lambda g, at: (0, 0, g))] * 3


def group_width(mixed):
    every = mixed.shape[-1] // 3
    width = 128 if every % 128 == 0 else every
    return every, width, every // width


def attend_forward(at, mixed):
    slots, tile, _ = mixed.shape
    every, width, groups = group_width(mixed)
    heads = width // HEAD
    length = slots * tile
    operands, specs = part_specs(mixed, width, groups)
    out, lse, peak = pl.pallas_call(
        functools.partial(forward_kernel, slots, tile, width),
        out_shape=(
            jax.ShapeDtypeStruct((slots, tile, every), BF),
            jax.ShapeDtypeStruct((groups, heads, length), F32),
            jax.ShapeDtypeStruct((groups, heads, tile), F32),
        ),
        grid_spec=pltpu.PrefetchScalarGridSpec(
            num_scalar_prefetch=1,
            grid=(groups,),
            in_specs=specs,
            out_specs=(
                pl.BlockSpec((slots, tile, width), lambda g, at: (0, 0, g)),
                pl.BlockSpec((None, heads, length), lambda g, at: (g, 0, 0)),
                pl.BlockSpec((None, heads, tile), lambda g, at: (g, 0, 0)),
            ),
            scratch_shapes=[pltpu.VMEM((length, width), BF), pltpu.VMEM((width, length), BF)],
        ),
        compiler_params=pltpu.CompilerParams(vmem_limit_bytes=40 << 20),
        cost_estimate=pl.CostEstimate(
            flops=2 * length * length * every * 4,
            transcendentals=length * length * every // HEAD // 2,
            bytes_accessed=8 * length * every,
        ),
        name="attend_forward",
    )(at, *operands)
    return out, lse, jnp.max(peak, axis=-1).reshape(-1)


def attend_backward(at, mixed, out, cot, lse):
    slots, tile, _ = mixed.shape
    every, width, groups = group_width(mixed)
    heads = width // HEAD
    length = slots * tile
    operands, specs = part_specs(mixed, width, groups)
    block = pl.BlockSpec((slots, tile, width), lambda g, at: (0, 0, g))
    shape = jax.ShapeDtypeStruct((slots, tile, every), BF)
    return pl.pallas_call(
        functools.partial(backward_kernel, slots, tile, width),
        out_shape=(shape, shape, shape),
        grid_spec=pltpu.PrefetchScalarGridSpec(
            num_scalar_prefetch=1,
            grid=(groups,),
            in_specs=specs
            + [block, block, pl.BlockSpec((None, heads, length), lambda g, at: (g, 0, 0))],
            out_specs=(block, block, block),
            scratch_shapes=[
                pltpu.VMEM((length, width), BF),
                pltpu.VMEM((length, width), BF),
                pltpu.VMEM((width, length), BF),
                pltpu.VMEM((length, width), F32),
                pltpu.VMEM((length, width), F32),
            ],
        ),
        compiler_params=pltpu.CompilerParams(vmem_limit_bytes=40 << 20),
        cost_estimate=pl.CostEstimate(
            flops=2 * length * length * every * 10,
            transcendentals=length * length * every // HEAD // 2,
            bytes_accessed=16 * length * every,
        ),
        name="attend_backward",
    )(at, *operands, out, cot, lse)


def norm_stats(values):
    centered = values - jnp.mean(values, axis=-1, keepdims=True)
    rate = lax.rsqrt(jnp.mean(centered * centered, axis=-1, keepdims=True) + 1e-05)
    return centered * rate, rate


def norm_back(cot, unit, rate, gain):
    e = cot * gain
    return rate * (
        e
        - jnp.mean(e, axis=-1, keepdims=True)
        - unit * jnp.mean(e * unit, axis=-1, keepdims=True)
    )


def gelu_pair(v):
    k0 = math.sqrt(2.0 / math.pi)
    square = v * v
    t = jnp.tanh(k0 * v * (1.0 + 0.044715 * square))
    half = 0.5 * (1.0 + t)
    slope = half + 0.5 * v * (1.0 - t * t) * (k0 * (1.0 + 3.0 * 0.044715 * square))
    return v * half, slope


def body(
    n, shards,
    tokens, first_gain, first_shift, attention_weight, attention_bias, output_weight, output_bias,
    second_gain, second_shift, expand_weight, expand_bias, contract_weight, contract_bias,
    cotangent, threshold,
):
    batch, tile, width = tokens.shape
    rows, qkv = attention_weight.shape
    every = qkv // 3
    heads = every // HEAD
    inner_rows = contract_weight.shape[0]
    inner = inner_rows * shards // n
    piece = inner_rows // n
    ratio = shards // n
    strip = output_weight.shape[1]
    s = lax.axis_index("seq")
    f = lax.axis_index("fsdp")
    at = s.astype(jnp.int32).reshape(1)

    def by_kind(v):
        lead = v.shape[:-1]
        return jnp.swapaxes(v.reshape(*lead, heads, 3, HEAD), -3, -2).reshape(*lead, qkv)

    def by_head(v):
        lead = v.shape[:-1]
        return jnp.swapaxes(v.reshape(*lead, 3, heads, HEAD), -3, -2).reshape(*lead, qkv)

    mixing = gather_rows(by_kind(attention_weight), f, "fsdp", shards).reshape(width, qkv)
    to_seq = jnp.concatenate(
        [
            jnp.swapaxes(expand_weight.reshape(rows, ratio, n, piece), 1, 2)
            .swapaxes(0, 1)
            .reshape(n, -1, strip),
            contract_weight.reshape(n, piece, strip),
            jnp.broadcast_to(output_weight[None], (n, rows, strip)),
        ],
        axis=1,
    )
    from_seq = lax.all_to_all(to_seq, "seq", 0, 0, tiled=True)
    cut = rows * ratio * piece // strip
    expand_rows = (
        from_seq[:, :cut].reshape(n, rows, ratio * piece).swapaxes(0, 1).reshape(rows, inner)
    )
    contract_rows = from_seq[:, cut : cut + piece].swapaxes(0, 1).reshape(piece, width)
    output_rows = from_seq[:, cut + piece :].swapaxes(0, 1).reshape(rows, width)
    output_full = gather_rows(output_rows, f, "fsdp", shards).reshape(n, every, width)
    output_full = jnp.concatenate(
        [lax.dynamic_index_in_dim(output_full, s ^ k, 0, keepdims=False) for k in range(n)]
    )
    if piece == rows:
        both = gather_rows(jnp.stack([expand_rows, contract_rows]), f, "fsdp", shards)
        expand = both[:, 0].reshape(width, inner)
        contract = both[:, 1].reshape(inner, width)
    else:
        expand = gather_rows(expand_rows, f, "fsdp", shards).reshape(width, inner)
        contract = gather_rows(contract_rows, f, "fsdp", shards).reshape(inner, width)

    mixing_bias = by_kind(lax.dynamic_slice_in_dim(attention_bias, s * qkv, qkv))
    inner_bias = lax.dynamic_index_in_dim(
        expand_bias.reshape(shards, n, piece), s, axis=1, keepdims=False
    ).reshape(inner)

    streams = range(batch)
    first_unit, first_rate, normed_first, mixed, attended_own, lse, peaks = ([None] * batch for _ in range(7))
    attended, residual = [None] * batch, [None] * batch
    second_unit, second_rate, normed_second = ([None] * batch for _ in range(3))
    cot_all = [None] * batch
    for b in streams:
        first_unit[b], first_rate[b] = norm_stats(tokens[b].astype(F32))
        own = (first_unit[b] * first_gain + first_shift).astype(BF)
        normed_first[b] = jnp.concatenate(gather_slots(own, "seq", n), axis=0)
    for b in streams:
        cot_all[b] = jnp.concatenate(gather_slots(cotangent[b], "seq", n), axis=0)
    for b in streams:
        mixed[b] = (
            (dot(normed_first[b], mixing, ((1,), (0,))) + mixing_bias)
            .astype(BF)
            .reshape(n, tile, qkv)
        )
        attended_own[b], lse[b], peaks[b] = attend_forward(at, mixed[b])
        attended[b] = jnp.concatenate(
            exchange_slots([attended_own[b][k] for k in range(n)], "seq", n), axis=-1
        )
    for b in streams:
        residual[b] = (
            tokens[b].astype(F32) + dot(attended[b], output_full, ((1,), (0,))) + output_bias
        )
        second_unit[b], second_rate[b] = norm_stats(residual[b])
        own = (second_unit[b] * second_gain + second_shift).astype(BF)
        normed_second[b] = jnp.concatenate(gather_slots(own, "seq", n), axis=0)

    active, hidden_cot, residual_cot, block_output = ([None] * batch for _ in range(4))
    branch_cot, heads_cot = [None] * batch, [None] * batch
    gains = []
    for b in streams:
        hidden = dot(normed_second[b], expand, ((1,), (0,))) + inner_bias
        value, slope = gelu_pair(hidden)
        active[b] = value.astype(BF)
        hidden_cot[b] = (dot(cot_all[b], contract, ((1,), (1,))) * slope).astype(BF)
        partial = dot(hidden_cot[b], expand, ((1,), (1,))).reshape(n, tile, width)
        second_cot = scatter_slots(partial, "seq", n)
        residual_cot[b] = cotangent[b].astype(F32) + norm_back(
            second_cot, second_unit[b], second_rate[b], second_gain
        )
        branch_cot[b] = residual_cot[b].astype(BF)
        gains.append(
            (
                jnp.sum(second_cot * second_unit[b], axis=0),
                jnp.sum(second_cot, axis=0),
                jnp.sum(branch_cot[b].astype(F32), axis=0),
                jnp.sum(cotangent[b].astype(F32), axis=0),
                jnp.sum(hidden_cot[b].astype(F32), axis=0),
            )
        )
        own_cot = dot(branch_cot[b], output_full, ((1,), (1,))).astype(BF)
        heads_cot[b] = jnp.stack(
            exchange_slots([own_cot[:, k * every : (k + 1) * every] for k in range(n)], "seq", n)
        )
    for b in streams:
        partial_out = dot(active[b], contract, ((1,), (0,))).reshape(n, tile, width)
        total = scatter_slots(partial_out, "seq", n)
        block_output[b] = (residual[b] + total + contract_bias).astype(BF)

    def over_streams(left, right):
        return functools.reduce(
            jnp.add, [dot(left[b], right[b], ((0,), (0,))) for b in streams]
        )

    def reduce_rows(grad):
        return scatter_rows(grad.reshape(shards, -1, grad.shape[-1]), f, "fsdp", shards)

    if piece == rows:
        joined = jnp.stack(
            [
                over_streams(normed_second, hidden_cot).astype(BF).reshape(shards, rows, inner),
                over_streams(active, cot_all).astype(BF).reshape(shards, piece, width),
            ],
            axis=1,
        )
        grad_expand, grad_contract = scatter_rows(joined, f, "fsdp", shards)
    else:
        grad_expand = reduce_rows(over_streams(normed_second, hidden_cot))
        grad_contract = reduce_rows(over_streams(active, cot_all))
    by_slot = over_streams(attended, branch_cot).astype(BF).reshape(n, every, width)
    grad_output = reduce_rows(
        jnp.concatenate(
            [lax.dynamic_index_in_dim(by_slot, s ^ k, 0, keepdims=False) for k in range(n)]
        )
    )
    back = lax.all_to_all(
        jnp.concatenate(
            [
                grad_expand.astype(BF)
                .reshape(rows, n, ratio * piece)
                .swapaxes(0, 1)
                .reshape(n, cut, strip),
                grad_contract.astype(BF).reshape(piece, n, strip).swapaxes(0, 1),
            ],
            axis=1,
        ),
        "seq",
        0,
        0,
        tiled=True,
    )
    grad_expand_own = (
        back[:, :cut]
        .reshape(n, rows, ratio, piece)
        .transpose(1, 2, 0, 3)
        .reshape(rows, ratio * n * piece)
        .astype(F32)
    )
    grad_contract_own = back[:, cut:].reshape(inner_rows, strip).astype(F32)
    grad_output_own = scatter_rows(
        grad_output.reshape(rows, n, strip).swapaxes(0, 1), s, "seq", n
    )

    mixed_cot, input_grad = [None] * batch, [None] * batch
    tail = []
    for b in streams:
        parts = attend_backward(at, mixed[b], attended_own[b], heads_cot[b], lse[b])
        mixed_cot[b] = jnp.concatenate(parts, axis=-1).reshape(n * tile, qkv)
        partial = dot(mixed_cot[b], mixing, ((1,), (1,))).reshape(n, tile, width)
        first_cot = scatter_slots(partial, "seq", n)
        input_grad[b] = residual_cot[b] + norm_back(
            first_cot, first_unit[b], first_rate[b], first_gain
        )
        tail.append(
            (
                jnp.sum(first_cot * first_unit[b], axis=0),
                jnp.sum(first_cot, axis=0),
                jnp.sum(mixed_cot[b].astype(F32), axis=0),
            )
        )
    grad_mixing = by_head(reduce_rows(over_streams(normed_first, mixed_cot).astype(BF)))

    axes = (("seq", n), ("fsdp", shards))
    mine = (jnp.arange(n) == s).astype(F32)
    second_gain_sum, second_shift_sum, output_sum, contract_sum, inner_sum = (
        functools.reduce(jnp.add, [g[j] for g in gains]) for j in range(5)
    )
    spread_inner = (inner_sum.reshape(shards, 1, piece) * mine[None, :, None]).reshape(-1)
    early = all_sum(
        jnp.concatenate(
            [second_gain_sum, second_shift_sum, output_sum, contract_sum, spread_inner]
        ).reshape(-1, 128),
        axes,
    ).reshape(-1)
    first_gain_sum, first_shift_sum, mixing_sum = (
        functools.reduce(jnp.add, [g[j] for g in tail]) for j in range(3)
    )
    spread_mixing = (mine[:, None] * by_head(mixing_sum)[None]).reshape(-1)
    late = all_sum(
        jnp.concatenate([first_gain_sum, first_shift_sum, spread_mixing]).reshape(-1, 128), axes
    ).reshape(-1)

    head_peak = functools.reduce(jnp.maximum, peaks)
    for bit in bits_of(shards):
        head_peak = jnp.maximum(head_peak, swap(head_peak, "fsdp", shards, bit))
    factor = jnp.sqrt(threshold[0] / jnp.maximum(head_peak, threshold[0]))
    multiplier = jnp.broadcast_to(
        jnp.stack([factor, factor, jnp.ones_like(factor)], axis=1)[:, :, None], (heads, 3, HEAD)
    ).reshape(qkv)
    clipped_weight = attention_weight.astype(F32) * multiplier[None, :]
    clipped_bias = lax.dynamic_slice_in_dim(attention_bias, s * qkv, qkv) * multiplier

    return (
        jnp.stack(block_output),
        jnp.stack(input_grad),
        late[:width],
        late[width : 2 * width],
        grad_mixing,
        late[2 * width :],
        grad_output_own,
        early[2 * width : 3 * width],
        early[:width],
        early[width : 2 * width],
        grad_expand_own,
        early[4 * width :],
        grad_contract_own,
        early[3 * width : 4 * width],
        head_peak,
        clipped_weight,
        clipped_bias,
    )


def solution(mesh):
    grid, both, whole, line = P("fsdp", "seq"), P("fsdp", "seq", None), P(), P("seq")
    return jax.shard_map(
        functools.partial(body, mesh.shape["seq"], mesh.shape["fsdp"]),
        mesh=mesh,
        in_specs=(
            both, whole, whole, grid, whole, grid, whole, whole, whole, grid, whole, grid, whole,
            both, whole,
        ),
        out_specs=(
            both, both, whole, whole, grid, whole, grid, whole, whole, whole, grid, whole, grid,
            whole, line, grid, line,
        ),
        check_vma=False,
    )
```

```python
import functools
import math

import jax
import jax.numpy as jnp
from jax import lax
from jax.experimental import pallas as pl
from jax.experimental.pallas import tpu as pltpu
from jax.sharding import PartitionSpec as P

HEAD = 64
LOG2E = math.log2(math.e)
BF = jnp.bfloat16
F32 = jnp.float32
ANY = pl.BlockSpec(memory_space=pl.ANY)


def swap(value, axis, size, bit):
    return lax.ppermute(value, axis, [(i, i ^ bit) for i in range(size)])


def bits_of(size):
    return [1 << p for p in range(size.bit_length() - 1)]


def gather_slots(value, axis, size, wait=()):
    slots = {0: value}
    for bit in reversed(bits_of(size)):
        for k in list(slots):
            sent = after(slots[k], *wait) if k and wait else slots[k]
            slots[k | bit] = swap(sent, axis, size, bit)
    return [slots[k] for k in range(size)]


def scatter_near(odd, even, axis, size):
    came = swap(odd, axis, size, 1)
    total = even.astype(F32) + came.astype(F32)
    return total[1::2].astype(BF), total[0::2], [even, came]


def scatter_far(sent, rest, terms, axis, size):
    terms = list(terms)
    for bit in bits_of(size)[1:]:
        came = swap(sent, axis, size, bit)
        terms.append(came)
        if came.shape[0] > 1:
            rest = rest + came.astype(F32)
            sent, rest = rest[1::2].astype(BF), rest[0::2]
    return terms


def scatter_sum(odd, even, axis, size, waits=()):
    rest, sent, steps = even.astype(F32), odd, []
    for step, bit in enumerate(bits_of(size)):
        came = swap(sent, axis, size, bit)
        steps.append(came)
        if step < len(waits):
            came = after(came, *waits[step])
        rest = rest + came.astype(F32)
        if rest.shape[0] > 1:
            sent, rest = rest[1::2].astype(BF), rest[0::2]
    return rest[0], steps


def scatter_rows(value, index, axis, size):
    for bit in bits_of(size):
        pairs = value.reshape(-1, 2, *value.shape[1:])
        own = ((index & bit) != 0).astype(jnp.int32)
        sent = lax.dynamic_index_in_dim(pairs, 1 - own, 1, keepdims=False).astype(BF)
        kept = lax.dynamic_index_in_dim(pairs, own, 1, keepdims=False).astype(F32)
        value = kept + swap(sent, axis, size, bit).astype(F32)
    return value[0]


def after(value, *others):
    return lax.optimization_barrier((value, *others))[0]


def nn(a, b):
    return lax.dot_general(a, b, (((1,), (0,)), ((), ())), preferred_element_type=F32)


def nt(a, b):
    return lax.dot_general(a, b, (((1,), (1,)), ((), ())), preferred_element_type=F32)


def full(shape):
    return pl.BlockSpec(shape, lambda i, at: (0,) * len(shape))


def entry(shape, at_entry=0):
    return pl.BlockSpec((None, *shape), lambda i, at: (at_entry,) + (0,) * len(shape))


def call(kernel, name, at, operands, in_specs, out_shape, out_specs, scratch, grid=1, flops=0, aliases=None):
    moved = sum(math.prod(o.shape) * o.dtype.itemsize for o in operands)
    return pl.pallas_call(
        kernel,
        out_shape=out_shape,
        grid_spec=pltpu.PrefetchScalarGridSpec(
            num_scalar_prefetch=1,
            grid=(grid,),
            in_specs=in_specs,
            out_specs=out_specs,
            scratch_shapes=scratch,
        ),
        compiler_params=pltpu.CompilerParams(vmem_limit_bytes=58 << 20),
        cost_estimate=pl.CostEstimate(flops=flops, transcendentals=0, bytes_accessed=moved),
        input_output_aliases=aliases or {},
        name=name,
    )(at, *operands)


def copies_of(pairs, sems):
    return [pltpu.make_async_copy(src, dst, sems.at[i]) for i, (src, dst) in enumerate(pairs)]


def begin(copies):
    for copy in copies:
        copy.start()


def finish(copies):
    for copy in copies:
        copy.wait()


def block_rows(index, rows):
    return pl.ds(pl.multiple_of(index * rows, rows), rows)


def weight_pairs(refs, views, target, f, start=0):
    rows = target.shape[0] // len(views)
    pairs = []
    for i, lead, slot in views:
        source = refs[i] if lead is None else refs[i].at[lead]
        if source.shape[-1] > target.shape[-1]:
            source = source.at[:, start : start + target.shape[-1]]
        pairs.append((source, target.at[block_rows(f ^ slot, rows)]))
    return pairs


def arrays_of(views):
    arrays, found = [], []
    for array, lead, slot in views:
        place = next((i for i, a in enumerate(arrays) if a is array), len(arrays))
        if place == len(arrays):
            arrays.append(array)
        found.append((place, lead, slot))
    return arrays, found


def head_mask(width, head):
    return (lax.broadcasted_iota(jnp.int32, (1, width), 1) // HEAD) == head


def causal(tile):
    keys = lax.broadcasted_iota(jnp.int32, (tile, tile), 0)
    queries = lax.broadcasted_iota(jnp.int32, (tile, tile), 1)
    return keys <= queries


def lanes(group, width):
    return pl.ds(pl.multiple_of(group * width, width), width)


def join(parts, axis):
    return parts[0] if len(parts) == 1 else jnp.concatenate(parts, axis=axis)


def forward_kernel(n, b, views, count, at_ref, *refs):
    normed, refs = refs[:n], refs[n:]
    pieces, refs = refs[:count], refs[count:]
    bias_ref, q_ref, k_ref, v_ref, o_ref, lse_ref, peak_ref = refs[:7]
    x_s, w_s, vt_s, x_sems, w_sems, e_sems = refs[-6:]
    s, f = at_ref[0], at_ref[1]
    _, tile, _ = x_s.shape
    extra = []
    if len(refs) == 14:
        extra = copies_of(weight_pairs(pieces, views, refs[7], f, w_s.shape[1]), e_sems)
    every = q_ref.shape[1]
    width = 128 if every % 128 == 0 else every
    heads, factor = width // HEAD, HEAD**-0.5 * LOG2E
    w_copies = copies_of(weight_pairs(pieces, views, w_s, f), w_sems)
    x_copies = copies_of([(normed[k].at[b], x_s.at[k]) for k in range(n)], x_sems)
    begin(w_copies)
    begin(x_copies)
    begin(extra)
    finish(w_copies)
    for k in range(n):
        x_copies[k].wait()
        mixed = (nn(x_s[k], w_s[...]) + bias_ref[...]).astype(BF)
        spot = block_rows(k ^ s, tile)
        parts = [
            join([mixed[:, (3 * h + j) * HEAD : (3 * h + j + 1) * HEAD] for h in range(every // HEAD)], 1)
            for j in range(3)
        ]
        q_ref[spot], k_ref[spot], v_ref[spot] = parts
        vt_s[:, spot] = parts[2].T

    @pl.loop(0, every // width)
    def _(g):
        cols = lanes(g, width)
        peaks = [None] * heads
        for i in range(n):
            q_tile = q_ref[i * tile : (i + 1) * tile, cols]
            limit = (i + 1) * tile
            step = min(limit, 4 * tile)
            outs = []
            for h in range(heads):
                q = jnp.where(head_mask(width, h), q_tile, jnp.zeros_like(q_tile))
                v_rows = pl.ds(pl.multiple_of(g * width + h * HEAD, HEAD), HEAD)
                top = total = acc = None
                for start in range(0, limit, step):
                    stop = min(start + step, limit)
                    found = nt(k_ref[start:stop, cols], q)
                    if stop == limit:
                        edge = stop - start - tile
                        masked = jnp.where(causal(tile), found[edge:], -jnp.inf)
                        found = masked if edge == 0 else jnp.concatenate([found[:edge], masked], axis=0)
                    high = jnp.max(found, axis=0, keepdims=True)
                    new_top = high if top is None else jnp.maximum(top, high)
                    grown = jnp.exp2((found - new_top) * factor)
                    part = jnp.sum(grown, axis=0, keepdims=True)
                    mixed = nn(vt_s[v_rows, start:stop], grown.astype(BF))
                    if top is None:
                        total, acc = part, mixed
                    else:
                        shrink = jnp.exp2((top - new_top) * factor)
                        total, acc = total * shrink + part, acc * shrink + mixed
                    top = new_top
                outs.append(acc / total)
                lse_ref[g, h : h + 1, i * tile : (i + 1) * tile] = top * factor + jnp.log2(total)
                peaks[h] = top if peaks[h] is None else jnp.maximum(peaks[h], top)
            o_ref[i, :, cols] = join(outs, 0).T.astype(BF)
        for h in range(heads):
            peak_ref[g, h : h + 1, :] = peaks[h] * HEAD**-0.5

    finish(extra)


def attend_forward(at, b, normed, pieces, bias, n, strip=0):
    _, tile, width = normed[0].shape
    arrays, views = arrays_of(pieces)
    qkv = bias.shape[0]
    every, length = qkv // 3, n * tile
    group = 128 if every % 128 == 0 else every
    part = jax.ShapeDtypeStruct((length, every), BF)
    stats = [(every // group, group // HEAD, length), (every // group, group // HEAD, tile)]
    found = call(
        functools.partial(forward_kernel, n, b, views, len(arrays)),
        "attend_forward",
        at,
        [*normed, *arrays, bias.reshape(1, qkv)],
        [ANY] * (n + len(arrays)) + [full((1, qkv))],
        [part] * 3
        + [jax.ShapeDtypeStruct((n, tile, every), BF)]
        + [jax.ShapeDtypeStruct(shape, F32) for shape in stats]
        + ([jax.ShapeDtypeStruct((width, strip), BF)] if strip else []),
        [full((length, every))] * 3
        + [full((n, tile, every))]
        + [full(shape) for shape in stats]
        + ([full((width, strip))] if strip else []),
        [
            pltpu.VMEM((n, tile, width), BF),
            pltpu.VMEM((width, qkv), BF),
            pltpu.VMEM((every, length), BF),
            pltpu.SemaphoreType.DMA((n,)),
            pltpu.SemaphoreType.DMA((len(views),)),
            pltpu.SemaphoreType.DMA((len(views),)),
        ],
        flops=2 * length * width * qkv + 8 * length * length * every,
    )
    parts, (out, lse, peak), extra = found[:3], found[3:6], found[6:]
    return parts, out, lse, jnp.max(peak, axis=-1).reshape(-1), extra


def backward_kernel(n, views, count, at_ref, *refs):
    q_ref, k_ref, v_ref, lse_ref, o_ref, g_ref = refs[:6]
    pieces, refs = refs[6 : 6 + count], refs[6 + count :]
    mix_ref, odd_ref, even_ref, bias_ref, w_s, kt_s, dq_s, dk_s, dv_s, mix_s, w_sems = refs
    s, f = at_ref[0], at_ref[1]
    _, tile, qkv = mix_ref.shape
    every, scale = qkv // 3, HEAD**-0.5
    width = 128 if every % 128 == 0 else every
    heads, factor = width // HEAD, scale * LOG2E
    w_copies = copies_of(weight_pairs(pieces, views, w_s, f), w_sems)
    begin(w_copies)
    kt_s[...] = k_ref[...].T

    @pl.loop(0, every // width)
    def _(g):
        cols = lanes(g, width)
        for i in reversed(range(n)):
            rows = slice(i * tile, (i + 1) * tile)
            limit = (i + 1) * tile
            step = min(limit, 4 * tile)
            q_tile, g_tile = q_ref[rows, cols], g_ref[i, :, cols]
            inner = (g_tile.astype(F32) * o_ref[i, :, cols].astype(F32)).T
            outs = []
            for h in range(heads):
                mask = head_mask(width, h)
                q = jnp.where(mask, q_tile, jnp.zeros_like(q_tile))
                cot = jnp.where(mask, g_tile, jnp.zeros_like(g_tile))
                delta = jnp.sum(inner[h * HEAD : (h + 1) * HEAD], axis=0, keepdims=True)
                lse = lse_ref[g, h : h + 1, rows]
                k_rows = pl.ds(pl.multiple_of(g * width + h * HEAD, HEAD), HEAD)
                acc = None
                for start in range(0, limit, step):
                    stop = min(start + step, limit)
                    probs = jnp.exp2(nt(k_ref[start:stop, cols], q) * factor - lse)
                    if stop == limit:
                        edge = stop - start - tile
                        masked = jnp.where(causal(tile), probs[edge:], 0.0)
                        probs = masked if edge == 0 else jnp.concatenate([probs[:edge], masked], axis=0)
                    spread = nt(v_ref[start:stop, cols], cot)
                    logit_cot = (probs * (spread - delta)).astype(BF)
                    dv_part = nn(probs.astype(BF), cot)
                    dk_part = nn(logit_cot, q)
                    if i == n - 1 and h == 0:
                        dv_s[start:stop] = dv_part
                        dk_s[start:stop] = dk_part
                    else:
                        dv_s[start:stop] += dv_part
                        dk_s[start:stop] += dk_part
                    dq_part = nn(kt_s[k_rows, start:stop], logit_cot)
                    acc = dq_part if acc is None else acc + dq_part
                outs.append(acc)
            dq_s[rows] = (join(outs, 0).T * scale).astype(BF)
        for i in range(n):
            rows = slice(i * tile, (i + 1) * tile)
            dq = dq_s[rows]
            dk = (dk_s[rows] * scale).astype(BF)
            dv = dv_s[rows].astype(BF)
            mix_s[rows, lanes(g, 3 * width)] = jnp.concatenate(
                [a[:, h * HEAD : (h + 1) * HEAD] for h in range(heads) for a in (dq, dk, dv)], axis=1
            )

    finish(w_copies)
    total = jnp.zeros((1, qkv), F32)
    for k in range(n):
        mixed_cot = mix_s[block_rows(k ^ s, tile)]
        mix_ref[k] = mixed_cot
        total = total + jnp.sum(mixed_cot.astype(F32), axis=0, keepdims=True)
        target = odd_ref if k & 1 else even_ref
        target[k >> 1] = nt(mixed_cot, w_s[...]).astype(BF)
    bias_ref[...] = total


def attend_backward(at, parts, lse, out, cot, pieces):
    n, tile, every = out.shape
    length, qkv = n * tile, 3 * every
    arrays, views = arrays_of(pieces)
    width = len(views) * arrays[0].shape[-2]
    group = 128 if every % 128 == 0 else every
    half = (n // 2, tile, width)
    return call(
        functools.partial(backward_kernel, n, views, len(arrays)),
        "attend_backward",
        at,
        [*parts, lse, out, cot, *arrays],
        [full((length, every))] * 3
        + [full(lse.shape)]
        + [full((n, tile, every))] * 2
        + [ANY] * len(arrays),
        [
            jax.ShapeDtypeStruct((n, tile, qkv), BF),
            jax.ShapeDtypeStruct(half, BF),
            jax.ShapeDtypeStruct(half, BF),
            jax.ShapeDtypeStruct((1, qkv), F32),
        ],
        [full((n, tile, qkv)), full(half), full(half), full((1, qkv))],
        [
            pltpu.VMEM((width, qkv), BF),
            pltpu.VMEM((every, length), BF),
            pltpu.VMEM((length, group), BF),
            pltpu.VMEM((length, group), F32),
            pltpu.VMEM((length, group), F32),
            pltpu.VMEM((length, qkv), BF),
            pltpu.SemaphoreType.DMA((len(views),)),
        ],
        flops=2 * length * width * qkv + 20 * length * length * every,
    )


def norm_stats(values):
    centered = values - jnp.mean(values, axis=-1, keepdims=True)
    rate = lax.rsqrt(jnp.mean(centered * centered, axis=-1, keepdims=True) + 1e-05)
    return centered * rate, rate


def norm_back(cot, unit, rate, gain):
    e = cot * gain
    return rate * (
        e
        - jnp.mean(e, axis=-1, keepdims=True)
        - unit * jnp.mean(e * unit, axis=-1, keepdims=True)
    )


def column_copies(refs, target, s, sems):
    strip = refs[0].shape[1]
    if len(refs) == 1:
        return copies_of([(refs[0], target)], sems)
    return copies_of([(ref, target.at[:, lanes(k ^ s, strip)]) for k, ref in enumerate(refs)], sems)


def project_kernel(count, paired, at_ref, *refs):
    came_ref, weights, refs = refs[0], refs[1 : 1 + count], refs[1 + count :]
    tokens_ref, bias_ref, gain_ref, shift_ref = refs[:4]
    residual_ref, normed_ref, c_s, w_s, c_sem, w_sems = refs[-6:]
    if paired:
        normed_ref[1] = refs[4][...]
        normed_ref = normed_ref.at[0]
    n, _, every = came_ref.shape
    copy = pltpu.make_async_copy(came_ref, c_s, c_sem)
    weights = column_copies(weights, w_s, at_ref[0], w_sems)
    copy.start()
    begin(weights)
    total = tokens_ref[...].astype(F32) + bias_ref[...]
    copy.wait()
    finish(weights)
    for k in range(n):
        total = total + nn(c_s[k], w_s[k * every : (k + 1) * every])
    residual_ref[...] = total
    unit, _ = norm_stats(total)
    normed_ref[...] = (unit * gain_ref[...] + shift_ref[...]).astype(BF)


def project(at, b, came, weights, tokens, bias, gain, shift, cotangent=None):
    _, tile, width = tokens.shape
    n, _, every = came.shape
    row, block = full((1, width)), entry((tile, width), b)
    paired = cotangent is not None
    shape = (2, tile, width) if paired else (tile, width)
    return call(
        functools.partial(project_kernel, len(weights), paired),
        "project",
        at,
        [came, *weights, tokens, *(v.reshape(1, width) for v in (bias, gain, shift))]
        + ([cotangent] if paired else []),
        [ANY] * (1 + len(weights)) + [block, row, row, row] + ([block] if paired else []),
        [jax.ShapeDtypeStruct((tile, width), F32), jax.ShapeDtypeStruct(shape, BF)],
        [full((tile, width)), full(shape)],
        [
            pltpu.VMEM((n, tile, every), BF),
            pltpu.VMEM((width, width), BF),
            pltpu.SemaphoreType.DMA,
            pltpu.SemaphoreType.DMA((len(weights),)),
        ],
        flops=2 * tile * width * width,
    )


def gelu_pair(v):
    k0 = math.sqrt(2.0 / math.pi)
    square = v * v
    t = jnp.tanh(v * (k0 + (k0 * 0.044715) * square))
    half = 0.5 + 0.5 * t
    slope = half + (0.5 * v) * (1.0 - t * t) * (k0 + (3.0 * 0.044715 * k0) * square)
    return v * half, slope


def slot_at(step, n):
    half = n // 2
    return jnp.where(step < half, 2 * step + 1, 2 * (step - half))


def hidden_kernel(n, views, arrays, count, at_ref, *refs):
    inputs, refs = refs[:arrays], refs[arrays:]
    found = [inputs[i] if lead is None else inputs[i].at[lead] for i, lead, _ in views]
    normed, cots = found[:n], found[n:]
    weights_in, refs = refs[:count], refs[count:]
    bias_ref = refs[0]
    active_ref, cot_ref, odd_ref, even_ref, out_odd_ref, out_even_ref, sum_ref = refs[1:8]
    x_s, c_s, expand_s, contract_s, x_sems, c_sems, w_sems = refs[8:]
    step = pl.program_id(0)
    k = slot_at(step, n)
    shards, inner = weights_in[0].shape[0], expand_s.shape[1]
    first = [weights_in[0].at[i, 0] if count == 1 else weights_in[0].at[i] for i in range(shards)]
    second = [weights_in[0].at[i, 1] if count == 1 else weights_in[1].at[i] for i in range(shards)]
    e_rows, c_rows = expand_s.shape[0] // shards, contract_s.shape[0] // shards
    order = list(range(1, n, 2)) + list(range(0, n, 2))
    x_copies = copies_of([(normed[j], x_s.at[j]) for j in order], x_sems)
    c_copies = copies_of([(cots[j], c_s.at[j]) for j in order], c_sems)
    weights = copies_of(
        [(a, expand_s.at[i * e_rows : (i + 1) * e_rows]) for i, a in enumerate(first)]
        + [(a, contract_s.at[i * c_rows : (i + 1) * c_rows]) for i, a in enumerate(second)],
        w_sems,
    )

    @pl.when(step == 0)
    def _():
        begin(x_copies[:1] + weights[:shards] + c_copies[:1] + weights[shards:])
        begin(x_copies[1:] + c_copies[1:])
        sum_ref[...] = jnp.zeros_like(sum_ref)

    for j in range(n):

        @pl.when(step == j)
        def _(j=j):
            if j == 0:
                finish(weights)
            x_copies[j].wait()
            c_copies[j].wait()

    part = min(inner, 256)
    x, c = x_s[k], c_s[k]
    for start in range(0, inner, part):
        cols = slice(start, start + part)
        hidden = nn(x, expand_s[:, cols]) + bias_ref[:, cols]
        value, slope = gelu_pair(hidden)
        active_ref[:, cols] = value.astype(BF)
        hidden_cot = (nt(c, contract_s[cols]) * slope).astype(BF)
        cot_ref[:, cols] = hidden_cot
        sum_ref[:, cols] += jnp.sum(hidden_cot.astype(F32), axis=0, keepdims=True)
    partial = nt(cot_ref[...], expand_s[...]).astype(BF)
    out = nn(active_ref[...], contract_s[...]).astype(BF)

    @pl.when(step < n // 2)
    def _():
        odd_ref[...] = partial
        out_odd_ref[...] = out

    @pl.when(step >= n // 2)
    def _():
        even_ref[...] = partial
        out_even_ref[...] = out


def hidden_layer(at, normed, cots, weights, bias):
    n = len(normed)
    arrays, views = arrays_of([*normed, *cots])
    tile, width = arrays[0].shape[-2:]
    inner = bias.shape[0]
    shards = weights[0].shape[0]
    half = n // 2
    slot = pl.BlockSpec((None, tile, inner), lambda j, at: (slot_at(j, n), 0, 0))
    early = lambda j: jnp.minimum(j, half - 1)
    later = lambda j: jnp.maximum(j - half, 0)
    pair = jax.ShapeDtypeStruct((half, tile, width), BF)
    wide = jax.ShapeDtypeStruct((n, tile, inner), BF)
    operands = [*arrays, *weights, bias.reshape(1, inner)]
    specs = [ANY] * (len(arrays) + len(weights)) + [full((1, inner))]
    near = pl.BlockSpec((None, tile, width), lambda j, at: (early(j), 0, 0))
    kept = pl.BlockSpec((None, tile, width), lambda j, at: (later(j), 0, 0))
    return call(
        functools.partial(hidden_kernel, n, views, len(arrays), len(weights)),
        "hidden_layer",
        at,
        operands,
        specs,
        [wide, wide, pair, pair, pair, pair, jax.ShapeDtypeStruct((1, inner), F32)],
        [
            slot,
            slot,
            near,
            kept,
            near,
            kept,
            full((1, inner)),
        ],
        [
            pltpu.VMEM((n, tile, width), BF),
            pltpu.VMEM((n, tile, width), BF),
            pltpu.VMEM((width, inner), BF),
            pltpu.VMEM((inner, width), BF),
            pltpu.SemaphoreType.DMA((n,)),
            pltpu.SemaphoreType.DMA((n,)),
            pltpu.SemaphoreType.DMA((2 * shards,)),
        ],
        grid=n,
        flops=8 * n * tile * width * inner,
    )


def added(terms):
    total = terms[0][...].astype(F32)
    for term in terms[1:]:
        total = total + term[...].astype(F32)
    return total


def row_sum(values):
    return jnp.sum(values, axis=0, keepdims=True)


def second_kernel(b, terms_in, count, at_ref, *refs):
    terms, refs = refs[:terms_in], refs[terms_in:]
    weights, refs = refs[:count], refs[count:]
    residual_ref, cot_ref, gain_ref = refs[:3]
    rescot_ref, branch_ref, sums_ref, out_ref, t_s, r_s, c_s, w_s, sems, w_sems = refs[3:]
    copies = copies_of(
        [(residual_ref, r_s), (cot_ref.at[b], c_s)]
        + [(term.at[0], t_s.at[i]) for i, term in enumerate(terms)],
        sems,
    )
    weights = column_copies(weights, w_s, at_ref[0], w_sems)
    begin(copies)
    begin(weights)
    finish(copies)
    second_cot = added([t_s.at[i] for i in range(terms_in)])
    unit, rate = norm_stats(r_s[...])
    cot = c_s[...].astype(F32)
    residual_cot = cot + norm_back(second_cot, unit, rate, gain_ref[...])
    rescot_ref[...] = residual_cot
    branch = residual_cot.astype(BF)
    branch_ref[...] = branch
    sums_ref[0:1] = row_sum(second_cot * unit)
    sums_ref[1:2] = row_sum(second_cot)
    sums_ref[2:3] = row_sum(branch.astype(F32))
    sums_ref[3:4] = row_sum(cot)
    finish(weights)
    n, _, every = out_ref.shape
    for k in range(n):
        out_ref[k] = nt(branch, w_s[k * every : (k + 1) * every]).astype(BF)


def row_part(tile):
    return tile // 2


def stream_rows(b, part, width):
    return pl.BlockSpec((None, part, width), lambda i, at: (b, i, 0))


def row_block(part, width):
    return pl.BlockSpec((part, width), lambda i, at: (i, 0))


def second_back(at, b, terms, weights, residual, cotangent, gain, n):
    tile, width = residual.shape
    every = width // n
    return call(
        functools.partial(second_kernel, b, len(terms), len(weights)),
        "second_back",
        at,
        [*terms, *weights, residual, cotangent, gain.reshape(1, width)],
        [ANY] * (len(terms) + len(weights) + 2) + [full((1, width))],
        [
            jax.ShapeDtypeStruct((tile, width), F32),
            jax.ShapeDtypeStruct((tile, width), BF),
            jax.ShapeDtypeStruct((4, width), F32),
            jax.ShapeDtypeStruct((n, tile, every), BF),
        ],
        [full((tile, width))] * 2 + [full((4, width)), full((n, tile, every))],
        [
            pltpu.VMEM((len(terms), tile, width), BF),
            pltpu.VMEM((tile, width), F32),
            pltpu.VMEM((tile, width), BF),
            pltpu.VMEM((width, width), BF),
            pltpu.SemaphoreType.DMA((len(terms) + 2,)),
            pltpu.SemaphoreType.DMA((len(weights),)),
        ],
        flops=2 * tile * width * width,
    )


def first_kernel(count, at_ref, *refs):
    terms, refs = refs[:count], refs[count:]
    tokens_ref, rescot_ref, gain_ref = refs[:3]
    out_ref, sums_ref = refs[-2:]

    @pl.when(pl.program_id(0) == 0)
    def _():
        sums_ref[...] = jnp.zeros_like(sums_ref)

    first_cot = added(terms)
    unit, rate = norm_stats(tokens_ref[...].astype(F32))
    out_ref[...] = rescot_ref[...] + norm_back(first_cot, unit, rate, gain_ref[...])
    sums_ref[0:1] += row_sum(first_cot * unit)
    sums_ref[1:2] += row_sum(first_cot)


def first_back(at, b, terms, tokens, rescot, gain, held):
    batch, tile, width = tokens.shape
    part = row_part(tile)
    operands = [*terms, tokens, rescot, gain.reshape(1, width)]
    specs = [stream_rows(0, part, width)] * len(terms) + [
        stream_rows(b, part, width),
        row_block(part, width),
        full((1, width)),
    ]
    aliases = {}
    if held is not None:
        aliases = {1 + len(operands): 0}
        operands, specs = operands + [held], specs + [ANY]
    return call(
        functools.partial(first_kernel, len(terms)),
        "first_back",
        at,
        operands,
        specs,
        [jax.ShapeDtypeStruct((batch, tile, width), F32), jax.ShapeDtypeStruct((2, width), F32)],
        [stream_rows(b, part, width), full((2, width))],
        [],
        grid=tile // part,
        aliases=aliases,
    )


def result_kernel(count, at_ref, *refs):
    terms, refs = refs[:count], refs[count:]
    residual_ref, bias_ref, out_ref = refs[0], refs[1], refs[-1]
    out_ref[...] = (residual_ref[...] + added(terms) + bias_ref[...]).astype(BF)


def result_out(at, b, batch, terms, residual, bias, held):
    tile, width = residual.shape
    part = row_part(tile)
    operands = [*terms, residual, bias.reshape(1, width)]
    specs = [stream_rows(0, part, width)] * len(terms) + [row_block(part, width), full((1, width))]
    aliases = {}
    if held is not None:
        aliases = {1 + len(operands): 0}
        operands, specs = operands + [held], specs + [ANY]
    return call(
        functools.partial(result_kernel, len(terms)),
        "result_out",
        at,
        operands,
        specs,
        jax.ShapeDtypeStruct((batch, tile, width), BF),
        stream_rows(b, part, width),
        [],
        grid=tile // part,
        aliases=aliases,
    )


def tn(a, b):
    return lax.dot_general(a, b, (((0,), (0,)), ((), ())), preferred_element_type=F32)


def grad_kernel(count, products, slotted, split, row_of, at_ref, *refs):
    inputs, refs = refs[:count], refs[count:]
    outs, (a_s, b_s, acc_s, sems) = refs[:-4], refs[-4:]
    step = pl.program_id(0)
    s, f = at_ref[0], at_ref[1]
    part = acc_s.shape[1]
    width = b_s.shape[2]
    blocks = width // part
    plans, used = [], 0
    for p, (left, right) in enumerate(products):
        rows = b_s.shape[1] // len(right)
        cols = a_s.shape[2] // split
        pairs = []
        for i, (operand, lead) in enumerate(right):
            span = slice(i * rows, (i + 1) * rows)
            for c in range(split):
                o, l = left[i * split + c]
                view = inputs[o] if l is None else inputs[o].at[l]
                pairs.append((view, a_s.at[p, span, c * cols : (c + 1) * cols]))
            view = inputs[operand] if lead is None else inputs[operand].at[lead]
            pairs.append((view, b_s.at[p, span]))
        plans.append([pltpu.make_async_copy(*pair, sems.at[used + i]) for i, pair in enumerate(pairs)])
        used += len(pairs)

    @pl.when(step == 0)
    def _():
        for plan in plans:
            begin(plan)
        plan, groups = plans[0], len(products[0][1])
        rows = b_s.shape[1] // groups
        for i in range(groups):
            finish(plan[i * (split + 1) : (i + 1) * (split + 1)])
            span = slice(i * rows, (i + 1) * rows)
            found = tn(a_s[0, span], b_s[0, span, :part])
            if i == 0:
                acc_s[...] = found
            else:
                acc_s[...] += found

    for p in range(1, len(products)):

        @pl.when(step == p * blocks)
        def _(p=p):
            finish(plans[p])

    if blocks * len(products) > 1:

        @pl.when(step > 0)
        def _():
            p = step // blocks
            acc_s[...] = tn(a_s[p], b_s[p, :, lanes(step % blocks, part)])

    if slotted:
        odd_ref, even_ref = outs
        rows = odd_ref.shape[1]
        for k in range(2 * odd_ref.shape[0]):
            target = odd_ref if k & 1 else even_ref
            target[k >> 1] = acc_s[block_rows(row_of(s, f, k), rows)].astype(BF)
    else:
        (out_ref,) = outs
        rows = out_ref.shape[1]
        for k in range(out_ref.shape[0]):
            out_ref[k] = acc_s[k * rows : (k + 1) * rows].astype(BF)


def weight_grad(at, operands, products, shards, split=1, row_of=None):
    def shape_of(view):
        return operands[view[0]].shape[-2:]

    left, right = products[0]
    tokens = sum(shape_of(v)[0] for v in right)
    height, width = shape_of(left[0])[1] * split, shape_of(right[0])[1]
    part = width if width <= 256 or width % 256 else 256
    blocks, rows = width // part, height // shards
    if row_of is not None:
        shapes = [jax.ShapeDtypeStruct((shards // 2, rows, width), BF)] * 2
        specs = [pl.BlockSpec((shards // 2, rows, part), lambda j, at: (0, 0, j))] * 2
    else:
        shapes = jax.ShapeDtypeStruct((shards, len(products), rows, width), BF)
        specs = pl.BlockSpec((shards, None, rows, part), lambda j, at: (0, j // blocks, 0, j % blocks))
    return call(
        functools.partial(grad_kernel, len(operands), products, row_of is not None, split, row_of),
        "weight_grad",
        at,
        operands,
        [ANY] * len(operands),
        shapes,
        specs,
        [
            pltpu.VMEM((len(products), tokens, height), BF),
            pltpu.VMEM((len(products), tokens, width), BF),
            pltpu.VMEM((height, part), F32),
            pltpu.SemaphoreType.DMA((sum(len(a) + len(b) for a, b in products),)),
        ],
        grid=blocks * len(products),
        flops=2 * tokens * height * width * len(products),
    )


def strip_kernel(n, batch, at_ref, *refs):
    came, branch, refs = refs[:batch], refs[batch : 2 * batch], refs[2 * batch :]
    odd_ref, even_ref, a_s, b_s, sems = refs
    step = pl.program_id(0)
    tile, every = came[0].shape[1:]
    pairs = []
    for b in range(batch):
        span = slice(b * tile, (b + 1) * tile)
        pairs += [(came[b].at[k], a_s.at[span, k * every : (k + 1) * every]) for k in range(n)]
        pairs.append((branch[b], b_s.at[span]))
    copies = copies_of(pairs, sems)

    @pl.when(step == 0)
    def _():
        begin(copies)
        finish(copies)

    strip = odd_ref.shape[1]
    found = tn(a_s[...], b_s[:, lanes(slot_at(step, n) ^ at_ref[0], strip)]).astype(BF)

    @pl.when(step < n // 2)
    def _():
        odd_ref[...] = found

    @pl.when(step >= n // 2)
    def _():
        even_ref[...] = found


def strip_grad(at, came, branch):
    n, tile, every = came[0].shape
    batch, width = len(came), branch[0].shape[1]
    half, strip = n // 2, width // n
    block = (None, n * every, strip)
    return call(
        functools.partial(strip_kernel, n, batch),
        "strip_grad",
        at,
        [*came, *branch],
        [ANY] * (2 * batch),
        [jax.ShapeDtypeStruct((half, n * every, strip), BF)] * 2,
        [
            pl.BlockSpec(block, lambda j, at: (jnp.minimum(j, half - 1), 0, 0)),
            pl.BlockSpec(block, lambda j, at: (jnp.maximum(j - half, 0), 0, 0)),
        ],
        [
            pltpu.VMEM((batch * tile, n * every), BF),
            pltpu.VMEM((batch * tile, width), BF),
            pltpu.SemaphoreType.DMA((batch * (n + 1),)),
        ],
        grid=n,
        flops=2 * batch * tile * n * every * width,
    )


def body(
    n, shards,
    tokens, first_gain, first_shift, attention_weight, attention_bias, output_weight, output_bias,
    second_gain, second_shift, expand_weight, expand_bias, contract_weight, contract_bias,
    cotangent, threshold,
):
    batch, tile, width = tokens.shape
    rows, qkv = attention_weight.shape
    every = qkv // 3
    heads = every // HEAD
    inner_rows = contract_weight.shape[0]
    inner = inner_rows * shards // n
    piece = inner_rows // n
    ratio = shards // n
    strip = output_weight.shape[1]
    s = lax.axis_index("seq").astype(jnp.int32)
    f = lax.axis_index("fsdp").astype(jnp.int32)
    at = jnp.stack([s, f])
    streams = range(batch)
    joined = piece == rows

    strips = strip % 128 == 0 and qkv % 128 == 0

    sent = jnp.concatenate([attention_weight, output_weight], axis=1) if strips else attention_weight
    qkv_slots = gather_slots(sent, "fsdp", shards)
    qkv_pieces = [(a, None, k) for k, a in enumerate(qkv_slots)]
    unit, _ = norm_stats(tokens.astype(F32))
    normed_own = (unit * first_gain + first_shift).astype(BF)
    normed_first = gather_slots(normed_own, "seq", n, qkv_slots[1:])
    expand_weight, contract_weight, _ = lax.optimization_barrier(
        (expand_weight, contract_weight, qkv_slots[2])
    )
    to_seq = jnp.concatenate(
        [
            jnp.swapaxes(expand_weight.reshape(rows, ratio, n, piece), 1, 2)
            .swapaxes(0, 1)
            .reshape(n, -1, strip),
            contract_weight.reshape(n, piece, strip),
        ],
        axis=1,
    )
    from_seq = lax.all_to_all(to_seq, "seq", 0, 0, tiled=True)
    cut = rows * ratio * piece // strip
    expand_rows = (
        from_seq[:, :cut].reshape(n, rows, ratio * piece).swapaxes(0, 1).reshape(rows, inner)
    )
    contract_rows = from_seq[:, cut:].swapaxes(0, 1).reshape(piece, width)
    if joined:
        stacked = after(jnp.stack([expand_rows, contract_rows]), *qkv_slots[1:], normed_first[n // 2])
        hidden_weights = [lax.all_gather(stacked, "fsdp")]
    else:
        hidden_weights = [lax.all_gather(w, "fsdp") for w in (expand_rows, contract_rows)]

    mixing_bias = lax.dynamic_slice_in_dim(attention_bias, s * qkv, qkv)
    inner_bias = lax.dynamic_index_in_dim(
        expand_bias.reshape(shards, n, piece), s, axis=1, keepdims=False
    ).reshape(inner)

    parts, outs, lse, peaks, came = ([None] * batch for _ in range(5))
    residual, pairs = [None] * batch, [None] * batch
    for b in streams:
        parts[b], outs[b], lse[b], peaks[b], extra = attend_forward(
            at, b, normed_first, qkv_pieces, mixing_bias, n, strip if strips and b == 0 else 0
        )
        sent = after(outs[b], came[b - 1]) if b else outs[b]
        came[b] = lax.all_to_all(sent, "seq", 0, 0, tiled=True)
        if b == 0:
            joint = extra
            cot_first = gather_slots(after(cotangent[0], normed_first[n // 2]), "seq", n, outs[:1])
    if strips:
        output_weights = gather_slots(after(joint[0], cot_first[n // 2]), "seq", n, outs[-1:])
    else:
        output_weights = [
            lax.all_gather(
                lax.all_gather(output_weight, "fsdp", tiled=True), "seq", axis=1, tiled=True
            )
        ]
    normed_own = [None] * batch
    for b in streams:
        residual[b], normed_own[b] = project(
            at, b, came[b], output_weights, tokens, output_bias, second_gain, second_shift,
            cotangent if b else None,
        )
    cot_pairs = [None] * batch
    for b in streams:
        if b == 0:
            own = gather_slots(after(normed_own[b], came[-1]), "seq", n, normed_own[-1:])
            pairs[b] = [(a, None, k) for k, a in enumerate(own)]
            cot_pairs[b] = [(a, None, k) for k, a in enumerate(cot_first)]
        else:
            own = gather_slots(after(normed_own[b], pairs[b - 1][n // 2][0]), "seq", n)
            pairs[b] = [(a, 0, k) for k, a in enumerate(own)]
            cot_pairs[b] = [(a, 1, k) for k, a in enumerate(own)]

    active, hidden_cot, inner_sums, rescot, branch, sums, cots = ([None] * batch for _ in range(7))
    second, out_parts, terms = [], [], None
    for b in streams:
        operands = list(pairs[b])
        if b:
            array = after(operands[0][0], second[-1][0])
            operands[0] = (array, *operands[0][1:])
        active[b], hidden_cot[b], odd, even, *out_part, inner_sums[b] = hidden_layer(
            at, operands, cot_pairs[b], hidden_weights, inner_bias
        )
        out_parts.append(out_part)
        odd = after(odd, second_terms[-1][-1] if b else pairs[-1][n // 2][0])
        if b == 0:
            second_terms = []
        second.append(scatter_near(odd, even, "seq", n))
        second_terms.append(scatter_far(*second[b], "seq", n))

    def second_step(b, *others):
        terms = second_terms[b]
        if others:
            terms[0] = after(terms[0], *others)
        rescot[b], branch[b], sums[b], slots = second_back(
            at, b, terms, output_weights, residual[b], cotangent, second_gain, n
        )
        cots[b] = lax.all_to_all(slots, "seq", 0, 0, tiled=True)

    second_step(0)

    def by_slot(first):
        return [(first + k, b) for b in streams for k in range(n)]

    def by_stream(first):
        return [(first + b, k) for b in streams for k in range(n)]

    def owned(s, f, k):
        return f ^ k

    arrays, views = arrays_of([v for b in streams for v in (*pairs[b], *cot_pairs[b])])
    views = [view[:2] for view in views]
    normed_views = [v for b in streams for v in views[2 * b * n : (2 * b + 1) * n]]
    cot_views = [v for b in streams for v in views[(2 * b + 1) * n : 2 * (b + 1) * n]]
    far = len(arrays)
    if joined:
        arrays[0] = after(arrays[0], second[-1][0], branch[0])
        both = weight_grad(
            at,
            [*arrays, *hidden_cot, *active],
            [(normed_views, by_stream(far)), (by_stream(far + batch), cot_views)],
            shards,
        )
        grad_expand, grad_contract = lax.psum_scatter(both, "fsdp").astype(F32)
        done = [both]
    else:
        grad_expand, _ = scatter_sum(
            *weight_grad(
                at, [*arrays, *hidden_cot], [(normed_views, by_stream(far))], shards, 1, owned
            ),
            "fsdp",
            shards,
        )
        grad_contract, _ = scatter_sum(
            *weight_grad(at, [*arrays, *active], [(by_stream(far), cot_views)], shards, 1, owned),
            "fsdp",
            shards,
        )
        done = []
    for b in streams[1:]:
        second_step(b, *done, cots[b - 1])
    if strips:
        output_odd, output_even = strip_grad(at, came, branch)
    else:
        product = functools.reduce(
            jnp.add,
            [
                jnp.einsum("kte,td->ked", came[b], branch[b], preferred_element_type=F32)
                for b in streams
            ],
        ).reshape(width, n, strip)
        output_odd, output_even = (
            jnp.stack(
                [
                    lax.dynamic_index_in_dim(product, s ^ k, 1, keepdims=False).astype(BF)
                    for k in range(first, n, 2)
                ]
            )
            for first in (1, 0)
        )
    cots[0] = after(cots[0], *done, output_odd)

    mixed_cot, mixing_sums, tail = [None] * batch, [None] * batch, [None] * batch
    input_grad = None
    near, block_output = None, None
    out_terms = [None] * batch
    for b in streams:
        cot = cots[b]
        if b == 0:
            out_near = scatter_near(after(out_parts[b][0], branch[-1]), out_parts[b][1], "seq", n)
            cot = after(cot, out_near[0])
            out_terms[b] = scatter_far(*out_near, "seq", n)
        else:
            cot = after(cot, near[0])
        mixed_cot[b], odd, even, mixing_sums[b] = attend_backward(
            at, parts[b], lse[b], outs[b], cot, qkv_pieces
        )
        odd = after(odd, out_terms[0][-1], *([terms[-1]] if b else []))
        near = scatter_near(odd, even, "seq", n)
        terms = scatter_far(*near, "seq", n)
        if b == batch - 1:
            grad_parts = weight_grad(
                at,
                [after(normed_first[0], near[0]), *normed_first[1:], *mixed_cot],
                [(by_slot(0), by_stream(n))],
                shards,
                1,
                owned,
            )
            terms[0] = after(terms[0], grad_parts[0])
        input_grad, tail[b] = first_back(
            at, b, terms, tokens, rescot[b], first_gain, input_grad
        )
    for b in streams[1:]:
        out_near = scatter_near(after(out_parts[b][0], near[0]), out_parts[b][1], "seq", n)
        out_terms[b] = scatter_far(after(out_near[0], terms[-1]), *out_near[1:], "seq", n)
    for b in streams:
        block_output = result_out(
            at, b, batch, out_terms[b], residual[b], contract_bias, block_output
        )
    grad_mixing, steps = scatter_sum(
        after(grad_parts[0], grad_expand), grad_parts[1], "fsdp", shards, [(out_terms[-1][-1],)]
    )
    output_near = scatter_near(output_odd, output_even, "seq", n)
    output_terms = scatter_far(*output_near, "seq", n)
    output_terms[-1] = after(output_terms[-1], steps[1])
    output_sum_rows = functools.reduce(jnp.add, [a[0].astype(F32) for a in output_terms])
    grad_output_own = scatter_rows(
        output_sum_rows.reshape(shards, rows, strip), f, "fsdp", shards
    )
    back = lax.all_to_all(
        jnp.concatenate(
            [
                grad_expand.astype(BF)
                .reshape(rows, n, ratio * piece)
                .swapaxes(0, 1)
                .reshape(n, cut, strip),
                grad_contract.astype(BF).reshape(piece, n, strip).swapaxes(0, 1),
            ],
            axis=1,
        ),
        "seq",
        0,
        0,
        tiled=True,
    )
    grad_expand_own = (
        back[:, :cut]
        .reshape(n, rows, ratio, piece)
        .transpose(1, 2, 0, 3)
        .reshape(rows, ratio * n * piece)
        .astype(F32)
    )
    grad_contract_own = back[:, cut:].reshape(inner_rows, strip).astype(F32)
    def over_streams(values):
        return functools.reduce(jnp.add, values)

    mine = jnp.arange(n) == s
    spread_inner = jnp.where(
        mine[None, :, None], over_streams(inner_sums).reshape(shards, 1, piece), 0.0
    )
    spread_mixing = jnp.where(mine[:, None], over_streams(mixing_sums), 0.0)
    peak = jnp.where(mine[:, None], functools.reduce(jnp.maximum, peaks)[None], -jnp.inf)
    top = jnp.pad(peak.reshape(-1), (0, 1024 - n * heads)).reshape(-1, 128)
    vectors = jnp.concatenate(
        [top]
        + [
            v.reshape(-1, 128)
            for v in (over_streams(sums), over_streams(tail), spread_inner, spread_mixing)
        ]
    )
    vectors = after(vectors, steps[1])
    is_top = jnp.arange(vectors.shape[0])[:, None] < top.shape[0]
    for axis, size in (("seq", n), ("fsdp", shards)):
        for bit in bits_of(size):
            other = swap(vectors, axis, size, bit)
            vectors = jnp.where(is_top, jnp.maximum(vectors, other), vectors + other)
    vectors = vectors.reshape(-1)
    ends = [1024]
    for length in [width] * 6 + [n * inner, n * qkv]:
        ends.append(ends[-1] + length)
    (
        second_gain_sum, second_shift_sum, output_sum, contract_sum, first_gain_sum, first_shift_sum,
        inner_sum, mixing_sum,
    ) = (vectors[a:b] for a, b in zip(ends, ends[1:]))

    head_peak = lax.dynamic_slice_in_dim(vectors, s * heads, heads)
    factor = jnp.sqrt(threshold[0] / jnp.maximum(head_peak, threshold[0]))
    multiplier = jnp.broadcast_to(
        jnp.stack([factor, factor, jnp.ones_like(factor)], axis=1)[:, :, None], (heads, 3, HEAD)
    ).reshape(qkv)
    clipped_weight = attention_weight.astype(F32) * multiplier[None, :]
    clipped_bias = mixing_bias * multiplier

    return (
        block_output,
        input_grad,
        first_gain_sum,
        first_shift_sum,
        grad_mixing,
        mixing_sum,
        grad_output_own,
        output_sum,
        second_gain_sum,
        second_shift_sum,
        grad_expand_own,
        inner_sum,
        grad_contract_own,
        contract_sum,
        head_peak,
        clipped_weight,
        clipped_bias,
    )


def solution(mesh):
    grid, both, whole, line = P("fsdp", "seq"), P("fsdp", "seq", None), P(), P("seq")
    return jax.shard_map(
        functools.partial(body, mesh.shape["seq"], mesh.shape["fsdp"]),
        mesh=mesh,
        in_specs=(
            both, whole, whole, grid, whole, grid, whole, whole, whole, grid, whole, grid, whole,
            both, whole,
        ),
        out_specs=(
            both, both, whole, whole, grid, whole, grid, whole, whole, whole, grid, whole, grid,
            whole, line, grid, line,
        ),
        check_vma=False,
    )
```

```python
import functools
import math

import jax
import jax.numpy as jnp
from jax import lax
from jax.experimental import pallas as pl
from jax.experimental.pallas import tpu as pltpu
from jax.sharding import PartitionSpec as P

HEAD = 64
LOG2E = math.log2(math.e)
BF = jnp.bfloat16
F32 = jnp.float32
ANY = pl.BlockSpec(memory_space=pl.ANY)


def swap(value, axis, size, bit):
    return lax.ppermute(value, axis, [(i, i ^ bit) for i in range(size)])


def bits_of(size):
    return [1 << p for p in range(size.bit_length() - 1)]


def gather_slots(value, axis, size, wait=()):
    slots = {0: value}
    for bit in reversed(bits_of(size)):
        for k in list(slots):
            sent = after(slots[k], *wait) if k and wait else slots[k]
            slots[k | bit] = swap(sent, axis, size, bit)
    return [slots[k] for k in range(size)]


def scatter_near(odd, even, axis, size):
    came = swap(odd, axis, size, 1)
    total = even.astype(F32) + came.astype(F32)
    return total[1::2].astype(BF), total[0::2], [even, came]


def scatter_far(sent, rest, terms, axis, size):
    terms = list(terms)
    for bit in bits_of(size)[1:]:
        came = swap(sent, axis, size, bit)
        terms.append(came)
        if came.shape[0] > 1:
            rest = rest + came.astype(F32)
            sent, rest = rest[1::2].astype(BF), rest[0::2]
    return terms


def scatter_sum(odd, even, axis, size, waits=()):
    rest, sent = even.astype(F32), odd
    for bit in bits_of(size):
        came = swap(sent, axis, size, bit)
        if bit == 1:
            first, *waits = lax.optimization_barrier((came, *waits)) if waits else (came,)
            came = first
        rest = rest + came.astype(F32)
        if rest.shape[0] > 1:
            sent, rest = rest[1::2].astype(BF), rest[0::2]
    return rest[0], first, waits


def scatter_rows(value, index, axis, size):
    for bit in bits_of(size):
        pairs = value.reshape(-1, 2, *value.shape[1:])
        own = ((index & bit) != 0).astype(jnp.int32)
        sent = lax.dynamic_index_in_dim(pairs, 1 - own, 1, keepdims=False).astype(BF)
        kept = lax.dynamic_index_in_dim(pairs, own, 1, keepdims=False).astype(F32)
        value = kept + swap(sent, axis, size, bit).astype(F32)
    return value[0]


def after(value, *others):
    return lax.optimization_barrier((value, *others))[0]


def nn(a, b):
    return lax.dot_general(a, b, (((1,), (0,)), ((), ())), preferred_element_type=F32)


def nt(a, b):
    return lax.dot_general(a, b, (((1,), (1,)), ((), ())), preferred_element_type=F32)


def full(shape):
    return pl.BlockSpec(shape, lambda i, at: (0,) * len(shape))


def entry(shape, at_entry=0):
    return pl.BlockSpec((None, *shape), lambda i, at: (at_entry,) + (0,) * len(shape))


def call(kernel, name, at, operands, in_specs, out_shape, out_specs, scratch, grid=1, flops=0, aliases=None):
    moved = sum(math.prod(o.shape) * o.dtype.itemsize for o in operands)
    return pl.pallas_call(
        kernel,
        out_shape=out_shape,
        grid_spec=pltpu.PrefetchScalarGridSpec(
            num_scalar_prefetch=1,
            grid=(grid,),
            in_specs=in_specs,
            out_specs=out_specs,
            scratch_shapes=scratch,
        ),
        compiler_params=pltpu.CompilerParams(vmem_limit_bytes=58 << 20),
        cost_estimate=pl.CostEstimate(flops=flops, transcendentals=0, bytes_accessed=moved),
        input_output_aliases=aliases or {},
        name=name,
    )(at, *operands)


def copies_of(pairs, sems):
    return [pltpu.make_async_copy(src, dst, sems.at[i]) for i, (src, dst) in enumerate(pairs)]


def begin(copies):
    for copy in copies:
        copy.start()


def finish(copies):
    for copy in copies:
        copy.wait()


def block_rows(index, rows):
    return pl.ds(pl.multiple_of(index * rows, rows), rows)


def weight_pairs(refs, views, target, f, start=0):
    rows = target.shape[0] // len(views)
    pairs = []
    for i, lead, slot in views:
        source = refs[i] if lead is None else refs[i].at[lead]
        if source.shape[-1] > target.shape[-1]:
            source = source.at[:, start : start + target.shape[-1]]
        pairs.append((source, target.at[block_rows(f ^ slot, rows)]))
    return pairs


def arrays_of(views):
    arrays, found = [], []
    for array, lead, slot in views:
        place = next((i for i, a in enumerate(arrays) if a is array), len(arrays))
        if place == len(arrays):
            arrays.append(array)
        found.append((place, lead, slot))
    return arrays, found


def head_mask(width, head):
    return (lax.broadcasted_iota(jnp.int32, (1, width), 1) // HEAD) == head


def causal(tile):
    keys = lax.broadcasted_iota(jnp.int32, (tile, tile), 0)
    queries = lax.broadcasted_iota(jnp.int32, (tile, tile), 1)
    return keys <= queries


def lanes(group, width):
    return pl.ds(pl.multiple_of(group * width, width), width)


def join(parts, axis):
    return parts[0] if len(parts) == 1 else jnp.concatenate(parts, axis=axis)


def forward_kernel(n, b, views, count, at_ref, *refs):
    normed, refs = refs[:n], refs[n:]
    pieces, refs = refs[:count], refs[count:]
    bias_ref, q_ref, k_ref, v_ref, o_ref, lse_ref, peak_ref = refs[:7]
    x_s, w_s, vt_s, x_sems, w_sems, e_sems = refs[-6:]
    s, f = at_ref[0], at_ref[1]
    _, tile, _ = x_s.shape
    extra = []
    if len(refs) == 14:
        extra = copies_of(weight_pairs(pieces, views, refs[7], f, w_s.shape[1]), e_sems)
    every = q_ref.shape[1]
    width = 128 if every % 128 == 0 else every
    heads, factor = width // HEAD, HEAD**-0.5 * LOG2E
    w_copies = copies_of(weight_pairs(pieces, views, w_s, f), w_sems)
    x_copies = copies_of([(normed[k].at[b], x_s.at[k]) for k in range(n)], x_sems)
    begin(w_copies)
    begin(x_copies)
    begin(extra)
    finish(w_copies)
    for k in range(n):
        x_copies[k].wait()
        mixed = (nn(x_s[k], w_s[...]) + bias_ref[...]).astype(BF)
        spot = block_rows(k ^ s, tile)
        parts = [
            join([mixed[:, (3 * h + j) * HEAD : (3 * h + j + 1) * HEAD] for h in range(every // HEAD)], 1)
            for j in range(3)
        ]
        q_ref[spot], k_ref[spot], v_ref[spot] = parts
        vt_s[:, spot] = parts[2].T

    @pl.loop(0, every // width)
    def _(g):
        cols = lanes(g, width)
        peaks = [None] * heads
        for i in range(n):
            q_tile = q_ref[i * tile : (i + 1) * tile, cols]
            limit = (i + 1) * tile
            step = min(limit, 4 * tile)
            outs = []
            for h in range(heads):
                q = jnp.where(head_mask(width, h), q_tile, jnp.zeros_like(q_tile))
                v_rows = pl.ds(pl.multiple_of(g * width + h * HEAD, HEAD), HEAD)
                top = total = acc = None
                for start in range(0, limit, step):
                    stop = min(start + step, limit)
                    found = nt(k_ref[start:stop, cols], q)
                    if stop == limit:
                        edge = stop - start - tile
                        masked = jnp.where(causal(tile), found[edge:], -jnp.inf)
                        found = masked if edge == 0 else jnp.concatenate([found[:edge], masked], axis=0)
                    high = jnp.max(found, axis=0, keepdims=True)
                    new_top = high if top is None else jnp.maximum(top, high)
                    grown = jnp.exp2((found - new_top) * factor)
                    part = jnp.sum(grown, axis=0, keepdims=True)
                    mixed = nn(vt_s[v_rows, start:stop], grown.astype(BF))
                    if top is None:
                        total, acc = part, mixed
                    else:
                        shrink = jnp.exp2((top - new_top) * factor)
                        total, acc = total * shrink + part, acc * shrink + mixed
                    top = new_top
                outs.append(acc / total)
                lse_ref[g, h : h + 1, i * tile : (i + 1) * tile] = top * factor + jnp.log2(total)
                peaks[h] = top if peaks[h] is None else jnp.maximum(peaks[h], top)
            o_ref[i, :, cols] = join(outs, 0).T.astype(BF)
        for h in range(heads):
            peak_ref[g, h : h + 1, :] = peaks[h] * HEAD**-0.5

    finish(extra)


def attend_forward(at, b, normed, pieces, bias, n, strip=0):
    _, tile, width = normed[0].shape
    arrays, views = arrays_of(pieces)
    qkv = bias.shape[0]
    every, length = qkv // 3, n * tile
    group = 128 if every % 128 == 0 else every
    part = jax.ShapeDtypeStruct((length, every), BF)
    stats = [(every // group, group // HEAD, length), (every // group, group // HEAD, tile)]
    found = call(
        functools.partial(forward_kernel, n, b, views, len(arrays)),
        "attend_forward",
        at,
        [*normed, *arrays, bias.reshape(1, qkv)],
        [ANY] * (n + len(arrays)) + [full((1, qkv))],
        [part] * 3
        + [jax.ShapeDtypeStruct((n, tile, every), BF)]
        + [jax.ShapeDtypeStruct(shape, F32) for shape in stats]
        + ([jax.ShapeDtypeStruct((width, strip), BF)] if strip else []),
        [full((length, every))] * 3
        + [full((n, tile, every))]
        + [full(shape) for shape in stats]
        + ([full((width, strip))] if strip else []),
        [
            pltpu.VMEM((n, tile, width), BF),
            pltpu.VMEM((width, qkv), BF),
            pltpu.VMEM((every, length), BF),
            pltpu.SemaphoreType.DMA((n,)),
            pltpu.SemaphoreType.DMA((len(views),)),
            pltpu.SemaphoreType.DMA((len(views),)),
        ],
        flops=2 * length * width * qkv + 8 * length * length * every,
    )
    parts, (out, lse, peak), extra = found[:3], found[3:6], found[6:]
    return parts, out, lse, jnp.max(peak, axis=-1).reshape(-1), extra


def backward_kernel(n, views, count, at_ref, *refs):
    q_ref, k_ref, v_ref, lse_ref, o_ref, g_ref = refs[:6]
    pieces, refs = refs[6 : 6 + count], refs[6 + count :]
    mix_ref, odd_ref, even_ref, bias_ref, w_s, kt_s, dq_s, dk_s, dv_s, mix_s, w_sems = refs
    s, f = at_ref[0], at_ref[1]
    _, tile, qkv = mix_ref.shape
    every, scale = qkv // 3, HEAD**-0.5
    width = 128 if every % 128 == 0 else every
    heads, factor = width // HEAD, scale * LOG2E
    w_copies = copies_of(weight_pairs(pieces, views, w_s, f), w_sems)
    begin(w_copies)
    kt_s[...] = k_ref[...].T

    @pl.loop(0, every // width)
    def _(g):
        cols = lanes(g, width)
        for i in reversed(range(n)):
            rows = slice(i * tile, (i + 1) * tile)
            limit = (i + 1) * tile
            step = min(limit, 4 * tile)
            q_tile, g_tile = q_ref[rows, cols], g_ref[i, :, cols]
            inner = (g_tile.astype(F32) * o_ref[i, :, cols].astype(F32)).T
            outs = []
            for h in range(heads):
                mask = head_mask(width, h)
                q = jnp.where(mask, q_tile, jnp.zeros_like(q_tile))
                cot = jnp.where(mask, g_tile, jnp.zeros_like(g_tile))
                delta = jnp.sum(inner[h * HEAD : (h + 1) * HEAD], axis=0, keepdims=True)
                lse = lse_ref[g, h : h + 1, rows]
                k_rows = pl.ds(pl.multiple_of(g * width + h * HEAD, HEAD), HEAD)
                acc = None
                for start in range(0, limit, step):
                    stop = min(start + step, limit)
                    probs = jnp.exp2(nt(k_ref[start:stop, cols], q) * factor - lse)
                    if stop == limit:
                        edge = stop - start - tile
                        masked = jnp.where(causal(tile), probs[edge:], 0.0)
                        probs = masked if edge == 0 else jnp.concatenate([probs[:edge], masked], axis=0)
                    spread = nt(v_ref[start:stop, cols], cot)
                    logit_cot = (probs * (spread - delta)).astype(BF)
                    dv_part = nn(probs.astype(BF), cot)
                    dk_part = nn(logit_cot, q)
                    if i == n - 1 and h == 0:
                        dv_s[start:stop] = dv_part
                        dk_s[start:stop] = dk_part
                    else:
                        dv_s[start:stop] += dv_part
                        dk_s[start:stop] += dk_part
                    dq_part = nn(kt_s[k_rows, start:stop], logit_cot)
                    acc = dq_part if acc is None else acc + dq_part
                outs.append(acc)
            dq_s[rows] = (join(outs, 0).T * scale).astype(BF)
        for i in range(n):
            rows = slice(i * tile, (i + 1) * tile)
            dq = dq_s[rows]
            dk = (dk_s[rows] * scale).astype(BF)
            dv = dv_s[rows].astype(BF)
            mix_s[rows, lanes(g, 3 * width)] = jnp.concatenate(
                [a[:, h * HEAD : (h + 1) * HEAD] for h in range(heads) for a in (dq, dk, dv)], axis=1
            )

    finish(w_copies)
    total = jnp.zeros((1, qkv), F32)
    for k in range(n):
        mixed_cot = mix_s[block_rows(k ^ s, tile)]
        mix_ref[k] = mixed_cot
        total = total + jnp.sum(mixed_cot.astype(F32), axis=0, keepdims=True)
        target = odd_ref if k & 1 else even_ref
        target[k >> 1] = nt(mixed_cot, w_s[...]).astype(BF)
    bias_ref[...] = total


def attend_backward(at, parts, lse, out, cot, pieces):
    n, tile, every = out.shape
    length, qkv = n * tile, 3 * every
    arrays, views = arrays_of(pieces)
    width = len(views) * arrays[0].shape[-2]
    group = 128 if every % 128 == 0 else every
    half = (n // 2, tile, width)
    return call(
        functools.partial(backward_kernel, n, views, len(arrays)),
        "attend_backward",
        at,
        [*parts, lse, out, cot, *arrays],
        [full((length, every))] * 3
        + [full(lse.shape)]
        + [full((n, tile, every))] * 2
        + [ANY] * len(arrays),
        [
            jax.ShapeDtypeStruct((n, tile, qkv), BF),
            jax.ShapeDtypeStruct(half, BF),
            jax.ShapeDtypeStruct(half, BF),
            jax.ShapeDtypeStruct((1, qkv), F32),
        ],
        [full((n, tile, qkv)), full(half), full(half), full((1, qkv))],
        [
            pltpu.VMEM((width, qkv), BF),
            pltpu.VMEM((every, length), BF),
            pltpu.VMEM((length, group), BF),
            pltpu.VMEM((length, group), F32),
            pltpu.VMEM((length, group), F32),
            pltpu.VMEM((length, qkv), BF),
            pltpu.SemaphoreType.DMA((len(views),)),
        ],
        flops=2 * length * width * qkv + 20 * length * length * every,
    )


def norm_stats(values):
    centered = values - jnp.mean(values, axis=-1, keepdims=True)
    rate = lax.rsqrt(jnp.mean(centered * centered, axis=-1, keepdims=True) + 1e-05)
    return centered * rate, rate


def norm_back(cot, unit, rate, gain):
    e = cot * gain
    return rate * (
        e
        - jnp.mean(e, axis=-1, keepdims=True)
        - unit * jnp.mean(e * unit, axis=-1, keepdims=True)
    )


def column_copies(refs, target, s, sems):
    strip = refs[0].shape[1]
    if len(refs) == 1:
        return copies_of([(refs[0], target)], sems)
    return copies_of([(ref, target.at[:, lanes(k ^ s, strip)]) for k, ref in enumerate(refs)], sems)


def project_kernel(count, paired, at_ref, *refs):
    came_ref, weights, refs = refs[0], refs[1 : 1 + count], refs[1 + count :]
    tokens_ref, bias_ref, gain_ref, shift_ref = refs[:4]
    residual_ref, normed_ref, c_s, w_s, c_sem, w_sems = refs[-6:]
    if paired:
        normed_ref[1] = refs[4][...]
        normed_ref = normed_ref.at[0]
    n, _, every = came_ref.shape
    copy = pltpu.make_async_copy(came_ref, c_s, c_sem)
    weights = column_copies(weights, w_s, at_ref[0], w_sems)
    copy.start()
    begin(weights)
    total = tokens_ref[...].astype(F32) + bias_ref[...]
    copy.wait()
    finish(weights)
    for k in range(n):
        total = total + nn(c_s[k], w_s[k * every : (k + 1) * every])
    residual_ref[...] = total
    unit, _ = norm_stats(total)
    normed_ref[...] = (unit * gain_ref[...] + shift_ref[...]).astype(BF)


def project(at, b, came, weights, tokens, bias, gain, shift, cotangent=None):
    _, tile, width = tokens.shape
    n, _, every = came.shape
    row, block = full((1, width)), entry((tile, width), b)
    paired = cotangent is not None
    shape = (2, tile, width) if paired else (tile, width)
    return call(
        functools.partial(project_kernel, len(weights), paired),
        "project",
        at,
        [came, *weights, tokens, *(v.reshape(1, width) for v in (bias, gain, shift))]
        + ([cotangent] if paired else []),
        [ANY] * (1 + len(weights)) + [block, row, row, row] + ([block] if paired else []),
        [jax.ShapeDtypeStruct((tile, width), F32), jax.ShapeDtypeStruct(shape, BF)],
        [full((tile, width)), full(shape)],
        [
            pltpu.VMEM((n, tile, every), BF),
            pltpu.VMEM((width, width), BF),
            pltpu.SemaphoreType.DMA,
            pltpu.SemaphoreType.DMA((len(weights),)),
        ],
        flops=2 * tile * width * width,
    )


def gelu_pair(v):
    k0 = math.sqrt(2.0 / math.pi)
    square = v * v
    t = jnp.tanh(v * (k0 + (k0 * 0.044715) * square))
    half = 0.5 + 0.5 * t
    slope = half + (0.5 * v) * (1.0 - t * t) * (k0 + (3.0 * 0.044715 * k0) * square)
    return v * half, slope


def slot_at(step, n):
    half = n // 2
    return jnp.where(step < half, 2 * step + 1, 2 * (step - half))


def hidden_kernel(n, views, arrays, count, at_ref, *refs):
    inputs, refs = refs[:arrays], refs[arrays:]
    found = [inputs[i] if lead is None else inputs[i].at[lead] for i, lead, _ in views]
    normed, cots = found[:n], found[n:]
    weights_in, refs = refs[:count], refs[count:]
    bias_ref = refs[0]
    active_ref, cot_ref, odd_ref, even_ref, out_odd_ref, out_even_ref, sum_ref = refs[1:8]
    x_s, c_s, expand_s, contract_s, x_sems, c_sems, w_sems = refs[8:]
    step = pl.program_id(0)
    k = slot_at(step, n)
    shards, inner = weights_in[0].shape[0], expand_s.shape[1]
    first = [weights_in[0].at[i, 0] if count == 1 else weights_in[0].at[i] for i in range(shards)]
    second = [weights_in[0].at[i, 1] if count == 1 else weights_in[1].at[i] for i in range(shards)]
    e_rows, c_rows = expand_s.shape[0] // shards, contract_s.shape[0] // shards
    order = list(range(1, n, 2)) + list(range(0, n, 2))
    x_copies = copies_of([(normed[j], x_s.at[j]) for j in order], x_sems)
    c_copies = copies_of([(cots[j], c_s.at[j]) for j in order], c_sems)
    weights = copies_of(
        [(a, expand_s.at[i * e_rows : (i + 1) * e_rows]) for i, a in enumerate(first)]
        + [(a, contract_s.at[i * c_rows : (i + 1) * c_rows]) for i, a in enumerate(second)],
        w_sems,
    )

    @pl.when(step == 0)
    def _():
        begin(x_copies[:1] + weights[:shards] + c_copies[:1] + weights[shards:])
        begin(x_copies[1:] + c_copies[1:])
        sum_ref[...] = jnp.zeros_like(sum_ref)

    for j in range(n):

        @pl.when(step == j)
        def _(j=j):
            if j == 0:
                finish(weights)
            x_copies[j].wait()
            c_copies[j].wait()

    part = min(inner, 256)
    x, c = x_s[k], c_s[k]
    for start in range(0, inner, part):
        cols = slice(start, start + part)
        hidden = nn(x, expand_s[:, cols]) + bias_ref[:, cols]
        value, slope = gelu_pair(hidden)
        active_ref[:, cols] = value.astype(BF)
        hidden_cot = (nt(c, contract_s[cols]) * slope).astype(BF)
        cot_ref[:, cols] = hidden_cot
        sum_ref[:, cols] += jnp.sum(hidden_cot.astype(F32), axis=0, keepdims=True)
    partial = nt(cot_ref[...], expand_s[...]).astype(BF)
    out = nn(active_ref[...], contract_s[...]).astype(BF)

    @pl.when(step < n // 2)
    def _():
        odd_ref[...] = partial
        out_odd_ref[...] = out

    @pl.when(step >= n // 2)
    def _():
        even_ref[...] = partial
        out_even_ref[...] = out


def hidden_layer(at, normed, cots, weights, bias):
    n = len(normed)
    arrays, views = arrays_of([*normed, *cots])
    tile, width = arrays[0].shape[-2:]
    inner = bias.shape[0]
    shards = weights[0].shape[0]
    half = n // 2
    slot = pl.BlockSpec((None, tile, inner), lambda j, at: (slot_at(j, n), 0, 0))
    early = lambda j: jnp.minimum(j, half - 1)
    later = lambda j: jnp.maximum(j - half, 0)
    pair = jax.ShapeDtypeStruct((half, tile, width), BF)
    wide = jax.ShapeDtypeStruct((n, tile, inner), BF)
    operands = [*arrays, *weights, bias.reshape(1, inner)]
    specs = [ANY] * (len(arrays) + len(weights)) + [full((1, inner))]
    near = pl.BlockSpec((None, tile, width), lambda j, at: (early(j), 0, 0))
    kept = pl.BlockSpec((None, tile, width), lambda j, at: (later(j), 0, 0))
    return call(
        functools.partial(hidden_kernel, n, views, len(arrays), len(weights)),
        "hidden_layer",
        at,
        operands,
        specs,
        [wide, wide, pair, pair, pair, pair, jax.ShapeDtypeStruct((1, inner), F32)],
        [
            slot,
            slot,
            near,
            kept,
            near,
            kept,
            full((1, inner)),
        ],
        [
            pltpu.VMEM((n, tile, width), BF),
            pltpu.VMEM((n, tile, width), BF),
            pltpu.VMEM((width, inner), BF),
            pltpu.VMEM((inner, width), BF),
            pltpu.SemaphoreType.DMA((n,)),
            pltpu.SemaphoreType.DMA((n,)),
            pltpu.SemaphoreType.DMA((2 * shards,)),
        ],
        grid=n,
        flops=8 * n * tile * width * inner,
    )


def added(terms):
    total = terms[0][...].astype(F32)
    for term in terms[1:]:
        total = total + term[...].astype(F32)
    return total


def row_sum(values):
    return jnp.sum(values, axis=0, keepdims=True)


def second_kernel(b, terms_in, count, at_ref, *refs):
    terms, refs = refs[:terms_in], refs[terms_in:]
    weights, refs = refs[:count], refs[count:]
    residual_ref, cot_ref, gain_ref = refs[:3]
    rescot_ref, branch_ref, sums_ref, out_ref, t_s, r_s, c_s, w_s, sems, w_sems = refs[3:]
    copies = copies_of(
        [(residual_ref, r_s), (cot_ref.at[b], c_s)]
        + [(term.at[0], t_s.at[i]) for i, term in enumerate(terms)],
        sems,
    )
    weights = column_copies(weights, w_s, at_ref[0], w_sems)
    begin(copies)
    begin(weights)
    finish(copies)
    second_cot = added([t_s.at[i] for i in range(terms_in)])
    unit, rate = norm_stats(r_s[...])
    cot = c_s[...].astype(F32)
    residual_cot = cot + norm_back(second_cot, unit, rate, gain_ref[...])
    rescot_ref[...] = residual_cot
    branch = residual_cot.astype(BF)
    branch_ref[...] = branch
    sums_ref[0:1] = row_sum(second_cot * unit)
    sums_ref[1:2] = row_sum(second_cot)
    sums_ref[2:3] = row_sum(branch.astype(F32))
    sums_ref[3:4] = row_sum(cot)
    finish(weights)
    n, _, every = out_ref.shape
    for k in range(n):
        out_ref[k] = nt(branch, w_s[k * every : (k + 1) * every]).astype(BF)


def row_part(tile):
    return tile // 2


def stream_rows(b, part, width):
    return pl.BlockSpec((None, part, width), lambda i, at: (b, i, 0))


def row_block(part, width):
    return pl.BlockSpec((part, width), lambda i, at: (i, 0))


def second_back(at, b, terms, weights, residual, cotangent, gain, n):
    tile, width = residual.shape
    every = width // n
    return call(
        functools.partial(second_kernel, b, len(terms), len(weights)),
        "second_back",
        at,
        [*terms, *weights, residual, cotangent, gain.reshape(1, width)],
        [ANY] * (len(terms) + len(weights) + 2) + [full((1, width))],
        [
            jax.ShapeDtypeStruct((tile, width), F32),
            jax.ShapeDtypeStruct((tile, width), BF),
            jax.ShapeDtypeStruct((4, width), F32),
            jax.ShapeDtypeStruct((n, tile, every), BF),
        ],
        [full((tile, width))] * 2 + [full((4, width)), full((n, tile, every))],
        [
            pltpu.VMEM((len(terms), tile, width), BF),
            pltpu.VMEM((tile, width), F32),
            pltpu.VMEM((tile, width), BF),
            pltpu.VMEM((width, width), BF),
            pltpu.SemaphoreType.DMA((len(terms) + 2,)),
            pltpu.SemaphoreType.DMA((len(weights),)),
        ],
        flops=2 * tile * width * width,
    )


def first_kernel(count, at_ref, *refs):
    terms, refs = refs[:count], refs[count:]
    tokens_ref, rescot_ref, gain_ref = refs[:3]
    out_ref, sums_ref = refs[-2:]

    @pl.when(pl.program_id(0) == 0)
    def _():
        sums_ref[...] = jnp.zeros_like(sums_ref)

    first_cot = added(terms)
    unit, rate = norm_stats(tokens_ref[...].astype(F32))
    out_ref[...] = rescot_ref[...] + norm_back(first_cot, unit, rate, gain_ref[...])
    sums_ref[0:1] += row_sum(first_cot * unit)
    sums_ref[1:2] += row_sum(first_cot)


def first_back(at, b, terms, tokens, rescot, gain, held):
    batch, tile, width = tokens.shape
    part = row_part(tile)
    operands = [*terms, tokens, rescot, gain.reshape(1, width)]
    specs = [stream_rows(0, part, width)] * len(terms) + [
        stream_rows(b, part, width),
        row_block(part, width),
        full((1, width)),
    ]
    aliases = {}
    if held is not None:
        aliases = {1 + len(operands): 0}
        operands, specs = operands + [held], specs + [ANY]
    return call(
        functools.partial(first_kernel, len(terms)),
        "first_back",
        at,
        operands,
        specs,
        [jax.ShapeDtypeStruct((batch, tile, width), F32), jax.ShapeDtypeStruct((2, width), F32)],
        [stream_rows(b, part, width), full((2, width))],
        [],
        grid=tile // part,
        aliases=aliases,
    )


def result_kernel(count, at_ref, *refs):
    terms, refs = refs[:count], refs[count:]
    residual_ref, bias_ref, out_ref = refs[0], refs[1], refs[-1]
    out_ref[...] = (residual_ref[...] + added(terms) + bias_ref[...]).astype(BF)


def result_out(at, b, batch, terms, residual, bias, held):
    tile, width = residual.shape
    part = row_part(tile)
    operands = [*terms, residual, bias.reshape(1, width)]
    specs = [stream_rows(0, part, width)] * len(terms) + [row_block(part, width), full((1, width))]
    aliases = {}
    if held is not None:
        aliases = {1 + len(operands): 0}
        operands, specs = operands + [held], specs + [ANY]
    return call(
        functools.partial(result_kernel, len(terms)),
        "result_out",
        at,
        operands,
        specs,
        jax.ShapeDtypeStruct((batch, tile, width), BF),
        stream_rows(b, part, width),
        [],
        grid=tile // part,
        aliases=aliases,
    )


def tn(a, b):
    return lax.dot_general(a, b, (((0,), (0,)), ((), ())), preferred_element_type=F32)


def grad_kernel(count, products, slotted, split, row_of, at_ref, *refs):
    inputs, refs = refs[:count], refs[count:]
    outs, (a_s, b_s, acc_s, sems) = refs[:-4], refs[-4:]
    step = pl.program_id(0)
    s, f = at_ref[0], at_ref[1]
    part = acc_s.shape[1]
    width = b_s.shape[2]
    blocks = width // part
    plans, used = [], 0
    for p, (left, right) in enumerate(products):
        rows = b_s.shape[1] // len(right)
        cols = a_s.shape[2] // split
        pairs = []
        for i, (operand, lead) in enumerate(right):
            span = slice(i * rows, (i + 1) * rows)
            for c in range(split):
                o, l = left[i * split + c]
                view = inputs[o] if l is None else inputs[o].at[l]
                pairs.append((view, a_s.at[p, span, c * cols : (c + 1) * cols]))
            view = inputs[operand] if lead is None else inputs[operand].at[lead]
            pairs.append((view, b_s.at[p, span]))
        plans.append([pltpu.make_async_copy(*pair, sems.at[used + i]) for i, pair in enumerate(pairs)])
        used += len(pairs)

    @pl.when(step == 0)
    def _():
        for plan in plans:
            begin(plan)
        plan, groups = plans[0], len(products[0][1])
        rows = b_s.shape[1] // groups
        for i in range(groups):
            finish(plan[i * (split + 1) : (i + 1) * (split + 1)])
            span = slice(i * rows, (i + 1) * rows)
            found = tn(a_s[0, span], b_s[0, span, :part])
            if i == 0:
                acc_s[...] = found
            else:
                acc_s[...] += found

    for p in range(1, len(products)):

        @pl.when(step == p * blocks)
        def _(p=p):
            finish(plans[p])

    if blocks * len(products) > 1:

        @pl.when(step > 0)
        def _():
            p = step // blocks
            acc_s[...] = tn(a_s[p], b_s[p, :, lanes(step % blocks, part)])

    if slotted:
        odd_ref, even_ref = outs
        rows = odd_ref.shape[1]
        for k in range(2 * odd_ref.shape[0]):
            target = odd_ref if k & 1 else even_ref
            target[k >> 1] = acc_s[block_rows(row_of(s, f, k), rows)].astype(BF)
    else:
        (out_ref,) = outs
        rows = out_ref.shape[1]
        for k in range(out_ref.shape[0]):
            out_ref[k] = acc_s[k * rows : (k + 1) * rows].astype(BF)


def weight_grad(at, operands, products, shards, split=1, row_of=None):
    def shape_of(view):
        return operands[view[0]].shape[-2:]

    left, right = products[0]
    tokens = sum(shape_of(v)[0] for v in right)
    height, width = shape_of(left[0])[1] * split, shape_of(right[0])[1]
    part = width if width <= 256 or width % 256 else 256
    blocks, rows = width // part, height // shards
    if row_of is not None:
        shapes = [jax.ShapeDtypeStruct((shards // 2, rows, width), BF)] * 2
        specs = [pl.BlockSpec((shards // 2, rows, part), lambda j, at: (0, 0, j))] * 2
    else:
        shapes = jax.ShapeDtypeStruct((shards, len(products), rows, width), BF)
        specs = pl.BlockSpec((shards, None, rows, part), lambda j, at: (0, j // blocks, 0, j % blocks))
    return call(
        functools.partial(grad_kernel, len(operands), products, row_of is not None, split, row_of),
        "weight_grad",
        at,
        operands,
        [ANY] * len(operands),
        shapes,
        specs,
        [
            pltpu.VMEM((len(products), tokens, height), BF),
            pltpu.VMEM((len(products), tokens, width), BF),
            pltpu.VMEM((height, part), F32),
            pltpu.SemaphoreType.DMA((sum(len(a) + len(b) for a, b in products),)),
        ],
        grid=blocks * len(products),
        flops=2 * tokens * height * width * len(products),
    )


def strip_kernel(n, batch, at_ref, *refs):
    came, branch, refs = refs[:batch], refs[batch : 2 * batch], refs[2 * batch :]
    odd_ref, even_ref, a_s, b_s, sems = refs
    step = pl.program_id(0)
    tile, every = came[0].shape[1:]
    pairs = []
    for b in range(batch):
        span = slice(b * tile, (b + 1) * tile)
        pairs += [(came[b].at[k], a_s.at[span, k * every : (k + 1) * every]) for k in range(n)]
        pairs.append((branch[b], b_s.at[span]))
    copies = copies_of(pairs, sems)

    @pl.when(step == 0)
    def _():
        begin(copies)
        finish(copies)

    strip = odd_ref.shape[1]
    found = tn(a_s[...], b_s[:, lanes(slot_at(step, n) ^ at_ref[0], strip)]).astype(BF)

    @pl.when(step < n // 2)
    def _():
        odd_ref[...] = found

    @pl.when(step >= n // 2)
    def _():
        even_ref[...] = found


def strip_grad(at, came, branch):
    n, tile, every = came[0].shape
    batch, width = len(came), branch[0].shape[1]
    half, strip = n // 2, width // n
    block = (None, n * every, strip)
    return call(
        functools.partial(strip_kernel, n, batch),
        "strip_grad",
        at,
        [*came, *branch],
        [ANY] * (2 * batch),
        [jax.ShapeDtypeStruct((half, n * every, strip), BF)] * 2,
        [
            pl.BlockSpec(block, lambda j, at: (jnp.minimum(j, half - 1), 0, 0)),
            pl.BlockSpec(block, lambda j, at: (jnp.maximum(j - half, 0), 0, 0)),
        ],
        [
            pltpu.VMEM((batch * tile, n * every), BF),
            pltpu.VMEM((batch * tile, width), BF),
            pltpu.SemaphoreType.DMA((batch * (n + 1),)),
        ],
        grid=n,
        flops=2 * batch * tile * n * every * width,
    )


def body(
    n, shards,
    tokens, first_gain, first_shift, attention_weight, attention_bias, output_weight, output_bias,
    second_gain, second_shift, expand_weight, expand_bias, contract_weight, contract_bias,
    cotangent, threshold,
):
    batch, tile, width = tokens.shape
    rows, qkv = attention_weight.shape
    every = qkv // 3
    heads = every // HEAD
    inner_rows = contract_weight.shape[0]
    inner = inner_rows * shards // n
    piece = inner_rows // n
    ratio = shards // n
    strip = output_weight.shape[1]
    s = lax.axis_index("seq").astype(jnp.int32)
    f = lax.axis_index("fsdp").astype(jnp.int32)
    at = jnp.stack([s, f])
    streams = range(batch)
    joined = piece == rows

    strips = strip % 128 == 0 and qkv % 128 == 0

    sent = jnp.concatenate([attention_weight, output_weight], axis=1) if strips else attention_weight
    qkv_slots = gather_slots(sent, "fsdp", shards)
    qkv_pieces = [(a, None, k) for k, a in enumerate(qkv_slots)]
    unit, _ = norm_stats(tokens.astype(F32))
    normed_own = (unit * first_gain + first_shift).astype(BF)
    normed_first = gather_slots(normed_own, "seq", n, qkv_slots[1:])
    expand_weight, contract_weight, *_ = lax.optimization_barrier(
        (expand_weight, contract_weight, *(qkv_slots[bit] for bit in bits_of(shards)))
    )
    to_seq = jnp.concatenate(
        [
            jnp.swapaxes(expand_weight.reshape(rows, ratio, n, piece), 1, 2)
            .swapaxes(0, 1)
            .reshape(n, -1, strip),
            contract_weight.reshape(n, piece, strip),
        ],
        axis=1,
    )
    from_seq = lax.all_to_all(to_seq, "seq", 0, 0, tiled=True)
    cut = rows * ratio * piece // strip
    expand_rows = (
        from_seq[:, :cut].reshape(n, rows, ratio * piece).swapaxes(0, 1).reshape(rows, inner)
    )
    contract_rows = from_seq[:, cut:].swapaxes(0, 1).reshape(piece, width)
    if joined:
        stacked = after(jnp.stack([expand_rows, contract_rows]), *qkv_slots[1:], normed_first[n // 2])
        hidden_weights = [lax.all_gather(stacked, "fsdp")]
    else:
        hidden_weights = [lax.all_gather(w, "fsdp") for w in (expand_rows, contract_rows)]

    mixing_bias = lax.dynamic_slice_in_dim(attention_bias, s * qkv, qkv)
    inner_bias = lax.dynamic_index_in_dim(
        expand_bias.reshape(shards, n, piece), s, axis=1, keepdims=False
    ).reshape(inner)

    parts, outs, lse, peaks, came = ([None] * batch for _ in range(5))
    residual, pairs = [None] * batch, [None] * batch
    for b in streams:
        parts[b], outs[b], lse[b], peaks[b], extra = attend_forward(
            at, b, normed_first, qkv_pieces, mixing_bias, n, strip if strips and b == 0 else 0
        )
        sent = after(outs[b], came[b - 1]) if b else outs[b]
        came[b] = lax.all_to_all(sent, "seq", 0, 0, tiled=True)
        if b == 0:
            joint = extra
            cot_first = gather_slots(after(cotangent[0], normed_first[n // 2]), "seq", n, outs[:1])
    if strips:
        output_weights = gather_slots(after(joint[0], cot_first[n // 2]), "seq", n, outs[-1:])
    else:
        output_weights = [
            lax.all_gather(
                lax.all_gather(output_weight, "fsdp", tiled=True), "seq", axis=1, tiled=True
            )
        ]
    normed_own = [None] * batch
    for b in streams:
        residual[b], normed_own[b] = project(
            at, b, came[b], output_weights, tokens, output_bias, second_gain, second_shift,
            cotangent if b else None,
        )
    cot_pairs = [None] * batch
    for b in streams:
        if b == 0:
            own = gather_slots(after(normed_own[b], came[-1]), "seq", n, normed_own[-1:])
            pairs[b] = [(a, None, k) for k, a in enumerate(own)]
            cot_pairs[b] = [(a, None, k) for k, a in enumerate(cot_first)]
        else:
            own = gather_slots(after(normed_own[b], pairs[b - 1][n // 2][0]), "seq", n)
            pairs[b] = [(a, 0, k) for k, a in enumerate(own)]
            cot_pairs[b] = [(a, 1, k) for k, a in enumerate(own)]

    active, hidden_cot, inner_sums, rescot, branch, sums, cots = ([None] * batch for _ in range(7))
    second, out_parts, terms = [], [], None
    for b in streams:
        operands = list(pairs[b])
        if b:
            array = after(operands[0][0], second[-1][0])
            operands[0] = (array, *operands[0][1:])
        active[b], hidden_cot[b], odd, even, *out_part, inner_sums[b] = hidden_layer(
            at, operands, cot_pairs[b], hidden_weights, inner_bias
        )
        out_parts.append(out_part)
        odd = after(odd, second_terms[-1][-1] if b else pairs[-1][n // 2][0])
        if b == 0:
            second_terms = []
        second.append(scatter_near(odd, even, "seq", n))
        second_terms.append(scatter_far(*second[b], "seq", n))

    def second_step(b, *others):
        terms = second_terms[b]
        if others:
            terms[0] = after(terms[0], *others)
        rescot[b], branch[b], sums[b], slots = second_back(
            at, b, terms, output_weights, residual[b], cotangent, second_gain, n
        )
        cots[b] = lax.all_to_all(slots, "seq", 0, 0, tiled=True)

    second_step(0)

    def by_slot(first):
        return [(first + k, b) for b in streams for k in range(n)]

    def by_stream(first):
        return [(first + b, k) for b in streams for k in range(n)]

    def owned(s, f, k):
        return f ^ k

    arrays, views = arrays_of([v for b in streams for v in (*pairs[b], *cot_pairs[b])])
    views = [view[:2] for view in views]
    normed_views = [v for b in streams for v in views[2 * b * n : (2 * b + 1) * n]]
    cot_views = [v for b in streams for v in views[(2 * b + 1) * n : 2 * (b + 1) * n]]
    far = len(arrays)
    if joined:
        arrays[0] = after(arrays[0], second[-1][0], branch[0])
        both = weight_grad(
            at,
            [*arrays, *hidden_cot, *active],
            [(normed_views, by_stream(far)), (by_stream(far + batch), cot_views)],
            shards,
        )
        scattered = [lax.psum_scatter(after(both, cots[0], second_terms[-1][-1]), "fsdp")]
        done = [both]
    else:
        grad_expand, *_ = scatter_sum(
            *weight_grad(
                at, [*arrays, *hidden_cot], [(normed_views, by_stream(far))], shards, 1, owned
            ),
            "fsdp",
            shards,
        )
        grad_contract, *_ = scatter_sum(
            *weight_grad(at, [*arrays, *active], [(by_stream(far), cot_views)], shards, 1, owned),
            "fsdp",
            shards,
        )
        scattered, done = [grad_expand, grad_contract], []
    for b in streams[1:]:
        second_step(b, *done, cots[b - 1])
    if strips:
        output_odd, output_even = strip_grad(at, came, branch)
    else:
        product = functools.reduce(
            jnp.add,
            [
                jnp.einsum("kte,td->ked", came[b], branch[b], preferred_element_type=F32)
                for b in streams
            ],
        ).reshape(width, n, strip)
        output_odd, output_even = (
            jnp.stack(
                [
                    lax.dynamic_index_in_dim(product, s ^ k, 1, keepdims=False).astype(BF)
                    for k in range(first, n, 2)
                ]
            )
            for first in (1, 0)
        )
    cots[0] = after(cots[0], *done, output_odd)

    mixed_cot, mixing_sums, tail = [None] * batch, [None] * batch, [None] * batch
    input_grad = None
    near, block_output = None, None
    out_terms = [None] * batch
    for b in streams:
        cot = cots[b]
        if b == 0:
            out_near = scatter_near(after(out_parts[b][0], branch[-1]), out_parts[b][1], "seq", n)
            cot = after(cot, out_near[0])
            out_terms[b] = scatter_far(*out_near, "seq", n)
        else:
            cot = after(cot, near[0])
        mixed_cot[b], odd, even, mixing_sums[b] = attend_backward(
            at, parts[b], lse[b], outs[b], cot, qkv_pieces
        )
        odd = after(odd, out_terms[0][-1], *([terms[-1]] if b else []))
        near = scatter_near(odd, even, "seq", n)
        terms = scatter_far(*near, "seq", n)
        if b == batch - 1:
            grad_parts = weight_grad(
                at,
                [after(normed_first[0], near[0]), *normed_first[1:], *mixed_cot],
                [(by_slot(0), by_stream(n))],
                shards,
                1,
                owned,
            )
            terms[0] = after(terms[0], grad_parts[0])
        input_grad, tail[b] = first_back(
            at, b, terms, tokens, rescot[b], first_gain, input_grad
        )
    for b in streams[1:]:
        out_near = scatter_near(after(out_parts[b][0], near[0]), out_parts[b][1], "seq", n)
        out_terms[b] = scatter_far(after(out_near[0], terms[-1]), *out_near[1:], "seq", n)
    for b in streams:
        block_output = result_out(
            at, b, batch, out_terms[b], residual[b], contract_bias, block_output
        )
    def over_streams(values):
        return functools.reduce(jnp.add, values)

    mine = jnp.arange(n) == s
    spread_inner = jnp.where(
        mine[None, :, None], over_streams(inner_sums).reshape(shards, 1, piece), 0.0
    )
    spread_mixing = jnp.where(mine[:, None], over_streams(mixing_sums), 0.0)
    peak = jnp.where(mine[:, None], functools.reduce(jnp.maximum, peaks)[None], -jnp.inf)
    top = jnp.pad(peak.reshape(-1), (0, 1024 - n * heads)).reshape(-1, 128)
    vectors = jnp.concatenate(
        [top]
        + [
            v.reshape(-1, 128)
            for v in (over_streams(sums), over_streams(tail), spread_inner, spread_mixing)
        ]
    )
    is_top = jnp.arange(vectors.shape[0])[:, None] < top.shape[0]

    def summed(vectors, axis, size):
        for bit in bits_of(size):
            other = swap(vectors, axis, size, bit)
            vectors = jnp.where(is_top, jnp.maximum(vectors, other), vectors + other)
        return vectors

    vectors = summed(vectors, "seq", n)
    grad_mixing, step, (vectors, *scattered, _) = scatter_sum(
        *grad_parts, "fsdp", shards, (vectors, *scattered, out_terms[-1][-1])
    )
    grad_expand, grad_contract = scattered[0] if joined else scattered
    back = lax.all_to_all(
        jnp.concatenate(
            [
                grad_expand.astype(BF)
                .reshape(rows, n, ratio * piece)
                .swapaxes(0, 1)
                .reshape(n, cut, strip),
                grad_contract.astype(BF).reshape(piece, n, strip).swapaxes(0, 1),
            ],
            axis=1,
        ),
        "seq",
        0,
        0,
        tiled=True,
    )
    grad_expand_own = (
        back[:, :cut]
        .reshape(n, rows, ratio, piece)
        .transpose(1, 2, 0, 3)
        .reshape(rows, ratio * n * piece)
        .astype(F32)
    )
    grad_contract_own = back[:, cut:].reshape(inner_rows, strip).astype(F32)
    output_near = scatter_near(output_odd, output_even, "seq", n)
    output_terms = scatter_far(*output_near, "seq", n)
    output_terms[-1] = after(output_terms[-1], step)
    output_sum_rows = functools.reduce(jnp.add, [a[0].astype(F32) for a in output_terms])
    grad_output_own = scatter_rows(
        output_sum_rows.reshape(shards, rows, strip), f, "fsdp", shards
    )
    vectors = summed(vectors, "fsdp", shards)
    vectors = vectors.reshape(-1)
    ends = [1024]
    for length in [width] * 6 + [n * inner, n * qkv]:
        ends.append(ends[-1] + length)
    (
        second_gain_sum, second_shift_sum, output_sum, contract_sum, first_gain_sum, first_shift_sum,
        inner_sum, mixing_sum,
    ) = (vectors[a:b] for a, b in zip(ends, ends[1:]))

    head_peak = lax.dynamic_slice_in_dim(vectors, s * heads, heads)
    factor = jnp.sqrt(threshold[0] / jnp.maximum(head_peak, threshold[0]))
    multiplier = jnp.broadcast_to(
        jnp.stack([factor, factor, jnp.ones_like(factor)], axis=1)[:, :, None], (heads, 3, HEAD)
    ).reshape(qkv)
    clipped_weight = attention_weight.astype(F32) * multiplier[None, :]
    clipped_bias = mixing_bias * multiplier

    return (
        block_output,
        input_grad,
        first_gain_sum,
        first_shift_sum,
        grad_mixing,
        mixing_sum,
        grad_output_own,
        output_sum,
        second_gain_sum,
        second_shift_sum,
        grad_expand_own,
        inner_sum,
        grad_contract_own,
        contract_sum,
        head_peak,
        clipped_weight,
        clipped_bias,
    )


def solution(mesh):
    grid, both, whole, line = P("fsdp", "seq"), P("fsdp", "seq", None), P(), P("seq")
    return jax.shard_map(
        functools.partial(body, mesh.shape["seq"], mesh.shape["fsdp"]),
        mesh=mesh,
        in_specs=(
            both, whole, whole, grid, whole, grid, whole, whole, whole, grid, whole, grid, whole,
            both, whole,
        ),
        out_specs=(
            both, both, whole, whole, grid, whole, grid, whole, whole, whole, grid, whole, grid,
            whole, line, grid, line,
        ),
        check_vma=False,
    )
```

```python
import functools
import math

import jax
import jax.numpy as jnp
from jax import lax
from jax.experimental import pallas as pl
from jax.experimental.pallas import tpu as pltpu
from jax.sharding import PartitionSpec as P

HEAD = 64
LOG2E = math.log2(math.e)
BF = jnp.bfloat16
F32 = jnp.float32
ANY = pl.BlockSpec(memory_space=pl.ANY)


def swap(value, axis, size, bit):
    return lax.ppermute(value, axis, [(i, i ^ bit) for i in range(size)])


def bits_of(size):
    return [1 << p for p in range(size.bit_length() - 1)]


def gather_slots(value, axis, size, wait=()):
    slots = {0: value}
    for bit in reversed(bits_of(size)):
        for k in list(slots):
            sent = after(slots[k], *wait) if k and wait else slots[k]
            slots[k | bit] = swap(sent, axis, size, bit)
    return [slots[k] for k in range(size)]


def scatter_near(odd, even, axis, size):
    came = swap(odd, axis, size, 1)
    total = even.astype(F32) + came.astype(F32)
    return total[1::2].astype(BF), total[0::2], [even, came]


def scatter_far(sent, rest, terms, axis, size):
    terms = list(terms)
    for bit in bits_of(size)[1:]:
        came = swap(sent, axis, size, bit)
        terms.append(came)
        if came.shape[0] > 1:
            rest = rest + came.astype(F32)
            sent, rest = rest[1::2].astype(BF), rest[0::2]
    return terms


def scatter_sum(odd, even, axis, size, hooks=()):
    rest, sent = even.astype(F32), odd
    for step, bit in enumerate(bits_of(size)):
        came = swap(sent, axis, size, bit)
        if step < len(hooks):
            came = hooks[step](came)
        rest = rest + came.astype(F32)
        if rest.shape[0] > 1:
            sent, rest = rest[1::2].astype(BF), rest[0::2]
    return rest[0]


def scatter_half(value, index, axis, size, bit, left):
    at = left.index(bit)
    own = ((index & bit) != 0).astype(jnp.int32)
    sent = lax.dynamic_index_in_dim(value, 1 - own, at, keepdims=False).astype(BF)
    kept = lax.dynamic_index_in_dim(value, own, at, keepdims=False).astype(F32)
    return kept, swap(sent, axis, size, bit), [b for b in left if b != bit]


def after(value, *others):
    return lax.optimization_barrier((value, *others))[0]


def nn(a, b):
    return lax.dot_general(a, b, (((1,), (0,)), ((), ())), preferred_element_type=F32)


def nt(a, b):
    return lax.dot_general(a, b, (((1,), (1,)), ((), ())), preferred_element_type=F32)


def full(shape):
    return pl.BlockSpec(shape, lambda i, at: (0,) * len(shape))


def entry(shape, at_entry=0):
    return pl.BlockSpec((None, *shape), lambda i, at: (at_entry,) + (0,) * len(shape))


def call(kernel, name, at, operands, in_specs, out_shape, out_specs, scratch, grid=1, flops=0, aliases=None):
    moved = sum(math.prod(o.shape) * o.dtype.itemsize for o in operands)
    return pl.pallas_call(
        kernel,
        out_shape=out_shape,
        grid_spec=pltpu.PrefetchScalarGridSpec(
            num_scalar_prefetch=1,
            grid=(grid,),
            in_specs=in_specs,
            out_specs=out_specs,
            scratch_shapes=scratch,
        ),
        compiler_params=pltpu.CompilerParams(vmem_limit_bytes=58 << 20),
        cost_estimate=pl.CostEstimate(flops=flops, transcendentals=0, bytes_accessed=moved),
        input_output_aliases=aliases or {},
        name=name,
    )(at, *operands)


def copies_of(pairs, sems):
    return [pltpu.make_async_copy(src, dst, sems.at[i]) for i, (src, dst) in enumerate(pairs)]


def begin(copies):
    for copy in copies:
        copy.start()


def finish(copies):
    for copy in copies:
        copy.wait()


def block_rows(index, rows):
    return pl.ds(pl.multiple_of(index * rows, rows), rows)


def weight_pairs(refs, views, target, f, start=0):
    rows = target.shape[0] // len(views)
    pairs = []
    for i, lead, slot in views:
        source = refs[i] if lead is None else refs[i].at[lead]
        if source.shape[-1] > target.shape[-1]:
            source = source.at[:, start : start + target.shape[-1]]
        pairs.append((source, target.at[block_rows(f ^ slot, rows)]))
    return pairs


def arrays_of(views):
    arrays, found = [], []
    for array, lead, slot in views:
        place = next((i for i, a in enumerate(arrays) if a is array), len(arrays))
        if place == len(arrays):
            arrays.append(array)
        found.append((place, lead, slot))
    return arrays, found


def head_mask(width, head):
    return (lax.broadcasted_iota(jnp.int32, (1, width), 1) // HEAD) == head


def causal(tile):
    keys = lax.broadcasted_iota(jnp.int32, (tile, tile), 0)
    queries = lax.broadcasted_iota(jnp.int32, (tile, tile), 1)
    return keys <= queries


def lanes(group, width):
    return pl.ds(pl.multiple_of(group * width, width), width)


def join(parts, axis):
    return parts[0] if len(parts) == 1 else jnp.concatenate(parts, axis=axis)


def forward_kernel(n, b, views, count, at_ref, *refs):
    normed, refs = refs[:n], refs[n:]
    pieces, refs = refs[:count], refs[count:]
    bias_ref, q_ref, k_ref, v_ref, o_ref, lse_ref, peak_ref = refs[:7]
    x_s, w_s, vt_s, x_sems, w_sems, e_sems = refs[-6:]
    s, f = at_ref[0], at_ref[1]
    _, tile, _ = x_s.shape
    extra = []
    if len(refs) == 14:
        extra = copies_of(weight_pairs(pieces, views, refs[7], f, w_s.shape[1]), e_sems)
    every = q_ref.shape[1]
    width = 128 if every % 128 == 0 else every
    heads, factor = width // HEAD, HEAD**-0.5 * LOG2E
    w_copies = copies_of(weight_pairs(pieces, views, w_s, f), w_sems)
    x_copies = copies_of([(normed[k].at[b], x_s.at[k]) for k in range(n)], x_sems)
    begin(w_copies)
    begin(x_copies)
    begin(extra)
    finish(w_copies)
    for k in range(n):
        x_copies[k].wait()
        mixed = (nn(x_s[k], w_s[...]) + bias_ref[...]).astype(BF)
        spot = block_rows(k ^ s, tile)
        parts = [
            join([mixed[:, (3 * h + j) * HEAD : (3 * h + j + 1) * HEAD] for h in range(every // HEAD)], 1)
            for j in range(3)
        ]
        q_ref[spot], k_ref[spot], v_ref[spot] = parts
        vt_s[:, spot] = parts[2].T

    @pl.loop(0, every // width)
    def _(g):
        cols = lanes(g, width)
        peaks = [None] * heads
        for i in range(n):
            q_tile = q_ref[i * tile : (i + 1) * tile, cols]
            limit = (i + 1) * tile
            step = min(limit, 4 * tile)
            outs = []
            for h in range(heads):
                q = jnp.where(head_mask(width, h), q_tile, jnp.zeros_like(q_tile))
                v_rows = pl.ds(pl.multiple_of(g * width + h * HEAD, HEAD), HEAD)
                top = total = acc = None
                for start in range(0, limit, step):
                    stop = min(start + step, limit)
                    found = nt(k_ref[start:stop, cols], q)
                    if stop == limit:
                        edge = stop - start - tile
                        masked = jnp.where(causal(tile), found[edge:], -jnp.inf)
                        found = masked if edge == 0 else jnp.concatenate([found[:edge], masked], axis=0)
                    high = jnp.max(found, axis=0, keepdims=True)
                    new_top = high if top is None else jnp.maximum(top, high)
                    grown = jnp.exp2((found - new_top) * factor)
                    part = jnp.sum(grown, axis=0, keepdims=True)
                    mixed = nn(vt_s[v_rows, start:stop], grown.astype(BF))
                    if top is None:
                        total, acc = part, mixed
                    else:
                        shrink = jnp.exp2((top - new_top) * factor)
                        total, acc = total * shrink + part, acc * shrink + mixed
                    top = new_top
                outs.append(acc / total)
                lse_ref[g, h : h + 1, i * tile : (i + 1) * tile] = top * factor + jnp.log2(total)
                peaks[h] = top if peaks[h] is None else jnp.maximum(peaks[h], top)
            o_ref[i, :, cols] = join(outs, 0).T.astype(BF)
        for h in range(heads):
            peak_ref[g, h : h + 1, :] = peaks[h] * HEAD**-0.5

    finish(extra)


def attend_forward(at, b, normed, pieces, bias, n, strip=0):
    _, tile, width = normed[0].shape
    arrays, views = arrays_of(pieces)
    qkv = bias.shape[0]
    every, length = qkv // 3, n * tile
    group = 128 if every % 128 == 0 else every
    part = jax.ShapeDtypeStruct((length, every), BF)
    stats = [(every // group, group // HEAD, length), (every // group, group // HEAD, tile)]
    found = call(
        functools.partial(forward_kernel, n, b, views, len(arrays)),
        "attend_forward",
        at,
        [*normed, *arrays, bias.reshape(1, qkv)],
        [ANY] * (n + len(arrays)) + [full((1, qkv))],
        [part] * 3
        + [jax.ShapeDtypeStruct((n, tile, every), BF)]
        + [jax.ShapeDtypeStruct(shape, F32) for shape in stats]
        + ([jax.ShapeDtypeStruct((width, strip), BF)] if strip else []),
        [full((length, every))] * 3
        + [full((n, tile, every))]
        + [full(shape) for shape in stats]
        + ([full((width, strip))] if strip else []),
        [
            pltpu.VMEM((n, tile, width), BF),
            pltpu.VMEM((width, qkv), BF),
            pltpu.VMEM((every, length), BF),
            pltpu.SemaphoreType.DMA((n,)),
            pltpu.SemaphoreType.DMA((len(views),)),
            pltpu.SemaphoreType.DMA((len(views),)),
        ],
        flops=2 * length * width * qkv + 8 * length * length * every,
    )
    parts, (out, lse, peak), extra = found[:3], found[3:6], found[6:]
    return parts, out, lse, jnp.max(peak, axis=-1).reshape(-1), extra


def backward_kernel(n, views, count, at_ref, *refs):
    q_ref, k_ref, v_ref, lse_ref, o_ref, g_ref = refs[:6]
    pieces, refs = refs[6 : 6 + count], refs[6 + count :]
    mix_ref, odd_ref, even_ref, bias_ref, w_s, kt_s, dq_s, dk_s, dv_s, mix_s, w_sems = refs
    s, f = at_ref[0], at_ref[1]
    _, tile, qkv = mix_ref.shape
    every, scale = qkv // 3, HEAD**-0.5
    width = 128 if every % 128 == 0 else every
    heads, factor = width // HEAD, scale * LOG2E
    w_copies = copies_of(weight_pairs(pieces, views, w_s, f), w_sems)
    begin(w_copies)
    kt_s[...] = k_ref[...].T

    @pl.loop(0, every // width)
    def _(g):
        cols = lanes(g, width)
        for i in reversed(range(n)):
            rows = slice(i * tile, (i + 1) * tile)
            limit = (i + 1) * tile
            step = min(limit, 4 * tile)
            q_tile, g_tile = q_ref[rows, cols], g_ref[i, :, cols]
            inner = (g_tile.astype(F32) * o_ref[i, :, cols].astype(F32)).T
            outs = []
            for h in range(heads):
                mask = head_mask(width, h)
                q = jnp.where(mask, q_tile, jnp.zeros_like(q_tile))
                cot = jnp.where(mask, g_tile, jnp.zeros_like(g_tile))
                delta = jnp.sum(inner[h * HEAD : (h + 1) * HEAD], axis=0, keepdims=True)
                lse = lse_ref[g, h : h + 1, rows]
                k_rows = pl.ds(pl.multiple_of(g * width + h * HEAD, HEAD), HEAD)
                acc = None
                for start in range(0, limit, step):
                    stop = min(start + step, limit)
                    probs = jnp.exp2(nt(k_ref[start:stop, cols], q) * factor - lse)
                    if stop == limit:
                        edge = stop - start - tile
                        masked = jnp.where(causal(tile), probs[edge:], 0.0)
                        probs = masked if edge == 0 else jnp.concatenate([probs[:edge], masked], axis=0)
                    spread = nt(v_ref[start:stop, cols], cot)
                    logit_cot = (probs * (spread - delta)).astype(BF)
                    dv_part = nn(probs.astype(BF), cot)
                    dk_part = nn(logit_cot, q)
                    if i == n - 1 and h == 0:
                        dv_s[start:stop] = dv_part
                        dk_s[start:stop] = dk_part
                    else:
                        dv_s[start:stop] += dv_part
                        dk_s[start:stop] += dk_part
                    dq_part = nn(kt_s[k_rows, start:stop], logit_cot)
                    acc = dq_part if acc is None else acc + dq_part
                outs.append(acc)
            dq_s[rows] = (join(outs, 0).T * scale).astype(BF)
        for i in range(n):
            rows = slice(i * tile, (i + 1) * tile)
            dq = dq_s[rows]
            dk = (dk_s[rows] * scale).astype(BF)
            dv = dv_s[rows].astype(BF)
            mix_s[rows, lanes(g, 3 * width)] = jnp.concatenate(
                [a[:, h * HEAD : (h + 1) * HEAD] for h in range(heads) for a in (dq, dk, dv)], axis=1
            )

    finish(w_copies)
    total = jnp.zeros((1, qkv), F32)
    for k in range(n):
        mixed_cot = mix_s[block_rows(k ^ s, tile)]
        mix_ref[k] = mixed_cot
        total = total + jnp.sum(mixed_cot.astype(F32), axis=0, keepdims=True)
        target = odd_ref if k & 1 else even_ref
        target[k >> 1] = nt(mixed_cot, w_s[...]).astype(BF)
    bias_ref[...] = total


def attend_backward(at, parts, lse, out, cot, pieces):
    n, tile, every = out.shape
    length, qkv = n * tile, 3 * every
    arrays, views = arrays_of(pieces)
    width = len(views) * arrays[0].shape[-2]
    group = 128 if every % 128 == 0 else every
    half = (n // 2, tile, width)
    return call(
        functools.partial(backward_kernel, n, views, len(arrays)),
        "attend_backward",
        at,
        [*parts, lse, out, cot, *arrays],
        [full((length, every))] * 3
        + [full(lse.shape)]
        + [full((n, tile, every))] * 2
        + [ANY] * len(arrays),
        [
            jax.ShapeDtypeStruct((n, tile, qkv), BF),
            jax.ShapeDtypeStruct(half, BF),
            jax.ShapeDtypeStruct(half, BF),
            jax.ShapeDtypeStruct((1, qkv), F32),
        ],
        [full((n, tile, qkv)), full(half), full(half), full((1, qkv))],
        [
            pltpu.VMEM((width, qkv), BF),
            pltpu.VMEM((every, length), BF),
            pltpu.VMEM((length, group), BF),
            pltpu.VMEM((length, group), F32),
            pltpu.VMEM((length, group), F32),
            pltpu.VMEM((length, qkv), BF),
            pltpu.SemaphoreType.DMA((len(views),)),
        ],
        flops=2 * length * width * qkv + 20 * length * length * every,
    )


def norm_stats(values):
    centered = values - jnp.mean(values, axis=-1, keepdims=True)
    rate = lax.rsqrt(jnp.mean(centered * centered, axis=-1, keepdims=True) + 1e-05)
    return centered * rate, rate


def norm_back(cot, unit, rate, gain):
    e = cot * gain
    return rate * (
        e
        - jnp.mean(e, axis=-1, keepdims=True)
        - unit * jnp.mean(e * unit, axis=-1, keepdims=True)
    )


def column_copies(refs, target, s, sems):
    strip = refs[0].shape[1]
    if len(refs) == 1:
        return copies_of([(refs[0], target)], sems)
    return copies_of([(ref, target.at[:, lanes(k ^ s, strip)]) for k, ref in enumerate(refs)], sems)


def project_kernel(count, paired, at_ref, *refs):
    came_ref, weights, refs = refs[0], refs[1 : 1 + count], refs[1 + count :]
    tokens_ref, bias_ref, gain_ref, shift_ref = refs[:4]
    residual_ref, normed_ref, c_s, w_s, c_sem, w_sems = refs[-6:]
    if paired:
        normed_ref[1] = refs[4][...]
        normed_ref = normed_ref.at[0]
    n, _, every = came_ref.shape
    copy = pltpu.make_async_copy(came_ref, c_s, c_sem)
    weights = column_copies(weights, w_s, at_ref[0], w_sems)
    copy.start()
    begin(weights)
    total = tokens_ref[...].astype(F32) + bias_ref[...]
    copy.wait()
    finish(weights)
    for k in range(n):
        total = total + nn(c_s[k], w_s[k * every : (k + 1) * every])
    residual_ref[...] = total
    unit, _ = norm_stats(total)
    normed_ref[...] = (unit * gain_ref[...] + shift_ref[...]).astype(BF)


def project(at, b, came, weights, tokens, bias, gain, shift, cotangent=None):
    _, tile, width = tokens.shape
    n, _, every = came.shape
    row, block = full((1, width)), entry((tile, width), b)
    paired = cotangent is not None
    shape = (2, tile, width) if paired else (tile, width)
    return call(
        functools.partial(project_kernel, len(weights), paired),
        "project",
        at,
        [came, *weights, tokens, *(v.reshape(1, width) for v in (bias, gain, shift))]
        + ([cotangent] if paired else []),
        [ANY] * (1 + len(weights)) + [block, row, row, row] + ([block] if paired else []),
        [jax.ShapeDtypeStruct((tile, width), F32), jax.ShapeDtypeStruct(shape, BF)],
        [full((tile, width)), full(shape)],
        [
            pltpu.VMEM((n, tile, every), BF),
            pltpu.VMEM((width, width), BF),
            pltpu.SemaphoreType.DMA,
            pltpu.SemaphoreType.DMA((len(weights),)),
        ],
        flops=2 * tile * width * width,
    )


def gelu_pair(v):
    k0 = math.sqrt(2.0 / math.pi)
    square = v * v
    t = jnp.tanh(v * (k0 + (k0 * 0.044715) * square))
    half = 0.5 + 0.5 * t
    slope = half + (0.5 * v) * (1.0 - t * t) * (k0 + (3.0 * 0.044715 * k0) * square)
    return v * half, slope


def slot_at(step, n):
    half = n // 2
    return jnp.where(step < half, 2 * step + 1, 2 * (step - half))


def hidden_kernel(n, views, arrays, count, at_ref, *refs):
    inputs, refs = refs[:arrays], refs[arrays:]
    found = [inputs[i] if lead is None else inputs[i].at[lead] for i, lead, _ in views]
    normed, cots = found[:n], found[n:]
    weights_in, refs = refs[:count], refs[count:]
    bias_ref = refs[0]
    active_ref, cot_ref, odd_ref, even_ref, out_odd_ref, out_even_ref, sum_ref = refs[1:8]
    x_s, c_s, expand_s, contract_s, x_sems, c_sems, w_sems = refs[8:]
    step = pl.program_id(0)
    k = slot_at(step, n)
    shards, inner = weights_in[0].shape[0], expand_s.shape[1]
    first = [weights_in[0].at[i, 0] if count == 1 else weights_in[0].at[i] for i in range(shards)]
    second = [weights_in[0].at[i, 1] if count == 1 else weights_in[1].at[i] for i in range(shards)]
    e_rows, c_rows = expand_s.shape[0] // shards, contract_s.shape[0] // shards
    order = list(range(1, n, 2)) + list(range(0, n, 2))
    x_copies = copies_of([(normed[j], x_s.at[j]) for j in order], x_sems)
    c_copies = copies_of([(cots[j], c_s.at[j]) for j in order], c_sems)
    weights = copies_of(
        [(a, expand_s.at[i * e_rows : (i + 1) * e_rows]) for i, a in enumerate(first)]
        + [(a, contract_s.at[i * c_rows : (i + 1) * c_rows]) for i, a in enumerate(second)],
        w_sems,
    )

    @pl.when(step == 0)
    def _():
        begin(x_copies[:1] + weights[:shards] + c_copies[:1] + weights[shards:])
        begin(x_copies[1:] + c_copies[1:])
        sum_ref[...] = jnp.zeros_like(sum_ref)

    for j in range(n):

        @pl.when(step == j)
        def _(j=j):
            if j == 0:
                finish(weights)
            x_copies[j].wait()
            c_copies[j].wait()

    part = min(inner, 256)
    x, c = x_s[k], c_s[k]
    for start in range(0, inner, part):
        cols = slice(start, start + part)
        hidden = nn(x, expand_s[:, cols]) + bias_ref[:, cols]
        value, slope = gelu_pair(hidden)
        active_ref[:, cols] = value.astype(BF)
        hidden_cot = (nt(c, contract_s[cols]) * slope).astype(BF)
        cot_ref[:, cols] = hidden_cot
        sum_ref[:, cols] += jnp.sum(hidden_cot.astype(F32), axis=0, keepdims=True)
    partial = nt(cot_ref[...], expand_s[...]).astype(BF)
    out = nn(active_ref[...], contract_s[...]).astype(BF)

    @pl.when(step < n // 2)
    def _():
        odd_ref[...] = partial
        out_odd_ref[...] = out

    @pl.when(step >= n // 2)
    def _():
        even_ref[...] = partial
        out_even_ref[...] = out


def hidden_layer(at, normed, cots, weights, bias):
    n = len(normed)
    arrays, views = arrays_of([*normed, *cots])
    tile, width = arrays[0].shape[-2:]
    inner = bias.shape[0]
    shards = weights[0].shape[0]
    half = n // 2
    slot = pl.BlockSpec((None, tile, inner), lambda j, at: (slot_at(j, n), 0, 0))
    early = lambda j: jnp.minimum(j, half - 1)
    later = lambda j: jnp.maximum(j - half, 0)
    pair = jax.ShapeDtypeStruct((half, tile, width), BF)
    wide = jax.ShapeDtypeStruct((n, tile, inner), BF)
    operands = [*arrays, *weights, bias.reshape(1, inner)]
    specs = [ANY] * (len(arrays) + len(weights)) + [full((1, inner))]
    near = pl.BlockSpec((None, tile, width), lambda j, at: (early(j), 0, 0))
    kept = pl.BlockSpec((None, tile, width), lambda j, at: (later(j), 0, 0))
    return call(
        functools.partial(hidden_kernel, n, views, len(arrays), len(weights)),
        "hidden_layer",
        at,
        operands,
        specs,
        [wide, wide, pair, pair, pair, pair, jax.ShapeDtypeStruct((1, inner), F32)],
        [
            slot,
            slot,
            near,
            kept,
            near,
            kept,
            full((1, inner)),
        ],
        [
            pltpu.VMEM((n, tile, width), BF),
            pltpu.VMEM((n, tile, width), BF),
            pltpu.VMEM((width, inner), BF),
            pltpu.VMEM((inner, width), BF),
            pltpu.SemaphoreType.DMA((n,)),
            pltpu.SemaphoreType.DMA((n,)),
            pltpu.SemaphoreType.DMA((2 * shards,)),
        ],
        grid=n,
        flops=8 * n * tile * width * inner,
    )


def added(terms):
    total = terms[0][...].astype(F32)
    for term in terms[1:]:
        total = total + term[...].astype(F32)
    return total


def row_sum(values):
    return jnp.sum(values, axis=0, keepdims=True)


def second_kernel(b, terms_in, count, at_ref, *refs):
    terms, refs = refs[:terms_in], refs[terms_in:]
    weights, refs = refs[:count], refs[count:]
    residual_ref, cot_ref, gain_ref = refs[:3]
    rescot_ref, branch_ref, sums_ref, out_ref, t_s, r_s, c_s, w_s, sems, w_sems = refs[3:]
    copies = copies_of(
        [(residual_ref, r_s), (cot_ref.at[b], c_s)]
        + [(term.at[0], t_s.at[i]) for i, term in enumerate(terms)],
        sems,
    )
    weights = column_copies(weights, w_s, at_ref[0], w_sems)
    begin(copies)
    begin(weights)
    finish(copies)
    second_cot = added([t_s.at[i] for i in range(terms_in)])
    unit, rate = norm_stats(r_s[...])
    cot = c_s[...].astype(F32)
    residual_cot = cot + norm_back(second_cot, unit, rate, gain_ref[...])
    rescot_ref[...] = residual_cot
    branch = residual_cot.astype(BF)
    branch_ref[...] = branch
    sums_ref[0:1] = row_sum(second_cot * unit)
    sums_ref[1:2] = row_sum(second_cot)
    sums_ref[2:3] = row_sum(branch.astype(F32))
    sums_ref[3:4] = row_sum(cot)
    finish(weights)
    n, _, every = out_ref.shape
    for k in range(n):
        out_ref[k] = nt(branch, w_s[k * every : (k + 1) * every]).astype(BF)


def row_part(tile):
    return tile // 2


def stream_rows(b, part, width):
    return pl.BlockSpec((None, part, width), lambda i, at: (b, i, 0))


def row_block(part, width):
    return pl.BlockSpec((part, width), lambda i, at: (i, 0))


def second_back(at, b, terms, weights, residual, cotangent, gain, n):
    tile, width = residual.shape
    every = width // n
    return call(
        functools.partial(second_kernel, b, len(terms), len(weights)),
        "second_back",
        at,
        [*terms, *weights, residual, cotangent, gain.reshape(1, width)],
        [ANY] * (len(terms) + len(weights) + 2) + [full((1, width))],
        [
            jax.ShapeDtypeStruct((tile, width), F32),
            jax.ShapeDtypeStruct((tile, width), BF),
            jax.ShapeDtypeStruct((4, width), F32),
            jax.ShapeDtypeStruct((n, tile, every), BF),
        ],
        [full((tile, width))] * 2 + [full((4, width)), full((n, tile, every))],
        [
            pltpu.VMEM((len(terms), tile, width), BF),
            pltpu.VMEM((tile, width), F32),
            pltpu.VMEM((tile, width), BF),
            pltpu.VMEM((width, width), BF),
            pltpu.SemaphoreType.DMA((len(terms) + 2,)),
            pltpu.SemaphoreType.DMA((len(weights),)),
        ],
        flops=2 * tile * width * width,
    )


def first_kernel(count, at_ref, *refs):
    terms, refs = refs[:count], refs[count:]
    tokens_ref, rescot_ref, gain_ref = refs[:3]
    out_ref, sums_ref = refs[-2:]

    @pl.when(pl.program_id(0) == 0)
    def _():
        sums_ref[...] = jnp.zeros_like(sums_ref)

    first_cot = added(terms)
    unit, rate = norm_stats(tokens_ref[...].astype(F32))
    out_ref[...] = rescot_ref[...] + norm_back(first_cot, unit, rate, gain_ref[...])
    sums_ref[0:1] += row_sum(first_cot * unit)
    sums_ref[1:2] += row_sum(first_cot)


def first_back(at, b, terms, tokens, rescot, gain, held):
    batch, tile, width = tokens.shape
    part = row_part(tile)
    operands = [*terms, tokens, rescot, gain.reshape(1, width)]
    specs = [stream_rows(0, part, width)] * len(terms) + [
        stream_rows(b, part, width),
        row_block(part, width),
        full((1, width)),
    ]
    aliases = {}
    if held is not None:
        aliases = {1 + len(operands): 0}
        operands, specs = operands + [held], specs + [ANY]
    return call(
        functools.partial(first_kernel, len(terms)),
        "first_back",
        at,
        operands,
        specs,
        [jax.ShapeDtypeStruct((batch, tile, width), F32), jax.ShapeDtypeStruct((2, width), F32)],
        [stream_rows(b, part, width), full((2, width))],
        [],
        grid=tile // part,
        aliases=aliases,
    )


def result_kernel(count, at_ref, *refs):
    terms, refs = refs[:count], refs[count:]
    residual_ref, bias_ref, out_ref = refs[0], refs[1], refs[-1]
    out_ref[...] = (residual_ref[...] + added(terms) + bias_ref[...]).astype(BF)


def result_out(at, b, batch, terms, residual, bias, held):
    tile, width = residual.shape
    part = row_part(tile)
    operands = [*terms, residual, bias.reshape(1, width)]
    specs = [stream_rows(0, part, width)] * len(terms) + [row_block(part, width), full((1, width))]
    aliases = {}
    if held is not None:
        aliases = {1 + len(operands): 0}
        operands, specs = operands + [held], specs + [ANY]
    return call(
        functools.partial(result_kernel, len(terms)),
        "result_out",
        at,
        operands,
        specs,
        jax.ShapeDtypeStruct((batch, tile, width), BF),
        stream_rows(b, part, width),
        [],
        grid=tile // part,
        aliases=aliases,
    )


def tn(a, b):
    return lax.dot_general(a, b, (((0,), (0,)), ((), ())), preferred_element_type=F32)


def grad_kernel(count, products, slotted, split, row_of, at_ref, *refs):
    inputs, refs = refs[:count], refs[count:]
    outs, (a_s, b_s, acc_s, sems) = refs[:-4], refs[-4:]
    step = pl.program_id(0)
    s, f = at_ref[0], at_ref[1]
    part = acc_s.shape[1]
    width = b_s.shape[2]
    blocks = width // part
    plans, used = [], 0
    for p, (left, right) in enumerate(products):
        rows = b_s.shape[1] // len(right)
        cols = a_s.shape[2] // split
        pairs = []
        for i, (operand, lead) in enumerate(right):
            span = slice(i * rows, (i + 1) * rows)
            for c in range(split):
                o, l = left[i * split + c]
                view = inputs[o] if l is None else inputs[o].at[l]
                pairs.append((view, a_s.at[p, span, c * cols : (c + 1) * cols]))
            view = inputs[operand] if lead is None else inputs[operand].at[lead]
            pairs.append((view, b_s.at[p, span]))
        plans.append([pltpu.make_async_copy(*pair, sems.at[used + i]) for i, pair in enumerate(pairs)])
        used += len(pairs)

    @pl.when(step == 0)
    def _():
        for plan in plans:
            begin(plan)
        plan, groups = plans[0], len(products[0][1])
        rows = b_s.shape[1] // groups
        for i in range(groups):
            finish(plan[i * (split + 1) : (i + 1) * (split + 1)])
            span = slice(i * rows, (i + 1) * rows)
            found = tn(a_s[0, span], b_s[0, span, :part])
            if i == 0:
                acc_s[...] = found
            else:
                acc_s[...] += found

    for p in range(1, len(products)):

        @pl.when(step == p * blocks)
        def _(p=p):
            finish(plans[p])

    if blocks * len(products) > 1:

        @pl.when(step > 0)
        def _():
            p = step // blocks
            acc_s[...] = tn(a_s[p], b_s[p, :, lanes(step % blocks, part)])

    if slotted:
        odd_ref, even_ref = outs
        rows = odd_ref.shape[1]
        for k in range(2 * odd_ref.shape[0]):
            target = odd_ref if k & 1 else even_ref
            target[k >> 1] = acc_s[block_rows(row_of(s, f, k), rows)].astype(BF)
    else:
        (out_ref,) = outs
        rows = out_ref.shape[1]
        for k in range(out_ref.shape[0]):
            out_ref[k] = acc_s[k * rows : (k + 1) * rows].astype(BF)


def weight_grad(at, operands, products, shards, split=1, row_of=None):
    def shape_of(view):
        return operands[view[0]].shape[-2:]

    left, right = products[0]
    tokens = sum(shape_of(v)[0] for v in right)
    height, width = shape_of(left[0])[1] * split, shape_of(right[0])[1]
    part = width if width <= 256 or width % 256 else 256
    blocks, rows = width // part, height // shards
    if row_of is not None:
        shapes = [jax.ShapeDtypeStruct((shards // 2, rows, width), BF)] * 2
        specs = [pl.BlockSpec((shards // 2, rows, part), lambda j, at: (0, 0, j))] * 2
    else:
        shapes = jax.ShapeDtypeStruct((shards, len(products), rows, width), BF)
        specs = pl.BlockSpec((shards, None, rows, part), lambda j, at: (0, j // blocks, 0, j % blocks))
    return call(
        functools.partial(grad_kernel, len(operands), products, row_of is not None, split, row_of),
        "weight_grad",
        at,
        operands,
        [ANY] * len(operands),
        shapes,
        specs,
        [
            pltpu.VMEM((len(products), tokens, height), BF),
            pltpu.VMEM((len(products), tokens, width), BF),
            pltpu.VMEM((height, part), F32),
            pltpu.SemaphoreType.DMA((sum(len(a) + len(b) for a, b in products),)),
        ],
        grid=blocks * len(products),
        flops=2 * tokens * height * width * len(products),
    )


def strip_kernel(n, batch, at_ref, *refs):
    came, branch, refs = refs[:batch], refs[batch : 2 * batch], refs[2 * batch :]
    odd_ref, even_ref, a_s, b_s, sems = refs
    step = pl.program_id(0)
    tile, every = came[0].shape[1:]
    pairs = []
    for b in range(batch):
        span = slice(b * tile, (b + 1) * tile)
        pairs += [(came[b].at[k], a_s.at[span, k * every : (k + 1) * every]) for k in range(n)]
        pairs.append((branch[b], b_s.at[span]))
    copies = copies_of(pairs, sems)

    @pl.when(step == 0)
    def _():
        begin(copies)
        finish(copies)

    strip = odd_ref.shape[1]
    found = tn(a_s[...], b_s[:, lanes(slot_at(step, n) ^ at_ref[0], strip)]).astype(BF)

    @pl.when(step < n // 2)
    def _():
        odd_ref[...] = found

    @pl.when(step >= n // 2)
    def _():
        even_ref[...] = found


def strip_grad(at, came, branch):
    n, tile, every = came[0].shape
    batch, width = len(came), branch[0].shape[1]
    half, strip = n // 2, width // n
    block = (None, n * every, strip)
    return call(
        functools.partial(strip_kernel, n, batch),
        "strip_grad",
        at,
        [*came, *branch],
        [ANY] * (2 * batch),
        [jax.ShapeDtypeStruct((half, n * every, strip), BF)] * 2,
        [
            pl.BlockSpec(block, lambda j, at: (jnp.minimum(j, half - 1), 0, 0)),
            pl.BlockSpec(block, lambda j, at: (jnp.maximum(j - half, 0), 0, 0)),
        ],
        [
            pltpu.VMEM((batch * tile, n * every), BF),
            pltpu.VMEM((batch * tile, width), BF),
            pltpu.SemaphoreType.DMA((batch * (n + 1),)),
        ],
        grid=n,
        flops=2 * batch * tile * n * every * width,
    )


def body(
    n, shards,
    tokens, first_gain, first_shift, attention_weight, attention_bias, output_weight, output_bias,
    second_gain, second_shift, expand_weight, expand_bias, contract_weight, contract_bias,
    cotangent, threshold,
):
    batch, tile, width = tokens.shape
    rows, qkv = attention_weight.shape
    every = qkv // 3
    heads = every // HEAD
    inner_rows = contract_weight.shape[0]
    inner = inner_rows * shards // n
    piece = inner_rows // n
    ratio = shards // n
    strip = output_weight.shape[1]
    s = lax.axis_index("seq").astype(jnp.int32)
    f = lax.axis_index("fsdp").astype(jnp.int32)
    at = jnp.stack([s, f])
    streams = range(batch)
    joined = piece == rows

    strips = strip % 128 == 0 and qkv % 128 == 0

    sent = jnp.concatenate([attention_weight, output_weight], axis=1) if strips else attention_weight
    qkv_slots = gather_slots(sent, "fsdp", shards)
    qkv_pieces = [(a, None, k) for k, a in enumerate(qkv_slots)]
    unit, _ = norm_stats(tokens.astype(F32))
    normed_own = (unit * first_gain + first_shift).astype(BF)
    normed_first = gather_slots(normed_own, "seq", n, qkv_slots[1:])
    expand_weight, contract_weight, *_ = lax.optimization_barrier(
        (expand_weight, contract_weight, *(qkv_slots[bit] for bit in bits_of(shards)))
    )
    to_seq = jnp.concatenate(
        [
            jnp.swapaxes(expand_weight.reshape(rows, ratio, n, piece), 1, 2)
            .swapaxes(0, 1)
            .reshape(n, -1, strip),
            contract_weight.reshape(n, piece, strip),
        ],
        axis=1,
    )
    from_seq = lax.all_to_all(to_seq, "seq", 0, 0, tiled=True)
    cut = rows * ratio * piece // strip
    expand_rows = (
        from_seq[:, :cut].reshape(n, rows, ratio * piece).swapaxes(0, 1).reshape(rows, inner)
    )
    contract_rows = from_seq[:, cut:].swapaxes(0, 1).reshape(piece, width)
    if joined:
        stacked = after(jnp.stack([expand_rows, contract_rows]), *qkv_slots[1:], normed_first[n // 2])
        hidden_weights = [lax.all_gather(stacked, "fsdp")]
    else:
        hidden_weights = [lax.all_gather(w, "fsdp") for w in (expand_rows, contract_rows)]

    mixing_bias = lax.dynamic_slice_in_dim(attention_bias, s * qkv, qkv)
    inner_bias = lax.dynamic_index_in_dim(
        expand_bias.reshape(shards, n, piece), s, axis=1, keepdims=False
    ).reshape(inner)

    parts, outs, lse, peaks, came = ([None] * batch for _ in range(5))
    residual, pairs = [None] * batch, [None] * batch
    for b in streams:
        parts[b], outs[b], lse[b], peaks[b], extra = attend_forward(
            at, b, normed_first, qkv_pieces, mixing_bias, n, strip if strips and b == 0 else 0
        )
        sent = after(outs[b], came[b - 1]) if b else outs[b]
        came[b] = lax.all_to_all(sent, "seq", 0, 0, tiled=True)
        if b == 0:
            joint = extra
            cot_first = gather_slots(after(cotangent[0], normed_first[n // 2]), "seq", n, outs[:1])
    if strips:
        output_weights = gather_slots(after(joint[0], cot_first[n // 2]), "seq", n, outs[-1:])
    else:
        output_weights = [
            lax.all_gather(
                lax.all_gather(output_weight, "fsdp", tiled=True), "seq", axis=1, tiled=True
            )
        ]
    normed_own = [None] * batch
    for b in streams:
        residual[b], normed_own[b] = project(
            at, b, came[b], output_weights, tokens, output_bias, second_gain, second_shift,
            cotangent if b else None,
        )
    cot_pairs = [None] * batch
    for b in streams:
        if b == 0:
            own = gather_slots(after(normed_own[b], came[-1]), "seq", n, normed_own[-1:])
            pairs[b] = [(a, None, k) for k, a in enumerate(own)]
            cot_pairs[b] = [(a, None, k) for k, a in enumerate(cot_first)]
        else:
            own = gather_slots(after(normed_own[b], pairs[b - 1][n // 2][0]), "seq", n)
            pairs[b] = [(a, 0, k) for k, a in enumerate(own)]
            cot_pairs[b] = [(a, 1, k) for k, a in enumerate(own)]

    active, hidden_cot, inner_sums, rescot, branch, sums, cots = ([None] * batch for _ in range(7))
    second, out_parts, terms = [], [], None
    for b in streams:
        operands = list(pairs[b])
        if b:
            array = after(operands[0][0], second[-1][0])
            operands[0] = (array, *operands[0][1:])
        active[b], hidden_cot[b], odd, even, *out_part, inner_sums[b] = hidden_layer(
            at, operands, cot_pairs[b], hidden_weights, inner_bias
        )
        out_parts.append(out_part)
        odd = after(odd, second_terms[-1][-1] if b else pairs[-1][n // 2][0])
        if b == 0:
            second_terms = []
        second.append(scatter_near(odd, even, "seq", n))
        second_terms.append(scatter_far(*second[b], "seq", n))

    def second_step(b, *others):
        terms = second_terms[b]
        if others:
            terms[0] = after(terms[0], *others)
        rescot[b], branch[b], sums[b], slots = second_back(
            at, b, terms, output_weights, residual[b], cotangent, second_gain, n
        )
        cots[b] = lax.all_to_all(slots, "seq", 0, 0, tiled=True)

    second_step(0)

    def by_slot(first):
        return [(first + k, b) for b in streams for k in range(n)]

    def by_stream(first):
        return [(first + b, k) for b in streams for k in range(n)]

    def owned(s, f, k):
        return f ^ k

    arrays, views = arrays_of([v for b in streams for v in (*pairs[b], *cot_pairs[b])])
    views = [view[:2] for view in views]
    normed_views = [v for b in streams for v in views[2 * b * n : (2 * b + 1) * n]]
    cot_views = [v for b in streams for v in views[(2 * b + 1) * n : 2 * (b + 1) * n]]
    far = len(arrays)
    if joined:
        arrays[0] = after(arrays[0], second[-1][0], branch[0])
        both = weight_grad(
            at,
            [*arrays, *hidden_cot, *active],
            [(normed_views, by_stream(far)), (by_stream(far + batch), cot_views)],
            shards,
        )
        scattered = [lax.psum_scatter(after(both, cots[0], second_terms[-1][-1]), "fsdp")]
        done = [both]
    else:
        grad_expand = scatter_sum(
            *weight_grad(
                at, [*arrays, *hidden_cot], [(normed_views, by_stream(far))], shards, 1, owned
            ),
            "fsdp",
            shards,
        )
        grad_contract = scatter_sum(
            *weight_grad(at, [*arrays, *active], [(by_stream(far), cot_views)], shards, 1, owned),
            "fsdp",
            shards,
        )
        scattered, done = [grad_expand, grad_contract], []
    for b in streams[1:]:
        second_step(b, *done, cots[b - 1])
    if strips:
        output_odd, output_even = strip_grad(at, came, branch)
    else:
        product = functools.reduce(
            jnp.add,
            [
                jnp.einsum("kte,td->ked", came[b], branch[b], preferred_element_type=F32)
                for b in streams
            ],
        ).reshape(width, n, strip)
        output_odd, output_even = (
            jnp.stack(
                [
                    lax.dynamic_index_in_dim(product, s ^ k, 1, keepdims=False).astype(BF)
                    for k in range(first, n, 2)
                ]
            )
            for first in (1, 0)
        )
    cots[0] = after(cots[0], *done, output_odd)

    mixed_cot, mixing_sums, tail = [None] * batch, [None] * batch, [None] * batch
    input_grad = None
    near, block_output = None, None
    out_terms = [None] * batch
    first_terms = []
    for b in streams:
        cot = cots[b]
        if b == 0:
            out_near = scatter_near(after(out_parts[b][0], branch[-1]), out_parts[b][1], "seq", n)
            cot = after(cot, out_near[0])
            out_terms[b] = scatter_far(*out_near, "seq", n)
        else:
            cot = after(cot, near[0])
        mixed_cot[b], odd, even, mixing_sums[b] = attend_backward(
            at, parts[b], lse[b], outs[b], cot, qkv_pieces
        )
        odd = after(odd, out_terms[0][-1], *([terms[-1]] if b else []))
        near = scatter_near(odd, even, "seq", n)
        terms = scatter_far(*near, "seq", n)
        first_terms.append(terms)
        if b == batch - 1:
            grad_parts = weight_grad(
                at,
                [after(normed_first[0], near[0]), *normed_first[1:], *mixed_cot],
                [(by_slot(0), by_stream(n))],
                shards,
                1,
                owned,
            )
    for b in streams:
        first_terms[b][0] = after(first_terms[b][0], grad_parts[0])
        input_grad, tail[b] = first_back(
            at, b, first_terms[b], tokens, rescot[b], first_gain, input_grad
        )
    for b in streams[1:]:
        out_near = scatter_near(after(out_parts[b][0], near[0]), out_parts[b][1], "seq", n)
        out_terms[b] = scatter_far(after(out_near[0], terms[-1]), *out_near[1:], "seq", n)
    def over_streams(values):
        return functools.reduce(jnp.add, values)

    mine = jnp.arange(n) == s
    spread_inner = jnp.where(
        mine[None, :, None], over_streams(inner_sums).reshape(shards, 1, piece), 0.0
    )
    spread_mixing = jnp.where(mine[:, None], over_streams(mixing_sums), 0.0)
    peak = jnp.where(mine[:, None], functools.reduce(jnp.maximum, peaks)[None], -jnp.inf)
    top = jnp.pad(peak.reshape(-1), (0, 1024 - n * heads)).reshape(-1, 128)
    vectors = jnp.concatenate(
        [top]
        + [
            v.reshape(-1, 128)
            for v in (over_streams(sums), over_streams(tail), spread_inner, spread_mixing)
        ]
    )
    is_top = jnp.arange(vectors.shape[0])[:, None] < top.shape[0]

    def summed(vectors, axis, size, bits):
        for bit in bits:
            other = swap(vectors, axis, size, bit)
            vectors = jnp.where(is_top, jnp.maximum(vectors, other), vectors + other)
        return vectors

    near_bit, far_bits = bits_of(shards)[0], bits_of(shards)[1:]
    vectors = summed(vectors, "fsdp", shards, far_bits)
    output_near = scatter_near(output_odd, output_even, "seq", n)
    output_terms = scatter_far(*output_near, "seq", n)
    output_terms[-1] = after(output_terms[-1], grad_parts[0])
    output = functools.reduce(jnp.add, [a[0].astype(F32) for a in output_terms])
    order = [*far_bits, near_bit]
    kept, other, left = scatter_half(
        output.reshape(*[2] * len(order), rows, strip), f, "fsdp", shards, order[0],
        bits_of(shards)[::-1],
    )
    held = {}

    def first_step(came):
        came, *held["hidden"] = lax.optimization_barrier((came, *scattered))
        first = summed(after(vectors, came), "fsdp", shards, [near_bit])
        first = summed(first, "seq", n, bits_of(n)[:-1])
        held["vectors"] = first, swap(first, "seq", n, bits_of(n)[-1])
        for b in streams[:-1]:
            out_terms[b][0] = after(out_terms[b][0], came)
        held["output"] = scatter_half(
            kept + after(other, came).astype(F32), f, "fsdp", shards, order[1], left
        )
        return came

    def second_step_over(came):
        came, *held["hidden"] = lax.optimization_barrier((came, *held["hidden"]))
        first, last = held["vectors"]
        last = after(last, came)
        held["vectors"] = jnp.where(is_top, jnp.maximum(first, last), first + last)
        kept, other, left = held["output"]
        held["output"] = kept, after(other, came), left
        out_terms[-1][0] = after(out_terms[-1][0], came)
        return came

    grad_mixing = scatter_sum(*grad_parts, "fsdp", shards, [first_step, second_step_over])
    for b in streams:
        block_output = result_out(
            at, b, batch, out_terms[b], residual[b], contract_bias, block_output
        )
    vectors, (kept, other, left) = held["vectors"], held["output"]
    for bit in order[2:]:
        kept, other, left = scatter_half(
            kept + other.astype(F32), f, "fsdp", shards, bit, left
        )
    grad_output_own = kept + other.astype(F32)
    grad_expand, grad_contract = held["hidden"][0] if joined else held["hidden"]
    back = lax.all_to_all(
        jnp.concatenate(
            [
                grad_expand.astype(BF)
                .reshape(rows, n, ratio * piece)
                .swapaxes(0, 1)
                .reshape(n, cut, strip),
                grad_contract.astype(BF).reshape(piece, n, strip).swapaxes(0, 1),
            ],
            axis=1,
        ),
        "seq",
        0,
        0,
        tiled=True,
    )
    grad_expand_own = (
        back[:, :cut]
        .reshape(n, rows, ratio, piece)
        .transpose(1, 2, 0, 3)
        .reshape(rows, ratio * n * piece)
        .astype(F32)
    )
    grad_contract_own = back[:, cut:].reshape(inner_rows, strip).astype(F32)
    vectors = vectors.reshape(-1)
    ends = [1024]
    for length in [width] * 6 + [n * inner, n * qkv]:
        ends.append(ends[-1] + length)
    (
        second_gain_sum, second_shift_sum, output_sum, contract_sum, first_gain_sum, first_shift_sum,
        inner_sum, mixing_sum,
    ) = (vectors[a:b] for a, b in zip(ends, ends[1:]))

    head_peak = lax.dynamic_slice_in_dim(vectors, s * heads, heads)
    factor = jnp.sqrt(threshold[0] / jnp.maximum(head_peak, threshold[0]))
    multiplier = jnp.broadcast_to(
        jnp.stack([factor, factor, jnp.ones_like(factor)], axis=1)[:, :, None], (heads, 3, HEAD)
    ).reshape(qkv)
    clipped_weight = attention_weight.astype(F32) * multiplier[None, :]
    clipped_bias = mixing_bias * multiplier

    return (
        block_output,
        input_grad,
        first_gain_sum,
        first_shift_sum,
        grad_mixing,
        mixing_sum,
        grad_output_own,
        output_sum,
        second_gain_sum,
        second_shift_sum,
        grad_expand_own,
        inner_sum,
        grad_contract_own,
        contract_sum,
        head_peak,
        clipped_weight,
        clipped_bias,
    )


def solution(mesh):
    grid, both, whole, line = P("fsdp", "seq"), P("fsdp", "seq", None), P(), P("seq")
    return jax.shard_map(
        functools.partial(body, mesh.shape["seq"], mesh.shape["fsdp"]),
        mesh=mesh,
        in_specs=(
            both, whole, whole, grid, whole, grid, whole, whole, whole, grid, whole, grid, whole,
            both, whole,
        ),
        out_specs=(
            both, both, whole, whole, grid, whole, grid, whole, whole, whole, grid, whole, grid,
            whole, line, grid, line,
        ),
        check_vma=False,
    )
```

```python
import functools
import math

import jax
import jax.numpy as jnp
from jax import lax
from jax.experimental import pallas as pl
from jax.experimental.pallas import tpu as pltpu
from jax.sharding import PartitionSpec as P

HEAD = 64
LOG2E = math.log2(math.e)
BF = jnp.bfloat16
F32 = jnp.float32
ANY = pl.BlockSpec(memory_space=pl.ANY)


def swap(value, axis, size, bit):
    return lax.ppermute(value, axis, [(i, i ^ bit) for i in range(size)])


def bits_of(size):
    return [1 << p for p in range(size.bit_length() - 1)]


def gather_slots(value, axis, size, wait=()):
    slots = {0: value}
    for bit in reversed(bits_of(size)):
        for k in list(slots):
            sent = after(slots[k], *wait) if k and wait else slots[k]
            slots[k | bit] = swap(sent, axis, size, bit)
    return [slots[k] for k in range(size)]


def scatter_near(odd, even, axis, size):
    came = swap(odd, axis, size, 1)
    total = even.astype(F32) + came.astype(F32)
    return total[1::2].astype(BF), total[0::2], [even, came]


def scatter_far(sent, rest, terms, axis, size):
    terms = list(terms)
    for bit in bits_of(size)[1:]:
        came = swap(sent, axis, size, bit)
        terms.append(came)
        if came.shape[0] > 1:
            rest = rest + came.astype(F32)
            sent, rest = rest[1::2].astype(BF), rest[0::2]
    return terms


def scatter_sum(odd, even, axis, size, hooks=()):
    rest, sent = even.astype(F32), odd
    for step, bit in enumerate(bits_of(size)):
        came = swap(sent, axis, size, bit)
        if step < len(hooks):
            came = hooks[step](came)
        rest = rest + came.astype(F32)
        if rest.shape[0] > 1:
            sent, rest = rest[1::2].astype(BF), rest[0::2]
    return rest[0]


def scatter_half(value, index, axis, size, bit, left):
    at = left.index(bit)
    own = ((index & bit) != 0).astype(jnp.int32)
    sent = lax.dynamic_index_in_dim(value, 1 - own, at, keepdims=False).astype(BF)
    kept = lax.dynamic_index_in_dim(value, own, at, keepdims=False).astype(F32)
    return kept, swap(sent, axis, size, bit), [b for b in left if b != bit]


def after(value, *others):
    return lax.optimization_barrier((value, *others))[0]


def nn(a, b):
    return lax.dot_general(a, b, (((1,), (0,)), ((), ())), preferred_element_type=F32)


def nt(a, b):
    return lax.dot_general(a, b, (((1,), (1,)), ((), ())), preferred_element_type=F32)


def full(shape):
    return pl.BlockSpec(shape, lambda i, at: (0,) * len(shape))


def entry(shape, at_entry=0):
    return pl.BlockSpec((None, *shape), lambda i, at: (at_entry,) + (0,) * len(shape))


def call(kernel, name, at, operands, in_specs, out_shape, out_specs, scratch, grid=1, flops=0, aliases=None):
    moved = sum(math.prod(o.shape) * o.dtype.itemsize for o in operands)
    return pl.pallas_call(
        kernel,
        out_shape=out_shape,
        grid_spec=pltpu.PrefetchScalarGridSpec(
            num_scalar_prefetch=1,
            grid=(grid,),
            in_specs=in_specs,
            out_specs=out_specs,
            scratch_shapes=scratch,
        ),
        compiler_params=pltpu.CompilerParams(vmem_limit_bytes=58 << 20),
        cost_estimate=pl.CostEstimate(flops=flops, transcendentals=0, bytes_accessed=moved),
        input_output_aliases=aliases or {},
        name=name,
    )(at, *operands)


def copies_of(pairs, sems):
    return [pltpu.make_async_copy(src, dst, sems.at[i]) for i, (src, dst) in enumerate(pairs)]


def begin(copies):
    for copy in copies:
        copy.start()


def finish(copies):
    for copy in copies:
        copy.wait()


def block_rows(index, rows):
    return pl.ds(pl.multiple_of(index * rows, rows), rows)


def weight_pairs(refs, views, target, f, start=0):
    rows = target.shape[0] // len(views)
    pairs = []
    for i, lead, slot in views:
        source = refs[i] if lead is None else refs[i].at[lead]
        if source.shape[-1] > target.shape[-1]:
            source = source.at[:, start : start + target.shape[-1]]
        pairs.append((source, target.at[block_rows(f ^ slot, rows)]))
    return pairs


def arrays_of(views):
    arrays, found = [], []
    for array, lead, slot in views:
        place = next((i for i, a in enumerate(arrays) if a is array), len(arrays))
        if place == len(arrays):
            arrays.append(array)
        found.append((place, lead, slot))
    return arrays, found


def head_mask(width, head):
    return (lax.broadcasted_iota(jnp.int32, (1, width), 1) // HEAD) == head


def causal(tile):
    keys = lax.broadcasted_iota(jnp.int32, (tile, tile), 0)
    queries = lax.broadcasted_iota(jnp.int32, (tile, tile), 1)
    return keys <= queries


def lanes(group, width):
    return pl.ds(pl.multiple_of(group * width, width), width)


def join(parts, axis):
    return parts[0] if len(parts) == 1 else jnp.concatenate(parts, axis=axis)


def forward_kernel(n, b, views, count, at_ref, *refs):
    normed, refs = refs[:n], refs[n:]
    pieces, refs = refs[:count], refs[count:]
    bias_ref, q_ref, k_ref, v_ref, o_ref, lse_ref, peak_ref = refs[:7]
    x_s, w_s, vt_s, x_sems, w_sems, e_sems = refs[-6:]
    s, f = at_ref[0], at_ref[1]
    _, tile, _ = x_s.shape
    extra = []
    if len(refs) == 14:
        extra = copies_of(weight_pairs(pieces, views, refs[7], f, w_s.shape[1]), e_sems)
    every = q_ref.shape[1]
    width = 128 if every % 128 == 0 else every
    heads, factor = width // HEAD, HEAD**-0.5 * LOG2E
    w_copies = copies_of(weight_pairs(pieces, views, w_s, f), w_sems)
    x_copies = copies_of([(normed[k].at[b], x_s.at[k]) for k in range(n)], x_sems)
    begin(w_copies)
    begin(x_copies)
    begin(extra)
    finish(w_copies)
    for k in range(n):
        x_copies[k].wait()
        mixed = (nn(x_s[k], w_s[...]) + bias_ref[...]).astype(BF)
        spot = block_rows(k ^ s, tile)
        parts = [
            join([mixed[:, (3 * h + j) * HEAD : (3 * h + j + 1) * HEAD] for h in range(every // HEAD)], 1)
            for j in range(3)
        ]
        q_ref[spot], k_ref[spot], v_ref[spot] = parts
        vt_s[:, spot] = parts[2].T

    @pl.loop(0, every // width)
    def _(g):
        cols = lanes(g, width)
        peaks = [None] * heads
        for i in range(n):
            q_tile = q_ref[i * tile : (i + 1) * tile, cols]
            limit = (i + 1) * tile
            step = min(limit, 4 * tile)
            outs = []
            for h in range(heads):
                q = jnp.where(head_mask(width, h), q_tile, jnp.zeros_like(q_tile))
                v_rows = pl.ds(pl.multiple_of(g * width + h * HEAD, HEAD), HEAD)
                top = total = acc = None
                for start in range(0, limit, step):
                    stop = min(start + step, limit)
                    found = nt(k_ref[start:stop, cols], q)
                    if stop == limit:
                        edge = stop - start - tile
                        masked = jnp.where(causal(tile), found[edge:], -jnp.inf)
                        found = masked if edge == 0 else jnp.concatenate([found[:edge], masked], axis=0)
                    high = jnp.max(found, axis=0, keepdims=True)
                    new_top = high if top is None else jnp.maximum(top, high)
                    grown = jnp.exp2((found - new_top) * factor)
                    part = jnp.sum(grown, axis=0, keepdims=True)
                    mixed = nn(vt_s[v_rows, start:stop], grown.astype(BF))
                    if top is None:
                        total, acc = part, mixed
                    else:
                        shrink = jnp.exp2((top - new_top) * factor)
                        total, acc = total * shrink + part, acc * shrink + mixed
                    top = new_top
                outs.append(acc / total)
                lse_ref[g, h : h + 1, i * tile : (i + 1) * tile] = top * factor + jnp.log2(total)
                peaks[h] = top if peaks[h] is None else jnp.maximum(peaks[h], top)
            o_ref[i, :, cols] = join(outs, 0).T.astype(BF)
        for h in range(heads):
            peak_ref[g, h : h + 1, :] = peaks[h] * HEAD**-0.5

    finish(extra)


def attend_forward(at, b, normed, pieces, bias, n, strip=0):
    _, tile, width = normed[0].shape
    arrays, views = arrays_of(pieces)
    qkv = bias.shape[0]
    every, length = qkv // 3, n * tile
    group = 128 if every % 128 == 0 else every
    part = jax.ShapeDtypeStruct((length, every), BF)
    stats = [(every // group, group // HEAD, length), (every // group, group // HEAD, tile)]
    found = call(
        functools.partial(forward_kernel, n, b, views, len(arrays)),
        "attend_forward",
        at,
        [*normed, *arrays, bias.reshape(1, qkv)],
        [ANY] * (n + len(arrays)) + [full((1, qkv))],
        [part] * 3
        + [jax.ShapeDtypeStruct((n, tile, every), BF)]
        + [jax.ShapeDtypeStruct(shape, F32) for shape in stats]
        + ([jax.ShapeDtypeStruct((width, strip), BF)] if strip else []),
        [full((length, every))] * 3
        + [full((n, tile, every))]
        + [full(shape) for shape in stats]
        + ([full((width, strip))] if strip else []),
        [
            pltpu.VMEM((n, tile, width), BF),
            pltpu.VMEM((width, qkv), BF),
            pltpu.VMEM((every, length), BF),
            pltpu.SemaphoreType.DMA((n,)),
            pltpu.SemaphoreType.DMA((len(views),)),
            pltpu.SemaphoreType.DMA((len(views),)),
        ],
        flops=2 * length * width * qkv + 8 * length * length * every,
    )
    parts, (out, lse, peak), extra = found[:3], found[3:6], found[6:]
    return parts, out, lse, jnp.max(peak, axis=-1).reshape(-1), extra


def backward_kernel(n, views, count, at_ref, *refs):
    q_ref, k_ref, v_ref, lse_ref, o_ref, g_ref = refs[:6]
    pieces, refs = refs[6 : 6 + count], refs[6 + count :]
    mix_ref, odd_ref, even_ref, bias_ref, w_s, kt_s, dq_s, dk_s, dv_s, mix_s, w_sems = refs
    s, f = at_ref[0], at_ref[1]
    _, tile, qkv = mix_ref.shape
    every, scale = qkv // 3, HEAD**-0.5
    width = 128 if every % 128 == 0 else every
    heads, factor = width // HEAD, scale * LOG2E
    w_copies = copies_of(weight_pairs(pieces, views, w_s, f), w_sems)
    begin(w_copies)
    kt_s[...] = k_ref[...].T

    @pl.loop(0, every // width)
    def _(g):
        cols = lanes(g, width)
        for i in reversed(range(n)):
            rows = slice(i * tile, (i + 1) * tile)
            limit = (i + 1) * tile
            step = min(limit, 4 * tile)
            q_tile, g_tile = q_ref[rows, cols], g_ref[i, :, cols]
            inner = (g_tile.astype(F32) * o_ref[i, :, cols].astype(F32)).T
            outs = []
            for h in range(heads):
                mask = head_mask(width, h)
                q = jnp.where(mask, q_tile, jnp.zeros_like(q_tile))
                cot = jnp.where(mask, g_tile, jnp.zeros_like(g_tile))
                delta = jnp.sum(inner[h * HEAD : (h + 1) * HEAD], axis=0, keepdims=True)
                lse = lse_ref[g, h : h + 1, rows]
                k_rows = pl.ds(pl.multiple_of(g * width + h * HEAD, HEAD), HEAD)
                acc = None
                for start in range(0, limit, step):
                    stop = min(start + step, limit)
                    probs = jnp.exp2(nt(k_ref[start:stop, cols], q) * factor - lse)
                    if stop == limit:
                        edge = stop - start - tile
                        masked = jnp.where(causal(tile), probs[edge:], 0.0)
                        probs = masked if edge == 0 else jnp.concatenate([probs[:edge], masked], axis=0)
                    spread = nt(v_ref[start:stop, cols], cot)
                    logit_cot = (probs * (spread - delta)).astype(BF)
                    dv_part = nn(probs.astype(BF), cot)
                    dk_part = nn(logit_cot, q)
                    if i == n - 1 and h == 0:
                        dv_s[start:stop] = dv_part
                        dk_s[start:stop] = dk_part
                    else:
                        dv_s[start:stop] += dv_part
                        dk_s[start:stop] += dk_part
                    dq_part = nn(kt_s[k_rows, start:stop], logit_cot)
                    acc = dq_part if acc is None else acc + dq_part
                outs.append(acc)
            dq_s[rows] = (join(outs, 0).T * scale).astype(BF)
        for i in range(n):
            rows = slice(i * tile, (i + 1) * tile)
            dq = dq_s[rows]
            dk = (dk_s[rows] * scale).astype(BF)
            dv = dv_s[rows].astype(BF)
            mix_s[rows, lanes(g, 3 * width)] = jnp.concatenate(
                [a[:, h * HEAD : (h + 1) * HEAD] for h in range(heads) for a in (dq, dk, dv)], axis=1
            )

    finish(w_copies)
    total = jnp.zeros((1, qkv), F32)
    for k in range(n):
        mixed_cot = mix_s[block_rows(k ^ s, tile)]
        mix_ref[k] = mixed_cot
        total = total + jnp.sum(mixed_cot.astype(F32), axis=0, keepdims=True)
        target = odd_ref if k & 1 else even_ref
        target[k >> 1] = nt(mixed_cot, w_s[...]).astype(BF)
    bias_ref[...] = total


def attend_backward(at, parts, lse, out, cot, pieces):
    n, tile, every = out.shape
    length, qkv = n * tile, 3 * every
    arrays, views = arrays_of(pieces)
    width = len(views) * arrays[0].shape[-2]
    group = 128 if every % 128 == 0 else every
    half = (n // 2, tile, width)
    return call(
        functools.partial(backward_kernel, n, views, len(arrays)),
        "attend_backward",
        at,
        [*parts, lse, out, cot, *arrays],
        [full((length, every))] * 3
        + [full(lse.shape)]
        + [full((n, tile, every))] * 2
        + [ANY] * len(arrays),
        [
            jax.ShapeDtypeStruct((n, tile, qkv), BF),
            jax.ShapeDtypeStruct(half, BF),
            jax.ShapeDtypeStruct(half, BF),
            jax.ShapeDtypeStruct((1, qkv), F32),
        ],
        [full((n, tile, qkv)), full(half), full(half), full((1, qkv))],
        [
            pltpu.VMEM((width, qkv), BF),
            pltpu.VMEM((every, length), BF),
            pltpu.VMEM((length, group), BF),
            pltpu.VMEM((length, group), F32),
            pltpu.VMEM((length, group), F32),
            pltpu.VMEM((length, qkv), BF),
            pltpu.SemaphoreType.DMA((len(views),)),
        ],
        flops=2 * length * width * qkv + 20 * length * length * every,
    )


def norm_stats(values):
    centered = values - jnp.mean(values, axis=-1, keepdims=True)
    rate = lax.rsqrt(jnp.mean(centered * centered, axis=-1, keepdims=True) + 1e-05)
    return centered * rate, rate


def norm_back(cot, unit, rate, gain):
    e = cot * gain
    return rate * (
        e
        - jnp.mean(e, axis=-1, keepdims=True)
        - unit * jnp.mean(e * unit, axis=-1, keepdims=True)
    )


def column_copies(refs, target, s, sems):
    strip = refs[0].shape[1]
    if len(refs) == 1:
        return copies_of([(refs[0], target)], sems)
    return copies_of([(ref, target.at[:, lanes(k ^ s, strip)]) for k, ref in enumerate(refs)], sems)


def project_kernel(count, paired, at_ref, *refs):
    came_ref, weights, refs = refs[0], refs[1 : 1 + count], refs[1 + count :]
    tokens_ref, bias_ref, gain_ref, shift_ref = refs[:4]
    residual_ref, normed_ref, c_s, w_s, c_sem, w_sems = refs[-6:]
    if paired:
        normed_ref[1] = refs[4][...]
        normed_ref = normed_ref.at[0]
    n, _, every = came_ref.shape
    copy = pltpu.make_async_copy(came_ref, c_s, c_sem)
    weights = column_copies(weights, w_s, at_ref[0], w_sems)
    copy.start()
    begin(weights)
    total = tokens_ref[...].astype(F32) + bias_ref[...]
    copy.wait()
    finish(weights)
    for k in range(n):
        total = total + nn(c_s[k], w_s[k * every : (k + 1) * every])
    residual_ref[...] = total
    unit, _ = norm_stats(total)
    normed_ref[...] = (unit * gain_ref[...] + shift_ref[...]).astype(BF)


def project(at, b, came, weights, tokens, bias, gain, shift, cotangent=None):
    _, tile, width = tokens.shape
    n, _, every = came.shape
    row, block = full((1, width)), entry((tile, width), b)
    paired = cotangent is not None
    shape = (2, tile, width) if paired else (tile, width)
    return call(
        functools.partial(project_kernel, len(weights), paired),
        "project",
        at,
        [came, *weights, tokens, *(v.reshape(1, width) for v in (bias, gain, shift))]
        + ([cotangent] if paired else []),
        [ANY] * (1 + len(weights)) + [block, row, row, row] + ([block] if paired else []),
        [jax.ShapeDtypeStruct((tile, width), F32), jax.ShapeDtypeStruct(shape, BF)],
        [full((tile, width)), full(shape)],
        [
            pltpu.VMEM((n, tile, every), BF),
            pltpu.VMEM((width, width), BF),
            pltpu.SemaphoreType.DMA,
            pltpu.SemaphoreType.DMA((len(weights),)),
        ],
        flops=2 * tile * width * width,
    )


def gelu_pair(v):
    k0 = math.sqrt(2.0 / math.pi)
    square = v * v
    t = jnp.tanh(v * (k0 + (k0 * 0.044715) * square))
    half = 0.5 + 0.5 * t
    slope = half + (0.5 * v) * (1.0 - t * t) * (k0 + (3.0 * 0.044715 * k0) * square)
    return v * half, slope


def slot_at(step, n):
    half = n // 2
    return jnp.where(step < half, 2 * step + 1, 2 * (step - half))


def hidden_kernel(n, views, arrays, count, at_ref, *refs):
    inputs, refs = refs[:arrays], refs[arrays:]
    found = [inputs[i] if lead is None else inputs[i].at[lead] for i, lead, _ in views]
    normed, cots = found[:n], found[n:]
    weights_in, refs = refs[:count], refs[count:]
    bias_ref = refs[0]
    active_ref, cot_ref, odd_ref, even_ref, out_odd_ref, out_even_ref, sum_ref = refs[1:8]
    x_s, c_s, expand_s, contract_s, x_sems, c_sems, w_sems = refs[8:]
    step = pl.program_id(0)
    k = slot_at(step, n)
    shards, inner = weights_in[0].shape[0], expand_s.shape[1]
    first = [weights_in[0].at[i, 0] if count == 1 else weights_in[0].at[i] for i in range(shards)]
    second = [weights_in[0].at[i, 1] if count == 1 else weights_in[1].at[i] for i in range(shards)]
    e_rows, c_rows = expand_s.shape[0] // shards, contract_s.shape[0] // shards
    order = list(range(1, n, 2)) + list(range(0, n, 2))
    x_copies = copies_of([(normed[j], x_s.at[j]) for j in order], x_sems)
    c_copies = copies_of([(cots[j], c_s.at[j]) for j in order], c_sems)
    weights = copies_of(
        [(a, expand_s.at[i * e_rows : (i + 1) * e_rows]) for i, a in enumerate(first)]
        + [(a, contract_s.at[i * c_rows : (i + 1) * c_rows]) for i, a in enumerate(second)],
        w_sems,
    )

    @pl.when(step == 0)
    def _():
        begin(x_copies[:1] + weights[:shards] + c_copies[:1] + weights[shards:])
        begin(x_copies[1:] + c_copies[1:])
        sum_ref[...] = jnp.zeros_like(sum_ref)

    for j in range(n):

        @pl.when(step == j)
        def _(j=j):
            if j == 0:
                finish(weights)
            x_copies[j].wait()
            c_copies[j].wait()

    part = min(inner, 256)
    x, c = x_s[k], c_s[k]
    for start in range(0, inner, part):
        cols = slice(start, start + part)
        hidden = nn(x, expand_s[:, cols]) + bias_ref[:, cols]
        value, slope = gelu_pair(hidden)
        active_ref[:, cols] = value.astype(BF)
        hidden_cot = (nt(c, contract_s[cols]) * slope).astype(BF)
        cot_ref[:, cols] = hidden_cot
        sum_ref[:, cols] += jnp.sum(hidden_cot.astype(F32), axis=0, keepdims=True)
    partial = nt(cot_ref[...], expand_s[...]).astype(BF)
    out = nn(active_ref[...], contract_s[...]).astype(BF)

    @pl.when(step < n // 2)
    def _():
        odd_ref[...] = partial
        out_odd_ref[...] = out

    @pl.when(step >= n // 2)
    def _():
        even_ref[...] = partial
        out_even_ref[...] = out


def hidden_layer(at, normed, cots, weights, bias):
    n = len(normed)
    arrays, views = arrays_of([*normed, *cots])
    tile, width = arrays[0].shape[-2:]
    inner = bias.shape[0]
    shards = weights[0].shape[0]
    half = n // 2
    slot = pl.BlockSpec((None, tile, inner), lambda j, at: (slot_at(j, n), 0, 0))
    early = lambda j: jnp.minimum(j, half - 1)
    later = lambda j: jnp.maximum(j - half, 0)
    pair = jax.ShapeDtypeStruct((half, tile, width), BF)
    wide = jax.ShapeDtypeStruct((n, tile, inner), BF)
    operands = [*arrays, *weights, bias.reshape(1, inner)]
    specs = [ANY] * (len(arrays) + len(weights)) + [full((1, inner))]
    near = pl.BlockSpec((None, tile, width), lambda j, at: (early(j), 0, 0))
    kept = pl.BlockSpec((None, tile, width), lambda j, at: (later(j), 0, 0))
    return call(
        functools.partial(hidden_kernel, n, views, len(arrays), len(weights)),
        "hidden_layer",
        at,
        operands,
        specs,
        [wide, wide, pair, pair, pair, pair, jax.ShapeDtypeStruct((1, inner), F32)],
        [
            slot,
            slot,
            near,
            kept,
            near,
            kept,
            full((1, inner)),
        ],
        [
            pltpu.VMEM((n, tile, width), BF),
            pltpu.VMEM((n, tile, width), BF),
            pltpu.VMEM((width, inner), BF),
            pltpu.VMEM((inner, width), BF),
            pltpu.SemaphoreType.DMA((n,)),
            pltpu.SemaphoreType.DMA((n,)),
            pltpu.SemaphoreType.DMA((2 * shards,)),
        ],
        grid=n,
        flops=8 * n * tile * width * inner,
    )


def added(terms):
    total = terms[0][...].astype(F32)
    for term in terms[1:]:
        total = total + term[...].astype(F32)
    return total


def row_sum(values):
    return jnp.sum(values, axis=0, keepdims=True)


def second_kernel(b, terms_in, count, at_ref, *refs):
    terms, refs = refs[:terms_in], refs[terms_in:]
    weights, refs = refs[:count], refs[count:]
    residual_ref, cot_ref, gain_ref = refs[:3]
    rescot_ref, branch_ref, sums_ref, out_ref, t_s, r_s, c_s, w_s, sems, w_sems = refs[3:]
    copies = copies_of(
        [(residual_ref, r_s), (cot_ref.at[b], c_s)]
        + [(term.at[0], t_s.at[i]) for i, term in enumerate(terms)],
        sems,
    )
    weights = column_copies(weights, w_s, at_ref[0], w_sems)
    begin(copies)
    begin(weights)
    finish(copies)
    second_cot = added([t_s.at[i] for i in range(terms_in)])
    unit, rate = norm_stats(r_s[...])
    cot = c_s[...].astype(F32)
    residual_cot = cot + norm_back(second_cot, unit, rate, gain_ref[...])
    rescot_ref[...] = residual_cot
    branch = residual_cot.astype(BF)
    branch_ref[...] = branch
    sums_ref[0:1] = row_sum(second_cot * unit)
    sums_ref[1:2] = row_sum(second_cot)
    sums_ref[2:3] = row_sum(branch.astype(F32))
    sums_ref[3:4] = row_sum(cot)
    finish(weights)
    n, _, every = out_ref.shape
    for k in range(n):
        out_ref[k] = nt(branch, w_s[k * every : (k + 1) * every]).astype(BF)


def row_part(tile):
    return tile // 2


def stream_rows(b, part, width):
    return pl.BlockSpec((None, part, width), lambda i, at: (b, i, 0))


def row_block(part, width):
    return pl.BlockSpec((part, width), lambda i, at: (i, 0))


def second_back(at, b, terms, weights, residual, cotangent, gain, n):
    tile, width = residual.shape
    every = width // n
    return call(
        functools.partial(second_kernel, b, len(terms), len(weights)),
        "second_back",
        at,
        [*terms, *weights, residual, cotangent, gain.reshape(1, width)],
        [ANY] * (len(terms) + len(weights) + 2) + [full((1, width))],
        [
            jax.ShapeDtypeStruct((tile, width), F32),
            jax.ShapeDtypeStruct((tile, width), BF),
            jax.ShapeDtypeStruct((4, width), F32),
            jax.ShapeDtypeStruct((n, tile, every), BF),
        ],
        [full((tile, width))] * 2 + [full((4, width)), full((n, tile, every))],
        [
            pltpu.VMEM((len(terms), tile, width), BF),
            pltpu.VMEM((tile, width), F32),
            pltpu.VMEM((tile, width), BF),
            pltpu.VMEM((width, width), BF),
            pltpu.SemaphoreType.DMA((len(terms) + 2,)),
            pltpu.SemaphoreType.DMA((len(weights),)),
        ],
        flops=2 * tile * width * width,
    )


def first_kernel(count, at_ref, *refs):
    terms, refs = refs[:count], refs[count:]
    tokens_ref, rescot_ref, gain_ref = refs[:3]
    out_ref, sums_ref = refs[-2:]

    @pl.when(pl.program_id(0) == 0)
    def _():
        sums_ref[...] = jnp.zeros_like(sums_ref)

    first_cot = added(terms)
    unit, rate = norm_stats(tokens_ref[...].astype(F32))
    out_ref[...] = rescot_ref[...] + norm_back(first_cot, unit, rate, gain_ref[...])
    sums_ref[0:1] += row_sum(first_cot * unit)
    sums_ref[1:2] += row_sum(first_cot)


def first_back(at, b, terms, tokens, rescot, gain, held):
    batch, tile, width = tokens.shape
    part = row_part(tile)
    operands = [*terms, tokens, rescot, gain.reshape(1, width)]
    specs = [stream_rows(0, part, width)] * len(terms) + [
        stream_rows(b, part, width),
        row_block(part, width),
        full((1, width)),
    ]
    aliases = {}
    if held is not None:
        aliases = {1 + len(operands): 0}
        operands, specs = operands + [held], specs + [ANY]
    return call(
        functools.partial(first_kernel, len(terms)),
        "first_back",
        at,
        operands,
        specs,
        [jax.ShapeDtypeStruct((batch, tile, width), F32), jax.ShapeDtypeStruct((2, width), F32)],
        [stream_rows(b, part, width), full((2, width))],
        [],
        grid=tile // part,
        aliases=aliases,
    )


def result_kernel(count, at_ref, *refs):
    terms, refs = refs[:count], refs[count:]
    residual_ref, bias_ref, out_ref = refs[0], refs[1], refs[-1]
    out_ref[...] = (residual_ref[...] + added(terms) + bias_ref[...]).astype(BF)


def result_out(at, b, batch, terms, residual, bias, held):
    tile, width = residual.shape
    part = row_part(tile)
    operands = [*terms, residual, bias.reshape(1, width)]
    specs = [stream_rows(0, part, width)] * len(terms) + [row_block(part, width), full((1, width))]
    aliases = {}
    if held is not None:
        aliases = {1 + len(operands): 0}
        operands, specs = operands + [held], specs + [ANY]
    return call(
        functools.partial(result_kernel, len(terms)),
        "result_out",
        at,
        operands,
        specs,
        jax.ShapeDtypeStruct((batch, tile, width), BF),
        stream_rows(b, part, width),
        [],
        grid=tile // part,
        aliases=aliases,
    )


def tn(a, b):
    return lax.dot_general(a, b, (((0,), (0,)), ((), ())), preferred_element_type=F32)


def grad_kernel(count, products, slotted, split, row_of, at_ref, *refs):
    inputs, refs = refs[:count], refs[count:]
    outs, (a_s, b_s, acc_s, sems) = refs[:-4], refs[-4:]
    step = pl.program_id(0)
    s, f = at_ref[0], at_ref[1]
    part = acc_s.shape[1]
    width = b_s.shape[2]
    blocks = width // part
    plans, used = [], 0
    for p, (left, right) in enumerate(products):
        rows = b_s.shape[1] // len(right)
        cols = a_s.shape[2] // split
        pairs = []
        for i, (operand, lead) in enumerate(right):
            span = slice(i * rows, (i + 1) * rows)
            for c in range(split):
                o, l = left[i * split + c]
                view = inputs[o] if l is None else inputs[o].at[l]
                pairs.append((view, a_s.at[p, span, c * cols : (c + 1) * cols]))
            view = inputs[operand] if lead is None else inputs[operand].at[lead]
            pairs.append((view, b_s.at[p, span]))
        plans.append([pltpu.make_async_copy(*pair, sems.at[used + i]) for i, pair in enumerate(pairs)])
        used += len(pairs)

    @pl.when(step == 0)
    def _():
        for plan in plans:
            begin(plan)
        plan, groups = plans[0], len(products[0][1])
        rows = b_s.shape[1] // groups
        for i in range(groups):
            finish(plan[i * (split + 1) : (i + 1) * (split + 1)])
            span = slice(i * rows, (i + 1) * rows)
            found = tn(a_s[0, span], b_s[0, span, :part])
            if i == 0:
                acc_s[...] = found
            else:
                acc_s[...] += found

    for p in range(1, len(products)):

        @pl.when(step == p * blocks)
        def _(p=p):
            finish(plans[p])

    if blocks * len(products) > 1:

        @pl.when(step > 0)
        def _():
            p = step // blocks
            acc_s[...] = tn(a_s[p], b_s[p, :, lanes(step % blocks, part)])

    if slotted:
        odd_ref, even_ref = outs
        rows = odd_ref.shape[1]
        for k in range(2 * odd_ref.shape[0]):
            target = odd_ref if k & 1 else even_ref
            target[k >> 1] = acc_s[block_rows(row_of(s, f, k), rows)].astype(BF)
    else:
        (out_ref,) = outs
        rows = out_ref.shape[1]
        for k in range(out_ref.shape[0]):
            out_ref[k] = acc_s[k * rows : (k + 1) * rows].astype(BF)


def weight_grad(at, operands, products, shards, split=1, row_of=None):
    def shape_of(view):
        return operands[view[0]].shape[-2:]

    left, right = products[0]
    tokens = sum(shape_of(v)[0] for v in right)
    height, width = shape_of(left[0])[1] * split, shape_of(right[0])[1]
    part = width if width <= 256 or width % 256 else 256
    blocks, rows = width // part, height // shards
    if row_of is not None:
        shapes = [jax.ShapeDtypeStruct((shards // 2, rows, width), BF)] * 2
        specs = [pl.BlockSpec((shards // 2, rows, part), lambda j, at: (0, 0, j))] * 2
    else:
        shapes = jax.ShapeDtypeStruct((shards, len(products), rows, width), BF)
        specs = pl.BlockSpec((shards, None, rows, part), lambda j, at: (0, j // blocks, 0, j % blocks))
    return call(
        functools.partial(grad_kernel, len(operands), products, row_of is not None, split, row_of),
        "weight_grad",
        at,
        operands,
        [ANY] * len(operands),
        shapes,
        specs,
        [
            pltpu.VMEM((len(products), tokens, height), BF),
            pltpu.VMEM((len(products), tokens, width), BF),
            pltpu.VMEM((height, part), F32),
            pltpu.SemaphoreType.DMA((sum(len(a) + len(b) for a, b in products),)),
        ],
        grid=blocks * len(products),
        flops=2 * tokens * height * width * len(products),
    )


def strip_kernel(n, batch, at_ref, *refs):
    came, branch, refs = refs[:batch], refs[batch : 2 * batch], refs[2 * batch :]
    odd_ref, even_ref, a_s, b_s, sems = refs
    step = pl.program_id(0)
    tile, every = came[0].shape[1:]
    pairs = []
    for b in range(batch):
        span = slice(b * tile, (b + 1) * tile)
        pairs += [(came[b].at[k], a_s.at[span, k * every : (k + 1) * every]) for k in range(n)]
        pairs.append((branch[b], b_s.at[span]))
    copies = copies_of(pairs, sems)

    @pl.when(step == 0)
    def _():
        begin(copies)
        finish(copies)

    strip = odd_ref.shape[1]
    found = tn(a_s[...], b_s[:, lanes(slot_at(step, n) ^ at_ref[0], strip)]).astype(BF)

    @pl.when(step < n // 2)
    def _():
        odd_ref[...] = found

    @pl.when(step >= n // 2)
    def _():
        even_ref[...] = found


def strip_grad(at, came, branch):
    n, tile, every = came[0].shape
    batch, width = len(came), branch[0].shape[1]
    half, strip = n // 2, width // n
    block = (None, n * every, strip)
    return call(
        functools.partial(strip_kernel, n, batch),
        "strip_grad",
        at,
        [*came, *branch],
        [ANY] * (2 * batch),
        [jax.ShapeDtypeStruct((half, n * every, strip), BF)] * 2,
        [
            pl.BlockSpec(block, lambda j, at: (jnp.minimum(j, half - 1), 0, 0)),
            pl.BlockSpec(block, lambda j, at: (jnp.maximum(j - half, 0), 0, 0)),
        ],
        [
            pltpu.VMEM((batch * tile, n * every), BF),
            pltpu.VMEM((batch * tile, width), BF),
            pltpu.SemaphoreType.DMA((batch * (n + 1),)),
        ],
        grid=n,
        flops=2 * batch * tile * n * every * width,
    )


def body(
    n, shards,
    tokens, first_gain, first_shift, attention_weight, attention_bias, output_weight, output_bias,
    second_gain, second_shift, expand_weight, expand_bias, contract_weight, contract_bias,
    cotangent, threshold,
):
    batch, tile, width = tokens.shape
    rows, qkv = attention_weight.shape
    every = qkv // 3
    heads = every // HEAD
    inner_rows = contract_weight.shape[0]
    inner = inner_rows * shards // n
    piece = inner_rows // n
    ratio = shards // n
    strip = output_weight.shape[1]
    s = lax.axis_index("seq").astype(jnp.int32)
    f = lax.axis_index("fsdp").astype(jnp.int32)
    at = jnp.stack([s, f])
    streams = range(batch)
    joined = piece == rows

    strips = strip % 128 == 0 and qkv % 128 == 0

    sent = jnp.concatenate([attention_weight, output_weight], axis=1) if strips else attention_weight
    qkv_slots = gather_slots(sent, "fsdp", shards)
    qkv_pieces = [(a, None, k) for k, a in enumerate(qkv_slots)]
    unit, _ = norm_stats(tokens.astype(F32))
    normed_own = (unit * first_gain + first_shift).astype(BF)
    normed_first = gather_slots(normed_own, "seq", n, qkv_slots[1:])
    expand_weight, contract_weight, *_ = lax.optimization_barrier(
        (expand_weight, contract_weight, *(qkv_slots[bit] for bit in bits_of(shards)))
    )
    to_seq = jnp.concatenate(
        [
            jnp.swapaxes(expand_weight.reshape(rows, ratio, n, piece), 1, 2)
            .swapaxes(0, 1)
            .reshape(n, -1, strip),
            contract_weight.reshape(n, piece, strip),
        ],
        axis=1,
    )
    from_seq = lax.all_to_all(to_seq, "seq", 0, 0, tiled=True)
    cut = rows * ratio * piece // strip
    expand_rows = (
        from_seq[:, :cut].reshape(n, rows, ratio * piece).swapaxes(0, 1).reshape(rows, inner)
    )
    contract_rows = from_seq[:, cut:].swapaxes(0, 1).reshape(piece, width)
    if joined:
        stacked = after(jnp.stack([expand_rows, contract_rows]), *qkv_slots[1:], normed_first[n // 2])
        hidden_weights = [lax.all_gather(stacked, "fsdp")]
    else:
        hidden_weights = [lax.all_gather(w, "fsdp") for w in (expand_rows, contract_rows)]

    mixing_bias = lax.dynamic_slice_in_dim(attention_bias, s * qkv, qkv)
    inner_bias = lax.dynamic_index_in_dim(
        expand_bias.reshape(shards, n, piece), s, axis=1, keepdims=False
    ).reshape(inner)

    parts, outs, lse, peaks, came = ([None] * batch for _ in range(5))
    residual, pairs = [None] * batch, [None] * batch
    for b in streams:
        parts[b], outs[b], lse[b], peaks[b], extra = attend_forward(
            at, b, normed_first, qkv_pieces, mixing_bias, n, strip if strips and b == 0 else 0
        )
        sent = after(outs[b], came[b - 1]) if b else outs[b]
        came[b] = lax.all_to_all(sent, "seq", 0, 0, tiled=True)
        if b == 0:
            joint = extra
            cot_first = gather_slots(after(cotangent[0], normed_first[n // 2]), "seq", n, outs[:1])
    if strips:
        output_weights = gather_slots(after(joint[0], cot_first[n // 2]), "seq", n, outs[-1:])
    else:
        output_weights = [
            lax.all_gather(
                lax.all_gather(output_weight, "fsdp", tiled=True), "seq", axis=1, tiled=True
            )
        ]
    normed_own = [None] * batch
    for b in streams:
        residual[b], normed_own[b] = project(
            at, b, came[b], output_weights, tokens, output_bias, second_gain, second_shift,
            cotangent if b else None,
        )
    cot_pairs = [None] * batch
    for b in streams:
        if b == 0:
            own = gather_slots(after(normed_own[b], came[-1]), "seq", n, normed_own[-1:])
            pairs[b] = [(a, None, k) for k, a in enumerate(own)]
            cot_pairs[b] = [(a, None, k) for k, a in enumerate(cot_first)]
        else:
            own = gather_slots(after(normed_own[b], pairs[b - 1][n // 2][0]), "seq", n)
            pairs[b] = [(a, 0, k) for k, a in enumerate(own)]
            cot_pairs[b] = [(a, 1, k) for k, a in enumerate(own)]

    active, hidden_cot, inner_sums, rescot, branch, sums, cots = ([None] * batch for _ in range(7))
    second, out_parts, terms = [], [], None
    for b in streams:
        operands = list(pairs[b])
        if b:
            array = after(operands[0][0], second[-1][0])
            operands[0] = (array, *operands[0][1:])
        active[b], hidden_cot[b], odd, even, *out_part, inner_sums[b] = hidden_layer(
            at, operands, cot_pairs[b], hidden_weights, inner_bias
        )
        out_parts.append(out_part)
        odd = after(odd, second_terms[-1][-1] if b else pairs[-1][n // 2][0])
        if b == 0:
            second_terms = []
        second.append(scatter_near(odd, even, "seq", n))
        second_terms.append(scatter_far(*second[b], "seq", n))

    def second_step(b, *others):
        terms = second_terms[b]
        if others:
            terms[0] = after(terms[0], *others)
        rescot[b], branch[b], sums[b], slots = second_back(
            at, b, terms, output_weights, residual[b], cotangent, second_gain, n
        )
        cots[b] = lax.all_to_all(slots, "seq", 0, 0, tiled=True)

    second_step(0)

    def by_slot(first):
        return [(first + k, b) for b in streams for k in range(n)]

    def by_stream(first):
        return [(first + b, k) for b in streams for k in range(n)]

    def owned(s, f, k):
        return f ^ k

    arrays, views = arrays_of([v for b in streams for v in (*pairs[b], *cot_pairs[b])])
    views = [view[:2] for view in views]
    normed_views = [v for b in streams for v in views[2 * b * n : (2 * b + 1) * n]]
    cot_views = [v for b in streams for v in views[(2 * b + 1) * n : 2 * (b + 1) * n]]
    far = len(arrays)
    if joined:
        arrays[0] = after(arrays[0], second[-1][0], branch[0])
        both = weight_grad(
            at,
            [*arrays, *hidden_cot, *active],
            [(normed_views, by_stream(far)), (by_stream(far + batch), cot_views)],
            shards,
        )
        scattered = [lax.psum_scatter(after(both, cots[0], second_terms[-1][-1]), "fsdp")]
        done = [both]
    else:
        grad_expand = scatter_sum(
            *weight_grad(
                at, [*arrays, *hidden_cot], [(normed_views, by_stream(far))], shards, 1, owned
            ),
            "fsdp",
            shards,
        )
        grad_contract = scatter_sum(
            *weight_grad(at, [*arrays, *active], [(by_stream(far), cot_views)], shards, 1, owned),
            "fsdp",
            shards,
        )
        scattered, done = [grad_expand, grad_contract], []
    for b in streams[1:]:
        second_step(b, *done, cots[b - 1])
    cots[0] = after(cots[0], *done, branch[-1])

    mixed_cot, mixing_sums, tail = [None] * batch, [None] * batch, [None] * batch
    input_grad = None
    near, block_output = None, None
    out_terms = [None] * batch
    first_terms = []
    for b in streams:
        cot = cots[b]
        if b == 0:
            out_near = scatter_near(after(out_parts[b][0], branch[0]), out_parts[b][1], "seq", n)
            cot = after(cot, out_near[0])
            out_terms[b] = scatter_far(*out_near, "seq", n)
        else:
            cot = after(cot, near[0], output_odd)
        mixed_cot[b], odd, even, mixing_sums[b] = attend_backward(
            at, parts[b], lse[b], outs[b], cot, qkv_pieces
        )
        odd = after(odd, out_terms[0][-1], terms[-1] if b else cots[-1])
        near = scatter_near(odd, even, "seq", n)
        terms = scatter_far(*near, "seq", n)
        first_terms.append(terms)
        if b == 0:
            if strips:
                output_odd, output_even = strip_grad(at, [after(came[0], mixed_cot[0]), *came[1:]], branch)
            else:
                product = functools.reduce(
                    jnp.add,
                    [
                        jnp.einsum("kte,td->ked", came[b], branch[b], preferred_element_type=F32)
                        for b in streams
                    ],
                ).reshape(width, n, strip)
                output_odd, output_even = (
                    jnp.stack(
                        [
                            lax.dynamic_index_in_dim(product, s ^ k, 1, keepdims=False).astype(BF)
                            for k in range(first, n, 2)
                        ]
                    )
                    for first in (1, 0)
                )
        if b == batch - 1:
            grad_parts = weight_grad(
                at,
                [after(normed_first[0], near[0]), *normed_first[1:], *mixed_cot],
                [(by_slot(0), by_stream(n))],
                shards,
                1,
                owned,
            )
    for b in streams:
        first_terms[b][0] = after(first_terms[b][0], grad_parts[0])
        input_grad, tail[b] = first_back(
            at, b, first_terms[b], tokens, rescot[b], first_gain, input_grad
        )
    for b in streams[1:]:
        out_near = scatter_near(after(out_parts[b][0], near[0]), out_parts[b][1], "seq", n)
        out_terms[b] = scatter_far(after(out_near[0], terms[-1]), *out_near[1:], "seq", n)
    def over_streams(values):
        return functools.reduce(jnp.add, values)

    mine = jnp.arange(n) == s
    spread_inner = jnp.where(
        mine[None, :, None], over_streams(inner_sums).reshape(shards, 1, piece), 0.0
    )
    spread_mixing = jnp.where(mine[:, None], over_streams(mixing_sums), 0.0)
    peak = jnp.where(mine[:, None], functools.reduce(jnp.maximum, peaks)[None], -jnp.inf)
    top = jnp.pad(peak.reshape(-1), (0, 1024 - n * heads)).reshape(-1, 128)
    vectors = jnp.concatenate(
        [top]
        + [
            v.reshape(-1, 128)
            for v in (over_streams(sums), over_streams(tail), spread_inner, spread_mixing)
        ]
    )
    is_top = jnp.arange(vectors.shape[0])[:, None] < top.shape[0]

    def summed(vectors, axis, size, bits):
        for bit in bits:
            other = swap(vectors, axis, size, bit)
            vectors = jnp.where(is_top, jnp.maximum(vectors, other), vectors + other)
        return vectors

    near_bit, far_bits = bits_of(shards)[0], bits_of(shards)[1:]
    vectors = summed(vectors, "fsdp", shards, far_bits)
    output_near = scatter_near(output_odd, output_even, "seq", n)
    output_terms = scatter_far(*output_near, "seq", n)
    output_terms[-1] = after(output_terms[-1], grad_parts[0])
    output = functools.reduce(jnp.add, [a[0].astype(F32) for a in output_terms])
    order = [*far_bits, near_bit]
    kept, other, left = scatter_half(
        output.reshape(*[2] * len(order), rows, strip), f, "fsdp", shards, order[0],
        bits_of(shards)[::-1],
    )
    held = {}

    def first_step(came):
        came, *held["hidden"] = lax.optimization_barrier((came, *scattered))
        first = summed(after(vectors, came), "fsdp", shards, [near_bit])
        first = summed(first, "seq", n, bits_of(n)[:-1])
        held["vectors"] = first, swap(first, "seq", n, bits_of(n)[-1])
        for b in streams[:-1]:
            out_terms[b][0] = after(out_terms[b][0], came)
        held["output"] = scatter_half(
            kept + after(other, came).astype(F32), f, "fsdp", shards, order[1], left
        )
        return came

    def second_step_over(came):
        came, *held["hidden"] = lax.optimization_barrier((came, *held["hidden"]))
        first, last = held["vectors"]
        last = after(last, came)
        held["vectors"] = jnp.where(is_top, jnp.maximum(first, last), first + last)
        kept, other, left = held["output"]
        held["output"] = kept, after(other, came), left
        out_terms[-1][0] = after(out_terms[-1][0], came)
        return came

    grad_mixing = scatter_sum(*grad_parts, "fsdp", shards, [first_step, second_step_over])
    for b in streams:
        block_output = result_out(
            at, b, batch, out_terms[b], residual[b], contract_bias, block_output
        )
    vectors, (kept, other, left) = held["vectors"], held["output"]
    for bit in order[2:]:
        kept, other, left = scatter_half(
            kept + other.astype(F32), f, "fsdp", shards, bit, left
        )
    grad_output_own = kept + other.astype(F32)
    grad_expand, grad_contract = held["hidden"][0] if joined else held["hidden"]
    back = lax.all_to_all(
        jnp.concatenate(
            [
                grad_expand.astype(BF)
                .reshape(rows, n, ratio * piece)
                .swapaxes(0, 1)
                .reshape(n, cut, strip),
                grad_contract.astype(BF).reshape(piece, n, strip).swapaxes(0, 1),
            ],
            axis=1,
        ),
        "seq",
        0,
        0,
        tiled=True,
    )
    grad_expand_own = (
        back[:, :cut]
        .reshape(n, rows, ratio, piece)
        .transpose(1, 2, 0, 3)
        .reshape(rows, ratio * n * piece)
        .astype(F32)
    )
    grad_contract_own = back[:, cut:].reshape(inner_rows, strip).astype(F32)
    vectors = vectors.reshape(-1)
    ends = [1024]
    for length in [width] * 6 + [n * inner, n * qkv]:
        ends.append(ends[-1] + length)
    (
        second_gain_sum, second_shift_sum, output_sum, contract_sum, first_gain_sum, first_shift_sum,
        inner_sum, mixing_sum,
    ) = (vectors[a:b] for a, b in zip(ends, ends[1:]))

    head_peak = lax.dynamic_slice_in_dim(vectors, s * heads, heads)
    factor = jnp.sqrt(threshold[0] / jnp.maximum(head_peak, threshold[0]))
    multiplier = jnp.broadcast_to(
        jnp.stack([factor, factor, jnp.ones_like(factor)], axis=1)[:, :, None], (heads, 3, HEAD)
    ).reshape(qkv)
    clipped_weight = attention_weight.astype(F32) * multiplier[None, :]
    clipped_bias = mixing_bias * multiplier

    return (
        block_output,
        input_grad,
        first_gain_sum,
        first_shift_sum,
        grad_mixing,
        mixing_sum,
        grad_output_own,
        output_sum,
        second_gain_sum,
        second_shift_sum,
        grad_expand_own,
        inner_sum,
        grad_contract_own,
        contract_sum,
        head_peak,
        clipped_weight,
        clipped_bias,
    )


def solution(mesh):
    grid, both, whole, line = P("fsdp", "seq"), P("fsdp", "seq", None), P(), P("seq")
    return jax.shard_map(
        functools.partial(body, mesh.shape["seq"], mesh.shape["fsdp"]),
        mesh=mesh,
        in_specs=(
            both, whole, whole, grid, whole, grid, whole, whole, whole, grid, whole, grid, whole,
            both, whole,
        ),
        out_specs=(
            both, both, whole, whole, grid, whole, grid, whole, whole, whole, grid, whole, grid,
            whole, line, grid, line,
        ),
        check_vma=False,
    )
```

```python
import functools
import math

import jax
import jax.numpy as jnp
from jax import lax
from jax.experimental import pallas as pl
from jax.experimental.pallas import tpu as pltpu
from jax.sharding import PartitionSpec as P

HEAD = 64
LOG2E = math.log2(math.e)
BF = jnp.bfloat16
F32 = jnp.float32
ANY = pl.BlockSpec(memory_space=pl.ANY)


def swap(value, axis, size, bit):
    return lax.ppermute(value, axis, [(i, i ^ bit) for i in range(size)])


def bits_of(size):
    return [1 << p for p in range(size.bit_length() - 1)]


def gather_slots(value, axis, size, wait=()):
    slots = {0: value}
    for bit in reversed(bits_of(size)):
        for k in list(slots):
            sent = after(slots[k], *wait) if k and wait else slots[k]
            slots[k | bit] = swap(sent, axis, size, bit)
    return [slots[k] for k in range(size)]


def scatter_near(odd, even, axis, size):
    came = swap(odd, axis, size, 1)
    total = even.astype(F32) + came.astype(F32)
    return total[1::2].astype(BF), total[0::2], [even, came]


def scatter_far(sent, rest, terms, axis, size):
    terms = list(terms)
    for bit in bits_of(size)[1:]:
        came = swap(sent, axis, size, bit)
        terms.append(came)
        if came.shape[0] > 1:
            rest = rest + came.astype(F32)
            sent, rest = rest[1::2].astype(BF), rest[0::2]
    return terms


def scatter_sum(odd, even, axis, size, hooks=()):
    rest, sent = even.astype(F32), odd
    for step, bit in enumerate(bits_of(size)):
        came = swap(sent, axis, size, bit)
        if step < len(hooks):
            came = hooks[step](came)
        rest = rest + came.astype(F32)
        if rest.shape[0] > 1:
            sent, rest = rest[1::2].astype(BF), rest[0::2]
    return rest[0]


def scatter_half(value, index, axis, size, bit, left):
    at = left.index(bit)
    own = ((index & bit) != 0).astype(jnp.int32)
    sent = lax.dynamic_index_in_dim(value, 1 - own, at, keepdims=False).astype(BF)
    kept = lax.dynamic_index_in_dim(value, own, at, keepdims=False).astype(F32)
    return kept, swap(sent, axis, size, bit), [b for b in left if b != bit]


def after(value, *others):
    return lax.optimization_barrier((value, *others))[0]


def nn(a, b):
    return lax.dot_general(a, b, (((1,), (0,)), ((), ())), preferred_element_type=F32)


def nt(a, b):
    return lax.dot_general(a, b, (((1,), (1,)), ((), ())), preferred_element_type=F32)


def full(shape):
    return pl.BlockSpec(shape, lambda i, at: (0,) * len(shape))


def entry(shape, at_entry=0):
    return pl.BlockSpec((None, *shape), lambda i, at: (at_entry,) + (0,) * len(shape))


def call(kernel, name, at, operands, in_specs, out_shape, out_specs, scratch, grid=1, flops=0, aliases=None):
    moved = sum(math.prod(o.shape) * o.dtype.itemsize for o in operands)
    return pl.pallas_call(
        kernel,
        out_shape=out_shape,
        grid_spec=pltpu.PrefetchScalarGridSpec(
            num_scalar_prefetch=1,
            grid=(grid,),
            in_specs=in_specs,
            out_specs=out_specs,
            scratch_shapes=scratch,
        ),
        compiler_params=pltpu.CompilerParams(vmem_limit_bytes=58 << 20),
        cost_estimate=pl.CostEstimate(flops=flops, transcendentals=0, bytes_accessed=moved),
        input_output_aliases=aliases or {},
        name=name,
    )(at, *operands)


def copies_of(pairs, sems):
    return [pltpu.make_async_copy(src, dst, sems.at[i]) for i, (src, dst) in enumerate(pairs)]


def begin(copies):
    for copy in copies:
        copy.start()


def finish(copies):
    for copy in copies:
        copy.wait()


def block_rows(index, rows):
    return pl.ds(pl.multiple_of(index * rows, rows), rows)


def weight_pairs(refs, views, target, f, start=0):
    rows = target.shape[0] // len(views)
    pairs = []
    for i, lead, slot in views:
        source = refs[i] if lead is None else refs[i].at[lead]
        if source.shape[-1] > target.shape[-1]:
            source = source.at[:, start : start + target.shape[-1]]
        pairs.append((source, target.at[block_rows(f ^ slot, rows)]))
    return pairs


def arrays_of(views):
    arrays, found = [], []
    for array, lead, slot in views:
        place = next((i for i, a in enumerate(arrays) if a is array), len(arrays))
        if place == len(arrays):
            arrays.append(array)
        found.append((place, lead, slot))
    return arrays, found


def head_mask(width, head):
    return (lax.broadcasted_iota(jnp.int32, (1, width), 1) // HEAD) == head


def causal(tile):
    keys = lax.broadcasted_iota(jnp.int32, (tile, tile), 0)
    queries = lax.broadcasted_iota(jnp.int32, (tile, tile), 1)
    return keys <= queries


def lanes(group, width):
    return pl.ds(pl.multiple_of(group * width, width), width)


def join(parts, axis):
    return parts[0] if len(parts) == 1 else jnp.concatenate(parts, axis=axis)


def forward_kernel(n, b, views, count, at_ref, *refs):
    normed, refs = refs[:n], refs[n:]
    pieces, refs = refs[:count], refs[count:]
    bias_ref, q_ref, k_ref, v_ref, o_ref, lse_ref, peak_ref = refs[:7]
    x_s, w_s, vt_s, x_sems, w_sems, e_sems = refs[-6:]
    s, f = at_ref[0], at_ref[1]
    _, tile, _ = x_s.shape
    extra = []
    if len(refs) == 14:
        extra = copies_of(weight_pairs(pieces, views, refs[7], f, w_s.shape[1]), e_sems)
    every = q_ref.shape[1]
    width = 128 if every % 128 == 0 else every
    heads, factor = width // HEAD, HEAD**-0.5 * LOG2E
    w_copies = copies_of(weight_pairs(pieces, views, w_s, f), w_sems)
    x_copies = copies_of([(normed[k].at[b], x_s.at[k]) for k in range(n)], x_sems)
    begin(w_copies)
    begin(x_copies)
    begin(extra)
    finish(w_copies)
    finish(x_copies)

    @pl.loop(0, n)
    def _(k):
        mixed = (nn(x_s[k], w_s[...]) + bias_ref[...]).astype(BF)
        spot = block_rows(k ^ s, tile)
        parts = [
            join([mixed[:, (3 * h + j) * HEAD : (3 * h + j + 1) * HEAD] for h in range(every // HEAD)], 1)
            for j in range(3)
        ]
        q_ref[spot], k_ref[spot], v_ref[spot] = parts
        vt_s[:, spot] = parts[2].T

    @pl.loop(0, every // width)
    def _(g):
        cols = lanes(g, width)
        peaks = [None] * heads
        for i in range(n):
            q_tile = q_ref[i * tile : (i + 1) * tile, cols]
            limit = (i + 1) * tile
            step = min(limit, 4 * tile)
            outs = []
            for h in range(heads):
                q = jnp.where(head_mask(width, h), q_tile, jnp.zeros_like(q_tile))
                v_rows = pl.ds(pl.multiple_of(g * width + h * HEAD, HEAD), HEAD)
                top = total = acc = None
                for start in range(0, limit, step):
                    stop = min(start + step, limit)
                    found = nt(k_ref[start:stop, cols], q)
                    if stop == limit:
                        edge = stop - start - tile
                        masked = jnp.where(causal(tile), found[edge:], -jnp.inf)
                        found = masked if edge == 0 else jnp.concatenate([found[:edge], masked], axis=0)
                    high = jnp.max(found, axis=0, keepdims=True)
                    new_top = high if top is None else jnp.maximum(top, high)
                    grown = jnp.exp2((found - new_top) * factor)
                    part = jnp.sum(grown, axis=0, keepdims=True)
                    mixed = nn(vt_s[v_rows, start:stop], grown.astype(BF))
                    if top is None:
                        total, acc = part, mixed
                    else:
                        shrink = jnp.exp2((top - new_top) * factor)
                        total, acc = total * shrink + part, acc * shrink + mixed
                    top = new_top
                outs.append(acc / total)
                lse_ref[g, h : h + 1, i * tile : (i + 1) * tile] = top * factor + jnp.log2(total)
                peaks[h] = top if peaks[h] is None else jnp.maximum(peaks[h], top)
            o_ref[i, :, cols] = join(outs, 0).T.astype(BF)
        for h in range(heads):
            peak_ref[g, h : h + 1, :] = peaks[h] * HEAD**-0.5

    finish(extra)


def attend_forward(at, b, normed, pieces, bias, n, strip=0):
    _, tile, width = normed[0].shape
    arrays, views = arrays_of(pieces)
    qkv = bias.shape[0]
    every, length = qkv // 3, n * tile
    group = 128 if every % 128 == 0 else every
    part = jax.ShapeDtypeStruct((length, every), BF)
    stats = [(every // group, group // HEAD, length), (every // group, group // HEAD, tile)]
    found = call(
        functools.partial(forward_kernel, n, b, views, len(arrays)),
        "attend_forward",
        at,
        [*normed, *arrays, bias.reshape(1, qkv)],
        [ANY] * (n + len(arrays)) + [full((1, qkv))],
        [part] * 3
        + [jax.ShapeDtypeStruct((n, tile, every), BF)]
        + [jax.ShapeDtypeStruct(shape, F32) for shape in stats]
        + ([jax.ShapeDtypeStruct((width, strip), BF)] if strip else []),
        [full((length, every))] * 3
        + [full((n, tile, every))]
        + [full(shape) for shape in stats]
        + ([full((width, strip))] if strip else []),
        [
            pltpu.VMEM((n, tile, width), BF),
            pltpu.VMEM((width, qkv), BF),
            pltpu.VMEM((every, length), BF),
            pltpu.SemaphoreType.DMA((n,)),
            pltpu.SemaphoreType.DMA((len(views),)),
            pltpu.SemaphoreType.DMA((len(views),)),
        ],
        flops=2 * length * width * qkv + 8 * length * length * every,
    )
    parts, (out, lse, peak), extra = found[:3], found[3:6], found[6:]
    return parts, out, lse, jnp.max(peak, axis=-1).reshape(-1), extra


def backward_kernel(n, views, count, at_ref, *refs):
    q_ref, k_ref, v_ref, lse_ref, o_ref, g_ref = refs[:6]
    pieces, refs = refs[6 : 6 + count], refs[6 + count :]
    mix_ref, odd_ref, even_ref, bias_ref, w_s, kt_s, dq_s, dk_s, dv_s, mix_s, w_sems = refs
    s, f = at_ref[0], at_ref[1]
    _, tile, qkv = mix_ref.shape
    every, scale = qkv // 3, HEAD**-0.5
    width = 128 if every % 128 == 0 else every
    heads, factor = width // HEAD, scale * LOG2E
    w_copies = copies_of(weight_pairs(pieces, views, w_s, f), w_sems)
    begin(w_copies)
    kt_s[...] = k_ref[...].T

    @pl.loop(0, every // width)
    def _(g):
        cols = lanes(g, width)
        for i in reversed(range(n)):
            rows = slice(i * tile, (i + 1) * tile)
            limit = (i + 1) * tile
            step = min(limit, 4 * tile)
            q_tile, g_tile = q_ref[rows, cols], g_ref[i, :, cols]
            inner = (g_tile.astype(F32) * o_ref[i, :, cols].astype(F32)).T
            outs = []
            for h in range(heads):
                mask = head_mask(width, h)
                q = jnp.where(mask, q_tile, jnp.zeros_like(q_tile))
                cot = jnp.where(mask, g_tile, jnp.zeros_like(g_tile))
                delta = jnp.sum(inner[h * HEAD : (h + 1) * HEAD], axis=0, keepdims=True)
                lse = lse_ref[g, h : h + 1, rows]
                k_rows = pl.ds(pl.multiple_of(g * width + h * HEAD, HEAD), HEAD)
                acc = None
                for start in range(0, limit, step):
                    stop = min(start + step, limit)
                    probs = jnp.exp2(nt(k_ref[start:stop, cols], q) * factor - lse)
                    if stop == limit:
                        edge = stop - start - tile
                        masked = jnp.where(causal(tile), probs[edge:], 0.0)
                        probs = masked if edge == 0 else jnp.concatenate([probs[:edge], masked], axis=0)
                    spread = nt(v_ref[start:stop, cols], cot)
                    logit_cot = (probs * (spread - delta)).astype(BF)
                    dv_part = nn(probs.astype(BF), cot)
                    dk_part = nn(logit_cot, q)
                    if i == n - 1 and h == 0:
                        dv_s[start:stop] = dv_part
                        dk_s[start:stop] = dk_part
                    else:
                        dv_s[start:stop] += dv_part
                        dk_s[start:stop] += dk_part
                    dq_part = nn(kt_s[k_rows, start:stop], logit_cot)
                    acc = dq_part if acc is None else acc + dq_part
                outs.append(acc)
            dq_s[rows] = (join(outs, 0).T * scale).astype(BF)
        for i in range(n):
            rows = slice(i * tile, (i + 1) * tile)
            dq = dq_s[rows]
            dk = (dk_s[rows] * scale).astype(BF)
            dv = dv_s[rows].astype(BF)
            mix_s[rows, lanes(g, 3 * width)] = jnp.concatenate(
                [a[:, h * HEAD : (h + 1) * HEAD] for h in range(heads) for a in (dq, dk, dv)], axis=1
            )

    finish(w_copies)
    bias_ref[...] = jnp.zeros_like(bias_ref)

    @pl.loop(0, n // 2)
    def _(j):
        for k, target in ((2 * j, even_ref), (2 * j + 1, odd_ref)):
            mixed_cot = mix_s[block_rows(k ^ s, tile)]
            mix_ref[k] = mixed_cot
            bias_ref[...] += row_sum(mixed_cot.astype(F32))
            target[j] = nt(mixed_cot, w_s[...]).astype(BF)


def attend_backward(at, parts, lse, out, cot, pieces):
    n, tile, every = out.shape
    length, qkv = n * tile, 3 * every
    arrays, views = arrays_of(pieces)
    width = len(views) * arrays[0].shape[-2]
    group = 128 if every % 128 == 0 else every
    half = (n // 2, tile, width)
    return call(
        functools.partial(backward_kernel, n, views, len(arrays)),
        "attend_backward",
        at,
        [*parts, lse, out, cot, *arrays],
        [full((length, every))] * 3
        + [full(lse.shape)]
        + [full((n, tile, every))] * 2
        + [ANY] * len(arrays),
        [
            jax.ShapeDtypeStruct((n, tile, qkv), BF),
            jax.ShapeDtypeStruct(half, BF),
            jax.ShapeDtypeStruct(half, BF),
            jax.ShapeDtypeStruct((1, qkv), F32),
        ],
        [full((n, tile, qkv)), full(half), full(half), full((1, qkv))],
        [
            pltpu.VMEM((width, qkv), BF),
            pltpu.VMEM((every, length), BF),
            pltpu.VMEM((length, group), BF),
            pltpu.VMEM((length, group), F32),
            pltpu.VMEM((length, group), F32),
            pltpu.VMEM((length, qkv), BF),
            pltpu.SemaphoreType.DMA((len(views),)),
        ],
        flops=2 * length * width * qkv + 20 * length * length * every,
    )


def norm_stats(values):
    centered = values - jnp.mean(values, axis=-1, keepdims=True)
    rate = lax.rsqrt(jnp.mean(centered * centered, axis=-1, keepdims=True) + 1e-05)
    return centered * rate, rate


def norm_back(cot, unit, rate, gain):
    e = cot * gain
    return rate * (
        e
        - jnp.mean(e, axis=-1, keepdims=True)
        - unit * jnp.mean(e * unit, axis=-1, keepdims=True)
    )


def column_copies(refs, target, s, sems):
    strip = refs[0].shape[1]
    if len(refs) == 1:
        return copies_of([(refs[0], target)], sems)
    return copies_of([(ref, target.at[:, lanes(k ^ s, strip)]) for k, ref in enumerate(refs)], sems)


def project_kernel(count, paired, at_ref, *refs):
    came_ref, weights, refs = refs[0], refs[1 : 1 + count], refs[1 + count :]
    tokens_ref, bias_ref, gain_ref, shift_ref = refs[:4]
    residual_ref, normed_ref, c_s, w_s, c_sem, w_sems = refs[-6:]
    if paired:
        normed_ref[1] = refs[4][...]
        normed_ref = normed_ref.at[0]
    n, _, every = came_ref.shape
    copy = pltpu.make_async_copy(came_ref, c_s, c_sem)
    weights = column_copies(weights, w_s, at_ref[0], w_sems)
    copy.start()
    begin(weights)
    total = tokens_ref[...].astype(F32) + bias_ref[...]
    copy.wait()
    finish(weights)
    for k in range(n):
        total = total + nn(c_s[k], w_s[k * every : (k + 1) * every])
    residual_ref[...] = total
    unit, _ = norm_stats(total)
    normed_ref[...] = (unit * gain_ref[...] + shift_ref[...]).astype(BF)


def project(at, b, came, weights, tokens, bias, gain, shift, cotangent=None):
    _, tile, width = tokens.shape
    n, _, every = came.shape
    row, block = full((1, width)), entry((tile, width), b)
    paired = cotangent is not None
    shape = (2, tile, width) if paired else (tile, width)
    return call(
        functools.partial(project_kernel, len(weights), paired),
        "project",
        at,
        [came, *weights, tokens, *(v.reshape(1, width) for v in (bias, gain, shift))]
        + ([cotangent] if paired else []),
        [ANY] * (1 + len(weights)) + [block, row, row, row] + ([block] if paired else []),
        [jax.ShapeDtypeStruct((tile, width), F32), jax.ShapeDtypeStruct(shape, BF)],
        [full((tile, width)), full(shape)],
        [
            pltpu.VMEM((n, tile, every), BF),
            pltpu.VMEM((width, width), BF),
            pltpu.SemaphoreType.DMA,
            pltpu.SemaphoreType.DMA((len(weights),)),
        ],
        flops=2 * tile * width * width,
    )


def gelu_pair(v):
    k0 = math.sqrt(2.0 / math.pi)
    square = v * v
    t = jnp.tanh(v * (k0 + (k0 * 0.044715) * square))
    half = 0.5 + 0.5 * t
    slope = half + (0.5 * v) * (1.0 - t * t) * (k0 + (3.0 * 0.044715 * k0) * square)
    return v * half, slope


def slot_at(step, n):
    half = n // 2
    return jnp.where(step < half, 2 * step + 1, 2 * (step - half))


def hidden_kernel(n, views, arrays, count, at_ref, *refs):
    inputs, refs = refs[:arrays], refs[arrays:]
    found = [inputs[i] if lead is None else inputs[i].at[lead] for i, lead, _ in views]
    normed, cots = found[:n], found[n:]
    weights_in, refs = refs[:count], refs[count:]
    bias_ref = refs[0]
    active_ref, cot_ref, odd_ref, even_ref, out_odd_ref, out_even_ref, sum_ref = refs[1:8]
    x_s, c_s, expand_s, contract_s, x_sems, c_sems, w_sems = refs[8:]
    step = pl.program_id(0)
    k = slot_at(step, n)
    shards, inner = weights_in[0].shape[0], expand_s.shape[1]
    first = [weights_in[0].at[i, 0] if count == 1 else weights_in[0].at[i] for i in range(shards)]
    second = [weights_in[0].at[i, 1] if count == 1 else weights_in[1].at[i] for i in range(shards)]
    e_rows, c_rows = expand_s.shape[0] // shards, contract_s.shape[0] // shards
    order = list(range(1, n, 2)) + list(range(0, n, 2))
    x_copies = copies_of([(normed[j], x_s.at[j]) for j in order], x_sems)
    c_copies = copies_of([(cots[j], c_s.at[j]) for j in order], c_sems)
    weights = copies_of(
        [(a, expand_s.at[i * e_rows : (i + 1) * e_rows]) for i, a in enumerate(first)]
        + [(a, contract_s.at[i * c_rows : (i + 1) * c_rows]) for i, a in enumerate(second)],
        w_sems,
    )

    @pl.when(step == 0)
    def _():
        begin(x_copies[:1] + weights[:shards] + c_copies[:1] + weights[shards:])
        begin(x_copies[1:] + c_copies[1:])
        sum_ref[...] = jnp.zeros_like(sum_ref)

    for j in range(n):

        @pl.when(step == j)
        def _(j=j):
            if j == 0:
                finish(weights)
            x_copies[j].wait()
            c_copies[j].wait()

    part = min(inner, 256)
    x, c = x_s[k], c_s[k]
    for start in range(0, inner, part):
        cols = slice(start, start + part)
        hidden = nn(x, expand_s[:, cols]) + bias_ref[:, cols]
        value, slope = gelu_pair(hidden)
        active_ref[:, cols] = value.astype(BF)
        hidden_cot = (nt(c, contract_s[cols]) * slope).astype(BF)
        cot_ref[:, cols] = hidden_cot
        sum_ref[:, cols] += jnp.sum(hidden_cot.astype(F32), axis=0, keepdims=True)
    partial = nt(cot_ref[...], expand_s[...]).astype(BF)
    out = nn(active_ref[...], contract_s[...]).astype(BF)

    @pl.when(step < n // 2)
    def _():
        odd_ref[...] = partial
        out_odd_ref[...] = out

    @pl.when(step >= n // 2)
    def _():
        even_ref[...] = partial
        out_even_ref[...] = out


def hidden_layer(at, normed, cots, weights, bias):
    n = len(normed)
    arrays, views = arrays_of([*normed, *cots])
    tile, width = arrays[0].shape[-2:]
    inner = bias.shape[0]
    shards = weights[0].shape[0]
    half = n // 2
    slot = pl.BlockSpec((None, tile, inner), lambda j, at: (slot_at(j, n), 0, 0))
    early = lambda j: jnp.minimum(j, half - 1)
    later = lambda j: jnp.maximum(j - half, 0)
    pair = jax.ShapeDtypeStruct((half, tile, width), BF)
    wide = jax.ShapeDtypeStruct((n, tile, inner), BF)
    operands = [*arrays, *weights, bias.reshape(1, inner)]
    specs = [ANY] * (len(arrays) + len(weights)) + [full((1, inner))]
    near = pl.BlockSpec((None, tile, width), lambda j, at: (early(j), 0, 0))
    kept = pl.BlockSpec((None, tile, width), lambda j, at: (later(j), 0, 0))
    return call(
        functools.partial(hidden_kernel, n, views, len(arrays), len(weights)),
        "hidden_layer",
        at,
        operands,
        specs,
        [wide, wide, pair, pair, pair, pair, jax.ShapeDtypeStruct((1, inner), F32)],
        [
            slot,
            slot,
            near,
            kept,
            near,
            kept,
            full((1, inner)),
        ],
        [
            pltpu.VMEM((n, tile, width), BF),
            pltpu.VMEM((n, tile, width), BF),
            pltpu.VMEM((width, inner), BF),
            pltpu.VMEM((inner, width), BF),
            pltpu.SemaphoreType.DMA((n,)),
            pltpu.SemaphoreType.DMA((n,)),
            pltpu.SemaphoreType.DMA((2 * shards,)),
        ],
        grid=n,
        flops=8 * n * tile * width * inner,
    )


def added(terms):
    total = terms[0][...].astype(F32)
    for term in terms[1:]:
        total = total + term[...].astype(F32)
    return total


def row_sum(values):
    return jnp.sum(values, axis=0, keepdims=True)


def second_kernel(b, terms_in, count, at_ref, *refs):
    terms, refs = refs[:terms_in], refs[terms_in:]
    weights, refs = refs[:count], refs[count:]
    residual_ref, cot_ref, gain_ref = refs[:3]
    rescot_ref, branch_ref, sums_ref, out_ref, t_s, r_s, c_s, w_s, sems, w_sems = refs[3:]
    copies = copies_of(
        [(residual_ref, r_s), (cot_ref.at[b], c_s)]
        + [(term.at[0], t_s.at[i]) for i, term in enumerate(terms)],
        sems,
    )
    weights = column_copies(weights, w_s, at_ref[0], w_sems)
    begin(copies)
    begin(weights)
    finish(copies)
    second_cot = added([t_s.at[i] for i in range(terms_in)])
    unit, rate = norm_stats(r_s[...])
    cot = c_s[...].astype(F32)
    residual_cot = cot + norm_back(second_cot, unit, rate, gain_ref[...])
    rescot_ref[...] = residual_cot
    branch = residual_cot.astype(BF)
    branch_ref[...] = branch
    sums_ref[0:1] = row_sum(second_cot * unit)
    sums_ref[1:2] = row_sum(second_cot)
    sums_ref[2:3] = row_sum(branch.astype(F32))
    sums_ref[3:4] = row_sum(cot)
    finish(weights)
    n, _, every = out_ref.shape
    for k in range(n):
        out_ref[k] = nt(branch, w_s[k * every : (k + 1) * every]).astype(BF)


def row_part(tile):
    return tile // 2


def stream_rows(b, part, width):
    return pl.BlockSpec((None, part, width), lambda i, at: (b, i, 0))


def row_block(part, width):
    return pl.BlockSpec((part, width), lambda i, at: (i, 0))


def second_back(at, b, terms, weights, residual, cotangent, gain, n):
    tile, width = residual.shape
    every = width // n
    return call(
        functools.partial(second_kernel, b, len(terms), len(weights)),
        "second_back",
        at,
        [*terms, *weights, residual, cotangent, gain.reshape(1, width)],
        [ANY] * (len(terms) + len(weights) + 2) + [full((1, width))],
        [
            jax.ShapeDtypeStruct((tile, width), F32),
            jax.ShapeDtypeStruct((tile, width), BF),
            jax.ShapeDtypeStruct((4, width), F32),
            jax.ShapeDtypeStruct((n, tile, every), BF),
        ],
        [full((tile, width))] * 2 + [full((4, width)), full((n, tile, every))],
        [
            pltpu.VMEM((len(terms), tile, width), BF),
            pltpu.VMEM((tile, width), F32),
            pltpu.VMEM((tile, width), BF),
            pltpu.VMEM((width, width), BF),
            pltpu.SemaphoreType.DMA((len(terms) + 2,)),
            pltpu.SemaphoreType.DMA((len(weights),)),
        ],
        flops=2 * tile * width * width,
    )


def first_kernel(count, at_ref, *refs):
    terms, refs = refs[:count], refs[count:]
    tokens_ref, rescot_ref, gain_ref = refs[:3]
    out_ref, sums_ref = refs[-2:]

    @pl.when(pl.program_id(0) == 0)
    def _():
        sums_ref[...] = jnp.zeros_like(sums_ref)

    first_cot = added(terms)
    unit, rate = norm_stats(tokens_ref[...].astype(F32))
    out_ref[...] = rescot_ref[...] + norm_back(first_cot, unit, rate, gain_ref[...])
    sums_ref[0:1] += row_sum(first_cot * unit)
    sums_ref[1:2] += row_sum(first_cot)


def first_back(at, b, terms, tokens, rescot, gain, held):
    batch, tile, width = tokens.shape
    part = row_part(tile)
    operands = [*terms, tokens, rescot, gain.reshape(1, width)]
    specs = [stream_rows(0, part, width)] * len(terms) + [
        stream_rows(b, part, width),
        row_block(part, width),
        full((1, width)),
    ]
    aliases = {}
    if held is not None:
        aliases = {1 + len(operands): 0}
        operands, specs = operands + [held], specs + [ANY]
    return call(
        functools.partial(first_kernel, len(terms)),
        "first_back",
        at,
        operands,
        specs,
        [jax.ShapeDtypeStruct((batch, tile, width), F32), jax.ShapeDtypeStruct((2, width), F32)],
        [stream_rows(b, part, width), full((2, width))],
        [],
        grid=tile // part,
        aliases=aliases,
    )


def result_kernel(count, at_ref, *refs):
    terms, refs = refs[:count], refs[count:]
    residual_ref, bias_ref, out_ref = refs[0], refs[1], refs[-1]
    out_ref[...] = (residual_ref[...] + added(terms) + bias_ref[...]).astype(BF)


def result_out(at, b, batch, terms, residual, bias, held):
    tile, width = residual.shape
    part = row_part(tile)
    operands = [*terms, residual, bias.reshape(1, width)]
    specs = [stream_rows(0, part, width)] * len(terms) + [row_block(part, width), full((1, width))]
    aliases = {}
    if held is not None:
        aliases = {1 + len(operands): 0}
        operands, specs = operands + [held], specs + [ANY]
    return call(
        functools.partial(result_kernel, len(terms)),
        "result_out",
        at,
        operands,
        specs,
        jax.ShapeDtypeStruct((batch, tile, width), BF),
        stream_rows(b, part, width),
        [],
        grid=tile // part,
        aliases=aliases,
    )


def tn(a, b):
    return lax.dot_general(a, b, (((0,), (0,)), ((), ())), preferred_element_type=F32)


def grad_kernel(count, products, slotted, split, row_of, at_ref, *refs):
    inputs, refs = refs[:count], refs[count:]
    outs, (a_s, b_s, acc_s, sems) = refs[:-4], refs[-4:]
    step = pl.program_id(0)
    s, f = at_ref[0], at_ref[1]
    part = acc_s.shape[1]
    width = b_s.shape[2]
    blocks = width // part
    plans, used = [], 0
    for p, (left, right) in enumerate(products):
        rows = b_s.shape[1] // len(right)
        cols = a_s.shape[2] // split
        pairs = []
        for i, (operand, lead) in enumerate(right):
            span = slice(i * rows, (i + 1) * rows)
            for c in range(split):
                o, l = left[i * split + c]
                view = inputs[o] if l is None else inputs[o].at[l]
                pairs.append((view, a_s.at[p, span, c * cols : (c + 1) * cols]))
            view = inputs[operand] if lead is None else inputs[operand].at[lead]
            pairs.append((view, b_s.at[p, span]))
        plans.append([pltpu.make_async_copy(*pair, sems.at[used + i]) for i, pair in enumerate(pairs)])
        used += len(pairs)

    @pl.when(step == 0)
    def _():
        for plan in plans:
            begin(plan)
        finish(plans[0])

    for p in range(1, len(products)):

        @pl.when(step == p * blocks)
        def _(p=p):
            finish(plans[p])

    p = step // blocks
    right = b_s[p] if blocks == 1 else b_s[p, :, lanes(step % blocks, part)]
    acc_s[...] = tn(a_s[p], right)

    if slotted:
        odd_ref, even_ref = outs
        rows = odd_ref.shape[1]
        for k in range(2 * odd_ref.shape[0]):
            target = odd_ref if k & 1 else even_ref
            target[k >> 1] = acc_s[block_rows(row_of(s, f, k), rows)].astype(BF)
    else:
        (out_ref,) = outs
        rows = out_ref.shape[1]
        for k in range(out_ref.shape[0]):
            out_ref[k] = acc_s[k * rows : (k + 1) * rows].astype(BF)


def weight_grad(at, operands, products, shards, split=1, row_of=None):
    def shape_of(view):
        return operands[view[0]].shape[-2:]

    left, right = products[0]
    tokens = sum(shape_of(v)[0] for v in right)
    height, width = shape_of(left[0])[1] * split, shape_of(right[0])[1]
    part = width if width <= 256 or width % 256 else 256
    blocks, rows = width // part, height // shards
    if row_of is not None:
        shapes = [jax.ShapeDtypeStruct((shards // 2, rows, width), BF)] * 2
        specs = [pl.BlockSpec((shards // 2, rows, part), lambda j, at: (0, 0, j))] * 2
    else:
        shapes = jax.ShapeDtypeStruct((shards, len(products), rows, width), BF)
        specs = pl.BlockSpec((shards, None, rows, part), lambda j, at: (0, j // blocks, 0, j % blocks))
    return call(
        functools.partial(grad_kernel, len(operands), products, row_of is not None, split, row_of),
        "weight_grad",
        at,
        operands,
        [ANY] * len(operands),
        shapes,
        specs,
        [
            pltpu.VMEM((len(products), tokens, height), BF),
            pltpu.VMEM((len(products), tokens, width), BF),
            pltpu.VMEM((height, part), F32),
            pltpu.SemaphoreType.DMA((sum(len(a) + len(b) for a, b in products),)),
        ],
        grid=blocks * len(products),
        flops=2 * tokens * height * width * len(products),
    )


def strip_kernel(n, batch, at_ref, *refs):
    came, branch, refs = refs[:batch], refs[batch : 2 * batch], refs[2 * batch :]
    odd_ref, even_ref, a_s, b_s, sems = refs
    step = pl.program_id(0)
    tile, every = came[0].shape[1:]
    pairs = []
    for b in range(batch):
        span = slice(b * tile, (b + 1) * tile)
        pairs += [(came[b].at[k], a_s.at[span, k * every : (k + 1) * every]) for k in range(n)]
        pairs.append((branch[b], b_s.at[span]))
    copies = copies_of(pairs, sems)

    @pl.when(step == 0)
    def _():
        begin(copies)
        finish(copies)

    strip = odd_ref.shape[1]
    found = tn(a_s[...], b_s[:, lanes(slot_at(step, n) ^ at_ref[0], strip)]).astype(BF)

    @pl.when(step < n // 2)
    def _():
        odd_ref[...] = found

    @pl.when(step >= n // 2)
    def _():
        even_ref[...] = found


def strip_grad(at, came, branch):
    n, tile, every = came[0].shape
    batch, width = len(came), branch[0].shape[1]
    half, strip = n // 2, width // n
    block = (None, n * every, strip)
    return call(
        functools.partial(strip_kernel, n, batch),
        "strip_grad",
        at,
        [*came, *branch],
        [ANY] * (2 * batch),
        [jax.ShapeDtypeStruct((half, n * every, strip), BF)] * 2,
        [
            pl.BlockSpec(block, lambda j, at: (jnp.minimum(j, half - 1), 0, 0)),
            pl.BlockSpec(block, lambda j, at: (jnp.maximum(j - half, 0), 0, 0)),
        ],
        [
            pltpu.VMEM((batch * tile, n * every), BF),
            pltpu.VMEM((batch * tile, width), BF),
            pltpu.SemaphoreType.DMA((batch * (n + 1),)),
        ],
        grid=n,
        flops=2 * batch * tile * n * every * width,
    )


def body(
    n, shards,
    tokens, first_gain, first_shift, attention_weight, attention_bias, output_weight, output_bias,
    second_gain, second_shift, expand_weight, expand_bias, contract_weight, contract_bias,
    cotangent, threshold,
):
    batch, tile, width = tokens.shape
    rows, qkv = attention_weight.shape
    every = qkv // 3
    heads = every // HEAD
    inner_rows = contract_weight.shape[0]
    inner = inner_rows * shards // n
    piece = inner_rows // n
    ratio = shards // n
    strip = output_weight.shape[1]
    s = lax.axis_index("seq").astype(jnp.int32)
    f = lax.axis_index("fsdp").astype(jnp.int32)
    at = jnp.stack([s, f])
    streams = range(batch)
    joined = piece == rows

    strips = strip % 128 == 0 and qkv % 128 == 0

    sent = jnp.concatenate([attention_weight, output_weight], axis=1) if strips else attention_weight
    qkv_slots = gather_slots(sent, "fsdp", shards)
    qkv_pieces = [(a, None, k) for k, a in enumerate(qkv_slots)]
    unit, _ = norm_stats(tokens.astype(F32))
    normed_own = (unit * first_gain + first_shift).astype(BF)
    normed_first = gather_slots(normed_own, "seq", n, qkv_slots[1:])
    expand_weight, contract_weight, *_ = lax.optimization_barrier(
        (expand_weight, contract_weight, *(qkv_slots[bit] for bit in bits_of(shards)))
    )
    to_seq = jnp.concatenate(
        [
            jnp.swapaxes(expand_weight.reshape(rows, ratio, n, piece), 1, 2)
            .swapaxes(0, 1)
            .reshape(n, -1, strip),
            contract_weight.reshape(n, piece, strip),
        ],
        axis=1,
    )
    from_seq = lax.all_to_all(to_seq, "seq", 0, 0, tiled=True)
    cut = rows * ratio * piece // strip
    expand_rows = (
        from_seq[:, :cut].reshape(n, rows, ratio * piece).swapaxes(0, 1).reshape(rows, inner)
    )
    contract_rows = from_seq[:, cut:].swapaxes(0, 1).reshape(piece, width)
    if joined:
        stacked = after(jnp.stack([expand_rows, contract_rows]), *qkv_slots[1:], normed_first[n // 2])
        hidden_weights = [lax.all_gather(stacked, "fsdp")]
    else:
        hidden_weights = [lax.all_gather(w, "fsdp") for w in (expand_rows, contract_rows)]

    mixing_bias = lax.dynamic_slice_in_dim(attention_bias, s * qkv, qkv)
    inner_bias = lax.dynamic_index_in_dim(
        expand_bias.reshape(shards, n, piece), s, axis=1, keepdims=False
    ).reshape(inner)

    parts, outs, lse, peaks, came = ([None] * batch for _ in range(5))
    residual, pairs = [None] * batch, [None] * batch
    for b in streams:
        parts[b], outs[b], lse[b], peaks[b], extra = attend_forward(
            at, b, normed_first, qkv_pieces, mixing_bias, n, strip if strips and b == 0 else 0
        )
        sent = after(outs[b], came[b - 1]) if b else outs[b]
        came[b] = lax.all_to_all(sent, "seq", 0, 0, tiled=True)
        if b == 0:
            joint = extra
            cot_first = gather_slots(after(cotangent[0], normed_first[n // 2]), "seq", n, outs[:1])
    if strips:
        output_weights = gather_slots(after(joint[0], cot_first[n // 2]), "seq", n, outs[-1:])
    else:
        output_weights = [
            lax.all_gather(
                lax.all_gather(output_weight, "fsdp", tiled=True), "seq", axis=1, tiled=True
            )
        ]
    normed_own = [None] * batch
    for b in streams:
        residual[b], normed_own[b] = project(
            at, b, came[b], output_weights, tokens, output_bias, second_gain, second_shift,
            cotangent if b else None,
        )
    cot_pairs = [None] * batch
    for b in streams:
        if b == 0:
            own = gather_slots(after(normed_own[b], came[-1]), "seq", n, normed_own[-1:])
            pairs[b] = [(a, None, k) for k, a in enumerate(own)]
            cot_pairs[b] = [(a, None, k) for k, a in enumerate(cot_first)]
        else:
            own = gather_slots(after(normed_own[b], pairs[b - 1][n // 2][0]), "seq", n)
            pairs[b] = [(a, 0, k) for k, a in enumerate(own)]
            cot_pairs[b] = [(a, 1, k) for k, a in enumerate(own)]

    active, hidden_cot, inner_sums, rescot, branch, sums, cots = ([None] * batch for _ in range(7))
    second, out_parts, terms = [], [], None
    for b in streams:
        operands = list(pairs[b])
        if b:
            array = after(operands[0][0], second[-1][0])
            operands[0] = (array, *operands[0][1:])
        active[b], hidden_cot[b], odd, even, *out_part, inner_sums[b] = hidden_layer(
            at, operands, cot_pairs[b], hidden_weights, inner_bias
        )
        out_parts.append(out_part)
        odd = after(odd, second_terms[-1][-1] if b else pairs[-1][n // 2][0])
        if b == 0:
            second_terms = []
        second.append(scatter_near(odd, even, "seq", n))
        second_terms.append(scatter_far(*second[b], "seq", n))

    def second_step(b, *others):
        terms = second_terms[b]
        if others:
            terms[0] = after(terms[0], *others)
        rescot[b], branch[b], sums[b], slots = second_back(
            at, b, terms, output_weights, residual[b], cotangent, second_gain, n
        )
        cots[b] = lax.all_to_all(slots, "seq", 0, 0, tiled=True)

    second_step(0)

    def by_slot(first):
        return [(first + k, b) for b in streams for k in range(n)]

    def by_stream(first):
        return [(first + b, k) for b in streams for k in range(n)]

    def owned(s, f, k):
        return f ^ k

    arrays, views = arrays_of([v for b in streams for v in (*pairs[b], *cot_pairs[b])])
    views = [view[:2] for view in views]
    normed_views = [v for b in streams for v in views[2 * b * n : (2 * b + 1) * n]]
    cot_views = [v for b in streams for v in views[(2 * b + 1) * n : 2 * (b + 1) * n]]
    far = len(arrays)
    if joined:
        arrays[0] = after(arrays[0], second[-1][0], branch[0])
        both = weight_grad(
            at,
            [*arrays, *hidden_cot, *active],
            [(normed_views, by_stream(far)), (by_stream(far + batch), cot_views)],
            shards,
        )
        scattered = [lax.psum_scatter(after(both, cots[0], second_terms[-1][-1]), "fsdp")]
        done = [both]
    else:
        grad_expand = scatter_sum(
            *weight_grad(
                at, [*arrays, *hidden_cot], [(normed_views, by_stream(far))], shards, 1, owned
            ),
            "fsdp",
            shards,
        )
        grad_contract = scatter_sum(
            *weight_grad(at, [*arrays, *active], [(by_stream(far), cot_views)], shards, 1, owned),
            "fsdp",
            shards,
        )
        scattered, done = [grad_expand, grad_contract], []
    for b in streams[1:]:
        second_step(b, *done, cots[b - 1])
    cots[0] = after(cots[0], *done, branch[-1])

    mixed_cot, mixing_sums, tail = [None] * batch, [None] * batch, [None] * batch
    input_grad = None
    near, block_output = None, None
    out_terms = [None] * batch
    first_terms = []
    for b in streams:
        cot = cots[b]
        if b == 0:
            out_near = scatter_near(after(out_parts[b][0], branch[0]), out_parts[b][1], "seq", n)
            cot = after(cot, out_near[0])
            out_terms[b] = scatter_far(*out_near, "seq", n)
        else:
            cot = after(cot, near[0], output_odd)
        mixed_cot[b], odd, even, mixing_sums[b] = attend_backward(
            at, parts[b], lse[b], outs[b], cot, qkv_pieces
        )
        odd = after(odd, out_terms[0][-1], terms[-1] if b else cots[-1])
        near = scatter_near(odd, even, "seq", n)
        terms = scatter_far(*near, "seq", n)
        first_terms.append(terms)
        if b == 0:
            if strips:
                output_odd, output_even = strip_grad(at, [after(came[0], mixed_cot[0]), *came[1:]], branch)
            else:
                product = functools.reduce(
                    jnp.add,
                    [
                        jnp.einsum("kte,td->ked", came[b], branch[b], preferred_element_type=F32)
                        for b in streams
                    ],
                ).reshape(width, n, strip)
                output_odd, output_even = (
                    jnp.stack(
                        [
                            lax.dynamic_index_in_dim(product, s ^ k, 1, keepdims=False).astype(BF)
                            for k in range(first, n, 2)
                        ]
                    )
                    for first in (1, 0)
                )
        if b == batch - 1:
            grad_parts = weight_grad(
                at,
                [after(normed_first[0], near[0]), *normed_first[1:], *mixed_cot],
                [(by_slot(0), by_stream(n))],
                shards,
                1,
                owned,
            )
    for b in streams:
        first_terms[b][0] = after(first_terms[b][0], grad_parts[0])
        input_grad, tail[b] = first_back(
            at, b, first_terms[b], tokens, rescot[b], first_gain, input_grad
        )
    for b in streams[1:]:
        out_near = scatter_near(after(out_parts[b][0], near[0]), out_parts[b][1], "seq", n)
        out_terms[b] = scatter_far(after(out_near[0], terms[-1]), *out_near[1:], "seq", n)
    def over_streams(values):
        return functools.reduce(jnp.add, values)

    mine = jnp.arange(n) == s
    spread_inner = jnp.where(
        mine[None, :, None], over_streams(inner_sums).reshape(shards, 1, piece), 0.0
    )
    spread_mixing = jnp.where(mine[:, None], over_streams(mixing_sums), 0.0)
    peak = jnp.where(mine[:, None], functools.reduce(jnp.maximum, peaks)[None], -jnp.inf)
    top = jnp.pad(peak.reshape(-1), (0, 1024 - n * heads)).reshape(-1, 128)
    vectors = jnp.concatenate(
        [top]
        + [
            v.reshape(-1, 128)
            for v in (over_streams(sums), over_streams(tail), spread_inner, spread_mixing)
        ]
    )
    is_top = jnp.arange(vectors.shape[0])[:, None] < top.shape[0]

    def summed(vectors, axis, size, bits):
        for bit in bits:
            other = swap(vectors, axis, size, bit)
            vectors = jnp.where(is_top, jnp.maximum(vectors, other), vectors + other)
        return vectors

    near_bit, far_bits = bits_of(shards)[0], bits_of(shards)[1:]
    vectors = summed(vectors, "fsdp", shards, far_bits)
    output_near = scatter_near(output_odd, output_even, "seq", n)
    output_terms = scatter_far(*output_near, "seq", n)
    output_terms[-1] = after(output_terms[-1], grad_parts[0])
    output = functools.reduce(jnp.add, [a[0].astype(F32) for a in output_terms])
    order = [*far_bits, near_bit]
    kept, other, left = scatter_half(
        output.reshape(*[2] * len(order), rows, strip), f, "fsdp", shards, order[0],
        bits_of(shards)[::-1],
    )
    held = {}

    def first_step(came):
        came, *held["hidden"] = lax.optimization_barrier((came, *scattered))
        first = summed(after(vectors, came), "fsdp", shards, [near_bit])
        first = summed(first, "seq", n, bits_of(n)[:-1])
        held["vectors"] = first, swap(first, "seq", n, bits_of(n)[-1])
        for b in streams[:-1]:
            out_terms[b][0] = after(out_terms[b][0], came)
        held["output"] = scatter_half(
            kept + after(other, came).astype(F32), f, "fsdp", shards, order[1], left
        )
        return came

    def second_step_over(came):
        came, *held["hidden"] = lax.optimization_barrier((came, *held["hidden"]))
        first, last = held["vectors"]
        last = after(last, came)
        held["vectors"] = jnp.where(is_top, jnp.maximum(first, last), first + last)
        kept, other, left = held["output"]
        held["output"] = kept, after(other, came), left
        out_terms[-1][0] = after(out_terms[-1][0], came)
        return came

    grad_mixing = scatter_sum(*grad_parts, "fsdp", shards, [first_step, second_step_over])
    for b in streams:
        block_output = result_out(
            at, b, batch, out_terms[b], residual[b], contract_bias, block_output
        )
    vectors, (kept, other, left) = held["vectors"], held["output"]
    for bit in order[2:]:
        kept, other, left = scatter_half(
            kept + other.astype(F32), f, "fsdp", shards, bit, left
        )
    grad_output_own = kept + other.astype(F32)
    grad_expand, grad_contract = held["hidden"][0] if joined else held["hidden"]
    back = lax.all_to_all(
        jnp.concatenate(
            [
                grad_expand.astype(BF)
                .reshape(rows, n, ratio * piece)
                .swapaxes(0, 1)
                .reshape(n, cut, strip),
                grad_contract.astype(BF).reshape(piece, n, strip).swapaxes(0, 1),
            ],
            axis=1,
        ),
        "seq",
        0,
        0,
        tiled=True,
    )
    grad_expand_own = (
        back[:, :cut]
        .reshape(n, rows, ratio, piece)
        .transpose(1, 2, 0, 3)
        .reshape(rows, ratio * n * piece)
        .astype(F32)
    )
    grad_contract_own = back[:, cut:].reshape(inner_rows, strip).astype(F32)
    vectors = vectors.reshape(-1)
    ends = [1024]
    for length in [width] * 6 + [n * inner, n * qkv]:
        ends.append(ends[-1] + length)
    (
        second_gain_sum, second_shift_sum, output_sum, contract_sum, first_gain_sum, first_shift_sum,
        inner_sum, mixing_sum,
    ) = (vectors[a:b] for a, b in zip(ends, ends[1:]))

    head_peak = lax.dynamic_slice_in_dim(vectors, s * heads, heads)
    factor = jnp.sqrt(threshold[0] / jnp.maximum(head_peak, threshold[0]))
    multiplier = jnp.broadcast_to(
        jnp.stack([factor, factor, jnp.ones_like(factor)], axis=1)[:, :, None], (heads, 3, HEAD)
    ).reshape(qkv)
    clipped_weight = attention_weight.astype(F32) * multiplier[None, :]
    clipped_bias = mixing_bias * multiplier

    return (
        block_output,
        input_grad,
        first_gain_sum,
        first_shift_sum,
        grad_mixing,
        mixing_sum,
        grad_output_own,
        output_sum,
        second_gain_sum,
        second_shift_sum,
        grad_expand_own,
        inner_sum,
        grad_contract_own,
        contract_sum,
        head_peak,
        clipped_weight,
        clipped_bias,
    )


def solution(mesh):
    grid, both, whole, line = P("fsdp", "seq"), P("fsdp", "seq", None), P(), P("seq")
    return jax.shard_map(
        functools.partial(body, mesh.shape["seq"], mesh.shape["fsdp"]),
        mesh=mesh,
        in_specs=(
            both, whole, whole, grid, whole, grid, whole, whole, whole, grid, whole, grid, whole,
            both, whole,
        ),
        out_specs=(
            both, both, whole, whole, grid, whole, grid, whole, whole, whole, grid, whole, grid,
            whole, line, grid, line,
        ),
        check_vma=False,
    )
```

```python
import functools
import math

import jax
import jax.numpy as jnp
from jax import lax
from jax.experimental import pallas as pl
from jax.experimental.pallas import tpu as pltpu
from jax.sharding import PartitionSpec as P

HEAD = 64
LOG2E = math.log2(math.e)
BF = jnp.bfloat16
F32 = jnp.float32
ANY = pl.BlockSpec(memory_space=pl.ANY)


def swap(value, axis, size, bit):
    return lax.ppermute(value, axis, [(i, i ^ bit) for i in range(size)])


def bits_of(size):
    return [1 << p for p in range(size.bit_length() - 1)]


def gather_slots(value, axis, size, wait=()):
    slots = {0: value}
    for bit in reversed(bits_of(size)):
        for k in list(slots):
            sent = after(slots[k], *wait) if k and wait else slots[k]
            slots[k | bit] = swap(sent, axis, size, bit)
    return [slots[k] for k in range(size)]


def scatter_near(odd, even, axis, size):
    came = swap(odd, axis, size, 1)
    total = even.astype(F32) + came.astype(F32)
    return total[1::2].astype(BF), total[0::2], [even, came]


def scatter_far(sent, rest, terms, axis, size):
    terms = list(terms)
    for bit in bits_of(size)[1:]:
        came = swap(sent, axis, size, bit)
        terms.append(came)
        if came.shape[0] > 1:
            rest = rest + came.astype(F32)
            sent, rest = rest[1::2].astype(BF), rest[0::2]
    return terms


def scatter_sum(odd, even, axis, size, hooks=()):
    rest, sent = even.astype(F32), odd
    for step, bit in enumerate(bits_of(size)):
        came = swap(sent, axis, size, bit)
        if step < len(hooks):
            came = hooks[step](came)
        rest = rest + came.astype(F32)
        if rest.shape[0] > 1:
            sent, rest = rest[1::2].astype(BF), rest[0::2]
    return rest[0]


def scatter_half(value, index, axis, size, bit, left):
    at = left.index(bit)
    own = ((index & bit) != 0).astype(jnp.int32)
    sent = lax.dynamic_index_in_dim(value, 1 - own, at, keepdims=False).astype(BF)
    kept = lax.dynamic_index_in_dim(value, own, at, keepdims=False).astype(F32)
    return kept, swap(sent, axis, size, bit), [b for b in left if b != bit]


def after(value, *others):
    return lax.optimization_barrier((value, *others))[0]


def nn(a, b):
    return lax.dot_general(a, b, (((1,), (0,)), ((), ())), preferred_element_type=F32)


def nt(a, b):
    return lax.dot_general(a, b, (((1,), (1,)), ((), ())), preferred_element_type=F32)


def full(shape):
    return pl.BlockSpec(shape, lambda i, at: (0,) * len(shape))


def entry(shape, at_entry=0):
    return pl.BlockSpec((None, *shape), lambda i, at: (at_entry,) + (0,) * len(shape))


def call(kernel, name, at, operands, in_specs, out_shape, out_specs, scratch, grid=1, flops=0, aliases=None):
    moved = sum(math.prod(o.shape) * o.dtype.itemsize for o in operands)
    return pl.pallas_call(
        kernel,
        out_shape=out_shape,
        grid_spec=pltpu.PrefetchScalarGridSpec(
            num_scalar_prefetch=1,
            grid=(grid,),
            in_specs=in_specs,
            out_specs=out_specs,
            scratch_shapes=scratch,
        ),
        compiler_params=pltpu.CompilerParams(vmem_limit_bytes=58 << 20),
        cost_estimate=pl.CostEstimate(flops=flops, transcendentals=0, bytes_accessed=moved),
        input_output_aliases=aliases or {},
        name=name,
    )(at, *operands)


def copies_of(pairs, sems):
    return [pltpu.make_async_copy(src, dst, sems.at[i]) for i, (src, dst) in enumerate(pairs)]


def begin(copies):
    for copy in copies:
        copy.start()


def finish(copies):
    for copy in copies:
        copy.wait()


def block_rows(index, rows):
    return pl.ds(pl.multiple_of(index * rows, rows), rows)


def weight_pairs(refs, views, target, f, start=0):
    rows = target.shape[0] // len(views)
    pairs = []
    for i, lead, slot in views:
        source = refs[i] if lead is None else refs[i].at[lead]
        if source.shape[-1] > target.shape[-1]:
            source = source.at[:, start : start + target.shape[-1]]
        pairs.append((source, target.at[block_rows(f ^ slot, rows)]))
    return pairs


def arrays_of(views):
    arrays, found = [], []
    for array, lead, slot in views:
        place = next((i for i, a in enumerate(arrays) if a is array), len(arrays))
        if place == len(arrays):
            arrays.append(array)
        found.append((place, lead, slot))
    return arrays, found


def head_mask(width, head):
    return (lax.broadcasted_iota(jnp.int32, (1, width), 1) // HEAD) == head


def causal(tile):
    keys = lax.broadcasted_iota(jnp.int32, (tile, tile), 0)
    queries = lax.broadcasted_iota(jnp.int32, (tile, tile), 1)
    return keys <= queries


def lanes(group, width):
    return pl.ds(pl.multiple_of(group * width, width), width)


def join(parts, axis):
    return parts[0] if len(parts) == 1 else jnp.concatenate(parts, axis=axis)


def forward_kernel(n, b, views, count, at_ref, *refs):
    normed, refs = refs[:n], refs[n:]
    pieces, refs = refs[:count], refs[count:]
    bias_ref, q_ref, k_ref, v_ref, o_ref, lse_ref, peak_ref = refs[:7]
    x_s, w_s, vt_s, x_sems, w_sems, e_sems = refs[-6:]
    s, f = at_ref[0], at_ref[1]
    _, tile, _ = x_s.shape
    extra = []
    if len(refs) == 14:
        extra = copies_of(weight_pairs(pieces, views, refs[7], f, w_s.shape[1]), e_sems)
    every = q_ref.shape[1]
    width = 128 if every % 128 == 0 else every
    heads, factor = width // HEAD, HEAD**-0.5 * LOG2E
    w_copies = copies_of(weight_pairs(pieces, views, w_s, f), w_sems)
    x_copies = copies_of([(normed[k].at[b], x_s.at[k]) for k in range(n)], x_sems)
    begin(w_copies)
    begin(x_copies)
    begin(extra)
    finish(w_copies)
    finish(x_copies)

    @pl.loop(0, n)
    def _(k):
        mixed = (nn(x_s[k], w_s[...]) + bias_ref[...]).astype(BF)
        spot = block_rows(k ^ s, tile)
        parts = [
            join([mixed[:, (3 * h + j) * HEAD : (3 * h + j + 1) * HEAD] for h in range(every // HEAD)], 1)
            for j in range(3)
        ]
        q_ref[spot], k_ref[spot], v_ref[spot] = parts
        vt_s[:, spot] = parts[2].T

    @pl.loop(0, every // width)
    def _(g):
        cols = lanes(g, width)
        peaks = [None] * heads
        for i in range(n):
            q_tile = q_ref[i * tile : (i + 1) * tile, cols]
            limit = (i + 1) * tile
            step = min(limit, 4 * tile)
            outs = []
            for h in range(heads):
                q = jnp.where(head_mask(width, h), q_tile, jnp.zeros_like(q_tile))
                v_rows = pl.ds(pl.multiple_of(g * width + h * HEAD, HEAD), HEAD)
                top = total = acc = None
                for start in range(0, limit, step):
                    stop = min(start + step, limit)
                    found = nt(k_ref[start:stop, cols], q)
                    if stop == limit:
                        edge = stop - start - tile
                        masked = jnp.where(causal(tile), found[edge:], -jnp.inf)
                        found = masked if edge == 0 else jnp.concatenate([found[:edge], masked], axis=0)
                    high = jnp.max(found, axis=0, keepdims=True)
                    new_top = high if top is None else jnp.maximum(top, high)
                    grown = jnp.exp2((found - new_top) * factor)
                    part = jnp.sum(grown, axis=0, keepdims=True)
                    mixed = nn(vt_s[v_rows, start:stop], grown.astype(BF))
                    if top is None:
                        total, acc = part, mixed
                    else:
                        shrink = jnp.exp2((top - new_top) * factor)
                        total, acc = total * shrink + part, acc * shrink + mixed
                    top = new_top
                outs.append(acc / total)
                lse_ref[g, h : h + 1, i * tile : (i + 1) * tile] = top * factor + jnp.log2(total)
                peaks[h] = top if peaks[h] is None else jnp.maximum(peaks[h], top)
            o_ref[i, :, cols] = join(outs, 0).T.astype(BF)
        for h in range(heads):
            peak_ref[g, h : h + 1, :] = peaks[h] * HEAD**-0.5

    finish(extra)


def attend_forward(at, b, normed, pieces, bias, n, strip=0):
    _, tile, width = normed[0].shape
    arrays, views = arrays_of(pieces)
    qkv = bias.shape[0]
    every, length = qkv // 3, n * tile
    group = 128 if every % 128 == 0 else every
    part = jax.ShapeDtypeStruct((length, every), BF)
    stats = [(every // group, group // HEAD, length), (every // group, group // HEAD, tile)]
    found = call(
        functools.partial(forward_kernel, n, b, views, len(arrays)),
        "attend_forward",
        at,
        [*normed, *arrays, bias.reshape(1, qkv)],
        [ANY] * (n + len(arrays)) + [full((1, qkv))],
        [part] * 3
        + [jax.ShapeDtypeStruct((n, tile, every), BF)]
        + [jax.ShapeDtypeStruct(shape, F32) for shape in stats]
        + ([jax.ShapeDtypeStruct((width, strip), BF)] if strip else []),
        [full((length, every))] * 3
        + [full((n, tile, every))]
        + [full(shape) for shape in stats]
        + ([full((width, strip))] if strip else []),
        [
            pltpu.VMEM((n, tile, width), BF),
            pltpu.VMEM((width, qkv), BF),
            pltpu.VMEM((every, length), BF),
            pltpu.SemaphoreType.DMA((n,)),
            pltpu.SemaphoreType.DMA((len(views),)),
            pltpu.SemaphoreType.DMA((len(views),)),
        ],
        flops=2 * length * width * qkv + 8 * length * length * every,
    )
    parts, (out, lse, peak), extra = found[:3], found[3:6], found[6:]
    return parts, out, lse, jnp.max(peak, axis=-1).reshape(-1), extra


def backward_kernel(n, views, count, at_ref, *refs):
    q_ref, k_ref, v_ref, lse_ref, o_ref, g_ref = refs[:6]
    pieces, refs = refs[6 : 6 + count], refs[6 + count :]
    mix_ref, odd_ref, even_ref, bias_ref, w_s, kt_s, dq_s, dk_s, dv_s, mix_s, w_sems = refs
    s, f = at_ref[0], at_ref[1]
    _, tile, qkv = mix_ref.shape
    every, scale = qkv // 3, HEAD**-0.5
    width = 128 if every % 128 == 0 else every
    heads, factor = width // HEAD, scale * LOG2E
    w_copies = copies_of(weight_pairs(pieces, views, w_s, f), w_sems)
    begin(w_copies)
    kt_s[...] = k_ref[...].T

    @pl.loop(0, every // width)
    def _(g):
        cols = lanes(g, width)
        for i in reversed(range(n)):
            rows = slice(i * tile, (i + 1) * tile)
            limit = (i + 1) * tile
            step = min(limit, 4 * tile)
            q_tile, g_tile = q_ref[rows, cols], g_ref[i, :, cols]
            inner = (g_tile.astype(F32) * o_ref[i, :, cols].astype(F32)).T
            outs = []
            for h in range(heads):
                mask = head_mask(width, h)
                q = jnp.where(mask, q_tile, jnp.zeros_like(q_tile))
                cot = jnp.where(mask, g_tile, jnp.zeros_like(g_tile))
                delta = jnp.sum(inner[h * HEAD : (h + 1) * HEAD], axis=0, keepdims=True)
                lse = lse_ref[g, h : h + 1, rows]
                k_rows = pl.ds(pl.multiple_of(g * width + h * HEAD, HEAD), HEAD)
                acc = None
                for start in range(0, limit, step):
                    stop = min(start + step, limit)
                    probs = jnp.exp2(nt(k_ref[start:stop, cols], q) * factor - lse)
                    if stop == limit:
                        edge = stop - start - tile
                        masked = jnp.where(causal(tile), probs[edge:], 0.0)
                        probs = masked if edge == 0 else jnp.concatenate([probs[:edge], masked], axis=0)
                    spread = nt(v_ref[start:stop, cols], cot)
                    logit_cot = (probs * (spread - delta)).astype(BF)
                    dv_part = nn(probs.astype(BF), cot)
                    dk_part = nn(logit_cot, q)
                    if i == n - 1 and h == 0:
                        dv_s[start:stop] = dv_part
                        dk_s[start:stop] = dk_part
                    else:
                        dv_s[start:stop] += dv_part
                        dk_s[start:stop] += dk_part
                    dq_part = nn(kt_s[k_rows, start:stop], logit_cot)
                    acc = dq_part if acc is None else acc + dq_part
                outs.append(acc)
            dq_s[rows] = (join(outs, 0).T * scale).astype(BF)
        for i in range(n):
            rows = slice(i * tile, (i + 1) * tile)
            dq = dq_s[rows]
            dk = (dk_s[rows] * scale).astype(BF)
            dv = dv_s[rows].astype(BF)
            mix_s[rows, lanes(g, 3 * width)] = jnp.concatenate(
                [a[:, h * HEAD : (h + 1) * HEAD] for h in range(heads) for a in (dq, dk, dv)], axis=1
            )

    finish(w_copies)
    bias_ref[...] = jnp.zeros_like(bias_ref)

    @pl.loop(0, n // 2)
    def _(j):
        for k, target in ((2 * j, even_ref), (2 * j + 1, odd_ref)):
            mixed_cot = mix_s[block_rows(k ^ s, tile)]
            mix_ref[k] = mixed_cot
            bias_ref[...] += row_sum(mixed_cot.astype(F32))
            target[j] = nt(mixed_cot, w_s[...]).astype(BF)


def attend_backward(at, parts, lse, out, cot, pieces):
    n, tile, every = out.shape
    length, qkv = n * tile, 3 * every
    arrays, views = arrays_of(pieces)
    width = len(views) * arrays[0].shape[-2]
    group = 128 if every % 128 == 0 else every
    half = (n // 2, tile, width)
    return call(
        functools.partial(backward_kernel, n, views, len(arrays)),
        "attend_backward",
        at,
        [*parts, lse, out, cot, *arrays],
        [full((length, every))] * 3
        + [full(lse.shape)]
        + [full((n, tile, every))] * 2
        + [ANY] * len(arrays),
        [
            jax.ShapeDtypeStruct((n, tile, qkv), BF),
            jax.ShapeDtypeStruct(half, BF),
            jax.ShapeDtypeStruct(half, BF),
            jax.ShapeDtypeStruct((1, qkv), F32),
        ],
        [full((n, tile, qkv)), full(half), full(half), full((1, qkv))],
        [
            pltpu.VMEM((width, qkv), BF),
            pltpu.VMEM((every, length), BF),
            pltpu.VMEM((length, group), BF),
            pltpu.VMEM((length, group), F32),
            pltpu.VMEM((length, group), F32),
            pltpu.VMEM((length, qkv), BF),
            pltpu.SemaphoreType.DMA((len(views),)),
        ],
        flops=2 * length * width * qkv + 20 * length * length * every,
    )


def norm_stats(values):
    centered = values - jnp.mean(values, axis=-1, keepdims=True)
    rate = lax.rsqrt(jnp.mean(centered * centered, axis=-1, keepdims=True) + 1e-05)
    return centered * rate, rate


def norm_back(cot, unit, rate, gain):
    e = cot * gain
    return rate * (
        e
        - jnp.mean(e, axis=-1, keepdims=True)
        - unit * jnp.mean(e * unit, axis=-1, keepdims=True)
    )


def column_copies(refs, target, s, sems):
    strip = refs[0].shape[1]
    if len(refs) == 1:
        return copies_of([(refs[0], target)], sems)
    return copies_of([(ref, target.at[:, lanes(k ^ s, strip)]) for k, ref in enumerate(refs)], sems)


def project_kernel(count, paired, at_ref, *refs):
    came_ref, weights, refs = refs[0], refs[1 : 1 + count], refs[1 + count :]
    tokens_ref, bias_ref, gain_ref, shift_ref = refs[:4]
    residual_ref, normed_ref, c_s, w_s, c_sem, w_sems = refs[-6:]
    if paired:
        normed_ref[1] = refs[4][...]
        normed_ref = normed_ref.at[0]
    n, _, every = came_ref.shape
    copy = pltpu.make_async_copy(came_ref, c_s, c_sem)
    weights = column_copies(weights, w_s, at_ref[0], w_sems)
    copy.start()
    begin(weights)
    total = tokens_ref[...].astype(F32) + bias_ref[...]
    copy.wait()
    finish(weights)
    for k in range(n):
        total = total + nn(c_s[k], w_s[k * every : (k + 1) * every])
    residual_ref[...] = total
    unit, _ = norm_stats(total)
    normed_ref[...] = (unit * gain_ref[...] + shift_ref[...]).astype(BF)


def project(at, b, came, weights, tokens, bias, gain, shift, cotangent=None):
    _, tile, width = tokens.shape
    n, _, every = came.shape
    row, block = full((1, width)), entry((tile, width), b)
    paired = cotangent is not None
    shape = (2, tile, width) if paired else (tile, width)
    return call(
        functools.partial(project_kernel, len(weights), paired),
        "project",
        at,
        [came, *weights, tokens, *(v.reshape(1, width) for v in (bias, gain, shift))]
        + ([cotangent] if paired else []),
        [ANY] * (1 + len(weights)) + [block, row, row, row] + ([block] if paired else []),
        [jax.ShapeDtypeStruct((tile, width), F32), jax.ShapeDtypeStruct(shape, BF)],
        [full((tile, width)), full(shape)],
        [
            pltpu.VMEM((n, tile, every), BF),
            pltpu.VMEM((width, width), BF),
            pltpu.SemaphoreType.DMA,
            pltpu.SemaphoreType.DMA((len(weights),)),
        ],
        flops=2 * tile * width * width,
    )


def gelu_pair(v):
    k0 = math.sqrt(2.0 / math.pi)
    square = v * v
    t = jnp.tanh(v * (k0 + (k0 * 0.044715) * square))
    half = 0.5 + 0.5 * t
    slope = half + (0.5 * v) * (1.0 - t * t) * (k0 + (3.0 * 0.044715 * k0) * square)
    return v * half, slope


def slot_at(step, n):
    half = n // 2
    return jnp.where(step < half, 2 * step + 1, 2 * (step - half))


def hidden_kernel(n, views, arrays, count, at_ref, *refs):
    inputs, refs = refs[:arrays], refs[arrays:]
    found = [inputs[i] if lead is None else inputs[i].at[lead] for i, lead, _ in views]
    normed, cots = found[:n], found[n:]
    weights_in, refs = refs[:count], refs[count:]
    bias_ref = refs[0]
    active_ref, cot_ref, odd_ref, even_ref, out_odd_ref, out_even_ref, sum_ref = refs[1:8]
    x_s, c_s, expand_s, contract_s, x_sems, c_sems, w_sems = refs[8:]
    step = pl.program_id(0)
    k = slot_at(step, n)
    shards, inner = weights_in[0].shape[0], expand_s.shape[1]
    first = [weights_in[0].at[i, 0] if count == 1 else weights_in[0].at[i] for i in range(shards)]
    second = [weights_in[0].at[i, 1] if count == 1 else weights_in[1].at[i] for i in range(shards)]
    e_rows, c_rows = expand_s.shape[0] // shards, contract_s.shape[0] // shards
    order = list(range(1, n, 2)) + list(range(0, n, 2))
    x_copies = copies_of([(normed[j], x_s.at[j]) for j in order], x_sems)
    c_copies = copies_of([(cots[j], c_s.at[j]) for j in order], c_sems)
    weights = copies_of(
        [(a, expand_s.at[i * e_rows : (i + 1) * e_rows]) for i, a in enumerate(first)]
        + [(a, contract_s.at[i * c_rows : (i + 1) * c_rows]) for i, a in enumerate(second)],
        w_sems,
    )

    @pl.when(step == 0)
    def _():
        begin(x_copies[:1] + weights[:shards] + c_copies[:1] + weights[shards:])
        begin(x_copies[1:] + c_copies[1:])
        sum_ref[...] = jnp.zeros_like(sum_ref)

    for j in range(n):

        @pl.when(step == j)
        def _(j=j):
            if j == 0:
                finish(weights)
            x_copies[j].wait()
            c_copies[j].wait()

    part = min(inner, 512)
    x, c = x_s[k], c_s[k]

    @pl.loop(0, inner // part)
    def _(i):
        cols = lanes(i, part)
        hidden = nn(x, expand_s[:, cols]) + bias_ref[:, cols]
        value, slope = gelu_pair(hidden)
        active_ref[:, cols] = value.astype(BF)
        hidden_cot = (nt(c, contract_s[block_rows(i, part)]) * slope).astype(BF)
        cot_ref[:, cols] = hidden_cot
        sum_ref[:, cols] += row_sum(hidden_cot.astype(F32))

    partial = nt(cot_ref[...], expand_s[...]).astype(BF)
    out = nn(active_ref[...], contract_s[...]).astype(BF)

    @pl.when(step < n // 2)
    def _():
        odd_ref[...] = partial
        out_odd_ref[...] = out

    @pl.when(step >= n // 2)
    def _():
        even_ref[...] = partial
        out_even_ref[...] = out


def hidden_layer(at, normed, cots, weights, bias):
    n = len(normed)
    arrays, views = arrays_of([*normed, *cots])
    tile, width = arrays[0].shape[-2:]
    inner = bias.shape[0]
    shards = weights[0].shape[0]
    half = n // 2
    slot = pl.BlockSpec((None, tile, inner), lambda j, at: (slot_at(j, n), 0, 0))
    early = lambda j: jnp.minimum(j, half - 1)
    later = lambda j: jnp.maximum(j - half, 0)
    pair = jax.ShapeDtypeStruct((half, tile, width), BF)
    wide = jax.ShapeDtypeStruct((n, tile, inner), BF)
    operands = [*arrays, *weights, bias.reshape(1, inner)]
    specs = [ANY] * (len(arrays) + len(weights)) + [full((1, inner))]
    near = pl.BlockSpec((None, tile, width), lambda j, at: (early(j), 0, 0))
    kept = pl.BlockSpec((None, tile, width), lambda j, at: (later(j), 0, 0))
    return call(
        functools.partial(hidden_kernel, n, views, len(arrays), len(weights)),
        "hidden_layer",
        at,
        operands,
        specs,
        [wide, wide, pair, pair, pair, pair, jax.ShapeDtypeStruct((1, inner), F32)],
        [
            slot,
            slot,
            near,
            kept,
            near,
            kept,
            full((1, inner)),
        ],
        [
            pltpu.VMEM((n, tile, width), BF),
            pltpu.VMEM((n, tile, width), BF),
            pltpu.VMEM((width, inner), BF),
            pltpu.VMEM((inner, width), BF),
            pltpu.SemaphoreType.DMA((n,)),
            pltpu.SemaphoreType.DMA((n,)),
            pltpu.SemaphoreType.DMA((2 * shards,)),
        ],
        grid=n,
        flops=8 * n * tile * width * inner,
    )


def added(terms):
    total = terms[0][...].astype(F32)
    for term in terms[1:]:
        total = total + term[...].astype(F32)
    return total


def row_sum(values):
    return jnp.sum(values, axis=0, keepdims=True)


def second_kernel(b, terms_in, count, at_ref, *refs):
    terms, refs = refs[:terms_in], refs[terms_in:]
    weights, refs = refs[:count], refs[count:]
    residual_ref, cot_ref, gain_ref = refs[:3]
    rescot_ref, branch_ref, sums_ref, out_ref, t_s, r_s, c_s, w_s, sems, w_sems = refs[3:]
    copies = copies_of(
        [(residual_ref, r_s), (cot_ref.at[b], c_s)]
        + [(term.at[0], t_s.at[i]) for i, term in enumerate(terms)],
        sems,
    )
    weights = column_copies(weights, w_s, at_ref[0], w_sems)
    begin(copies)
    begin(weights)
    finish(copies)
    second_cot = added([t_s.at[i] for i in range(terms_in)])
    unit, rate = norm_stats(r_s[...])
    cot = c_s[...].astype(F32)
    residual_cot = cot + norm_back(second_cot, unit, rate, gain_ref[...])
    rescot_ref[...] = residual_cot
    branch = residual_cot.astype(BF)
    branch_ref[...] = branch
    sums_ref[0:1] = row_sum(second_cot * unit)
    sums_ref[1:2] = row_sum(second_cot)
    sums_ref[2:3] = row_sum(branch.astype(F32))
    sums_ref[3:4] = row_sum(cot)
    finish(weights)
    n, _, every = out_ref.shape
    for k in range(n):
        out_ref[k] = nt(branch, w_s[k * every : (k + 1) * every]).astype(BF)


def row_part(tile):
    return tile // 2


def stream_rows(b, part, width):
    return pl.BlockSpec((None, part, width), lambda i, at: (b, i, 0))


def row_block(part, width):
    return pl.BlockSpec((part, width), lambda i, at: (i, 0))


def second_back(at, b, terms, weights, residual, cotangent, gain, n):
    tile, width = residual.shape
    every = width // n
    return call(
        functools.partial(second_kernel, b, len(terms), len(weights)),
        "second_back",
        at,
        [*terms, *weights, residual, cotangent, gain.reshape(1, width)],
        [ANY] * (len(terms) + len(weights) + 2) + [full((1, width))],
        [
            jax.ShapeDtypeStruct((tile, width), F32),
            jax.ShapeDtypeStruct((tile, width), BF),
            jax.ShapeDtypeStruct((4, width), F32),
            jax.ShapeDtypeStruct((n, tile, every), BF),
        ],
        [full((tile, width))] * 2 + [full((4, width)), full((n, tile, every))],
        [
            pltpu.VMEM((len(terms), tile, width), BF),
            pltpu.VMEM((tile, width), F32),
            pltpu.VMEM((tile, width), BF),
            pltpu.VMEM((width, width), BF),
            pltpu.SemaphoreType.DMA((len(terms) + 2,)),
            pltpu.SemaphoreType.DMA((len(weights),)),
        ],
        flops=2 * tile * width * width,
    )


def first_kernel(count, at_ref, *refs):
    terms, refs = refs[:count], refs[count:]
    tokens_ref, rescot_ref, gain_ref = refs[:3]
    out_ref, sums_ref = refs[-2:]

    @pl.when(pl.program_id(0) == 0)
    def _():
        sums_ref[...] = jnp.zeros_like(sums_ref)

    first_cot = added(terms)
    unit, rate = norm_stats(tokens_ref[...].astype(F32))
    out_ref[...] = rescot_ref[...] + norm_back(first_cot, unit, rate, gain_ref[...])
    sums_ref[0:1] += row_sum(first_cot * unit)
    sums_ref[1:2] += row_sum(first_cot)


def first_back(at, b, terms, tokens, rescot, gain, held):
    batch, tile, width = tokens.shape
    part = row_part(tile)
    operands = [*terms, tokens, rescot, gain.reshape(1, width)]
    specs = [stream_rows(0, part, width)] * len(terms) + [
        stream_rows(b, part, width),
        row_block(part, width),
        full((1, width)),
    ]
    aliases = {}
    if held is not None:
        aliases = {1 + len(operands): 0}
        operands, specs = operands + [held], specs + [ANY]
    return call(
        functools.partial(first_kernel, len(terms)),
        "first_back",
        at,
        operands,
        specs,
        [jax.ShapeDtypeStruct((batch, tile, width), F32), jax.ShapeDtypeStruct((2, width), F32)],
        [stream_rows(b, part, width), full((2, width))],
        [],
        grid=tile // part,
        aliases=aliases,
    )


def result_kernel(count, at_ref, *refs):
    terms, refs = refs[:count], refs[count:]
    residual_ref, bias_ref, out_ref = refs[0], refs[1], refs[-1]
    out_ref[...] = (residual_ref[...] + added(terms) + bias_ref[...]).astype(BF)


def result_out(at, b, batch, terms, residual, bias, held):
    tile, width = residual.shape
    part = row_part(tile)
    operands = [*terms, residual, bias.reshape(1, width)]
    specs = [stream_rows(0, part, width)] * len(terms) + [row_block(part, width), full((1, width))]
    aliases = {}
    if held is not None:
        aliases = {1 + len(operands): 0}
        operands, specs = operands + [held], specs + [ANY]
    return call(
        functools.partial(result_kernel, len(terms)),
        "result_out",
        at,
        operands,
        specs,
        jax.ShapeDtypeStruct((batch, tile, width), BF),
        stream_rows(b, part, width),
        [],
        grid=tile // part,
        aliases=aliases,
    )


def tn(a, b):
    return lax.dot_general(a, b, (((0,), (0,)), ((), ())), preferred_element_type=F32)


def grad_kernel(count, products, slotted, split, row_of, at_ref, *refs):
    inputs, refs = refs[:count], refs[count:]
    outs, (a_s, b_s, acc_s, sems) = refs[:-4], refs[-4:]
    step = pl.program_id(0)
    s, f = at_ref[0], at_ref[1]
    part = acc_s.shape[1]
    width = b_s.shape[2]
    blocks = width // part
    plans, used = [], 0
    for p, (left, right) in enumerate(products):
        rows = b_s.shape[1] // len(right)
        cols = a_s.shape[2] // split
        pairs = []
        for i, (operand, lead) in enumerate(right):
            span = slice(i * rows, (i + 1) * rows)
            for c in range(split):
                o, l = left[i * split + c]
                view = inputs[o] if l is None else inputs[o].at[l]
                pairs.append((view, a_s.at[p, span, c * cols : (c + 1) * cols]))
            view = inputs[operand] if lead is None else inputs[operand].at[lead]
            pairs.append((view, b_s.at[p, span]))
        plans.append([pltpu.make_async_copy(*pair, sems.at[used + i]) for i, pair in enumerate(pairs)])
        used += len(pairs)

    @pl.when(step == 0)
    def _():
        for plan in plans:
            begin(plan)
        finish(plans[0])

    for p in range(1, len(products)):

        @pl.when(step == p * blocks)
        def _(p=p):
            finish(plans[p])

    p = step // blocks
    right = b_s[p] if blocks == 1 else b_s[p, :, lanes(step % blocks, part)]
    acc_s[...] = tn(a_s[p], right)

    if slotted:
        odd_ref, even_ref = outs
        rows = odd_ref.shape[1]
        for k in range(2 * odd_ref.shape[0]):
            target = odd_ref if k & 1 else even_ref
            target[k >> 1] = acc_s[block_rows(row_of(s, f, k), rows)].astype(BF)
    else:
        (out_ref,) = outs
        rows = out_ref.shape[1]
        for k in range(out_ref.shape[0]):
            out_ref[k] = acc_s[k * rows : (k + 1) * rows].astype(BF)


def weight_grad(at, operands, products, shards, split=1, row_of=None):
    def shape_of(view):
        return operands[view[0]].shape[-2:]

    left, right = products[0]
    tokens = sum(shape_of(v)[0] for v in right)
    height, width = shape_of(left[0])[1] * split, shape_of(right[0])[1]
    part = width if width <= 256 or width % 256 else 256
    blocks, rows = width // part, height // shards
    if row_of is not None:
        shapes = [jax.ShapeDtypeStruct((shards // 2, rows, width), BF)] * 2
        specs = [pl.BlockSpec((shards // 2, rows, part), lambda j, at: (0, 0, j))] * 2
    else:
        shapes = jax.ShapeDtypeStruct((shards, len(products), rows, width), BF)
        specs = pl.BlockSpec((shards, None, rows, part), lambda j, at: (0, j // blocks, 0, j % blocks))
    return call(
        functools.partial(grad_kernel, len(operands), products, row_of is not None, split, row_of),
        "weight_grad",
        at,
        operands,
        [ANY] * len(operands),
        shapes,
        specs,
        [
            pltpu.VMEM((len(products), tokens, height), BF),
            pltpu.VMEM((len(products), tokens, width), BF),
            pltpu.VMEM((height, part), F32),
            pltpu.SemaphoreType.DMA((sum(len(a) + len(b) for a, b in products),)),
        ],
        grid=blocks * len(products),
        flops=2 * tokens * height * width * len(products),
    )


def strip_kernel(n, batch, at_ref, *refs):
    came, branch, refs = refs[:batch], refs[batch : 2 * batch], refs[2 * batch :]
    odd_ref, even_ref, a_s, b_s, sems = refs
    step = pl.program_id(0)
    tile, every = came[0].shape[1:]
    pairs = []
    for b in range(batch):
        span = slice(b * tile, (b + 1) * tile)
        pairs += [(came[b].at[k], a_s.at[span, k * every : (k + 1) * every]) for k in range(n)]
        pairs.append((branch[b], b_s.at[span]))
    copies = copies_of(pairs, sems)

    @pl.when(step == 0)
    def _():
        begin(copies)
        finish(copies)

    strip = odd_ref.shape[1]
    found = tn(a_s[...], b_s[:, lanes(slot_at(step, n) ^ at_ref[0], strip)]).astype(BF)

    @pl.when(step < n // 2)
    def _():
        odd_ref[...] = found

    @pl.when(step >= n // 2)
    def _():
        even_ref[...] = found


def strip_grad(at, came, branch):
    n, tile, every = came[0].shape
    batch, width = len(came), branch[0].shape[1]
    half, strip = n // 2, width // n
    block = (None, n * every, strip)
    return call(
        functools.partial(strip_kernel, n, batch),
        "strip_grad",
        at,
        [*came, *branch],
        [ANY] * (2 * batch),
        [jax.ShapeDtypeStruct((half, n * every, strip), BF)] * 2,
        [
            pl.BlockSpec(block, lambda j, at: (jnp.minimum(j, half - 1), 0, 0)),
            pl.BlockSpec(block, lambda j, at: (jnp.maximum(j - half, 0), 0, 0)),
        ],
        [
            pltpu.VMEM((batch * tile, n * every), BF),
            pltpu.VMEM((batch * tile, width), BF),
            pltpu.SemaphoreType.DMA((batch * (n + 1),)),
        ],
        grid=n,
        flops=2 * batch * tile * n * every * width,
    )


def body(
    n, shards,
    tokens, first_gain, first_shift, attention_weight, attention_bias, output_weight, output_bias,
    second_gain, second_shift, expand_weight, expand_bias, contract_weight, contract_bias,
    cotangent, threshold,
):
    batch, tile, width = tokens.shape
    rows, qkv = attention_weight.shape
    every = qkv // 3
    heads = every // HEAD
    inner_rows = contract_weight.shape[0]
    inner = inner_rows * shards // n
    piece = inner_rows // n
    ratio = shards // n
    strip = output_weight.shape[1]
    s = lax.axis_index("seq").astype(jnp.int32)
    f = lax.axis_index("fsdp").astype(jnp.int32)
    at = jnp.stack([s, f])
    streams = range(batch)
    joined = piece == rows

    strips = strip % 128 == 0 and qkv % 128 == 0

    sent = jnp.concatenate([attention_weight, output_weight], axis=1) if strips else attention_weight
    qkv_slots = gather_slots(sent, "fsdp", shards)
    qkv_pieces = [(a, None, k) for k, a in enumerate(qkv_slots)]
    unit, _ = norm_stats(tokens.astype(F32))
    normed_own = (unit * first_gain + first_shift).astype(BF)
    normed_first = gather_slots(normed_own, "seq", n, qkv_slots[1:])
    expand_weight, contract_weight, *_ = lax.optimization_barrier(
        (expand_weight, contract_weight, *(qkv_slots[bit] for bit in bits_of(shards)))
    )
    to_seq = jnp.concatenate(
        [
            jnp.swapaxes(expand_weight.reshape(rows, ratio, n, piece), 1, 2)
            .swapaxes(0, 1)
            .reshape(n, -1, strip),
            contract_weight.reshape(n, piece, strip),
        ],
        axis=1,
    )
    from_seq = lax.all_to_all(to_seq, "seq", 0, 0, tiled=True)
    cut = rows * ratio * piece // strip
    expand_rows = (
        from_seq[:, :cut].reshape(n, rows, ratio * piece).swapaxes(0, 1).reshape(rows, inner)
    )
    contract_rows = from_seq[:, cut:].swapaxes(0, 1).reshape(piece, width)
    if joined:
        stacked = after(jnp.stack([expand_rows, contract_rows]), *qkv_slots[1:], normed_first[n // 2])
        hidden_weights = [lax.all_gather(stacked, "fsdp")]
    else:
        hidden_weights = [lax.all_gather(w, "fsdp") for w in (expand_rows, contract_rows)]

    mixing_bias = lax.dynamic_slice_in_dim(attention_bias, s * qkv, qkv)
    inner_bias = lax.dynamic_index_in_dim(
        expand_bias.reshape(shards, n, piece), s, axis=1, keepdims=False
    ).reshape(inner)

    parts, outs, lse, peaks, came = ([None] * batch for _ in range(5))
    residual, pairs = [None] * batch, [None] * batch
    for b in streams:
        parts[b], outs[b], lse[b], peaks[b], extra = attend_forward(
            at, b, normed_first, qkv_pieces, mixing_bias, n, strip if strips and b == 0 else 0
        )
        sent = after(outs[b], came[b - 1]) if b else outs[b]
        came[b] = lax.all_to_all(sent, "seq", 0, 0, tiled=True)
        if b == 0:
            joint = extra
            cot_first = gather_slots(after(cotangent[0], normed_first[n // 2]), "seq", n, outs[:1])
    if strips:
        output_weights = gather_slots(after(joint[0], cot_first[n // 2]), "seq", n, outs[-1:])
    else:
        output_weights = [
            lax.all_gather(
                lax.all_gather(output_weight, "fsdp", tiled=True), "seq", axis=1, tiled=True
            )
        ]
    normed_own = [None] * batch
    for b in streams:
        residual[b], normed_own[b] = project(
            at, b, came[b], output_weights, tokens, output_bias, second_gain, second_shift,
            cotangent if b else None,
        )
    cot_pairs = [None] * batch
    for b in streams:
        if b == 0:
            own = gather_slots(after(normed_own[b], came[-1]), "seq", n, normed_own[-1:])
            pairs[b] = [(a, None, k) for k, a in enumerate(own)]
            cot_pairs[b] = [(a, None, k) for k, a in enumerate(cot_first)]
        else:
            own = gather_slots(after(normed_own[b], pairs[b - 1][n // 2][0]), "seq", n)
            pairs[b] = [(a, 0, k) for k, a in enumerate(own)]
            cot_pairs[b] = [(a, 1, k) for k, a in enumerate(own)]

    active, hidden_cot, inner_sums, rescot, branch, sums, cots = ([None] * batch for _ in range(7))
    second, out_parts, terms = [], [], None
    for b in streams:
        operands = list(pairs[b])
        if b:
            array = after(operands[0][0], second[-1][0])
            operands[0] = (array, *operands[0][1:])
        active[b], hidden_cot[b], odd, even, *out_part, inner_sums[b] = hidden_layer(
            at, operands, cot_pairs[b], hidden_weights, inner_bias
        )
        out_parts.append(out_part)
        odd = after(odd, second_terms[-1][-1] if b else pairs[-1][n // 2][0])
        if b == 0:
            second_terms = []
        second.append(scatter_near(odd, even, "seq", n))
        second_terms.append(scatter_far(*second[b], "seq", n))

    def second_step(b, *others):
        terms = second_terms[b]
        if others:
            terms[0] = after(terms[0], *others)
        rescot[b], branch[b], sums[b], slots = second_back(
            at, b, terms, output_weights, residual[b], cotangent, second_gain, n
        )
        cots[b] = lax.all_to_all(slots, "seq", 0, 0, tiled=True)

    second_step(0)

    def by_slot(first):
        return [(first + k, b) for b in streams for k in range(n)]

    def by_stream(first):
        return [(first + b, k) for b in streams for k in range(n)]

    def owned(s, f, k):
        return f ^ k

    arrays, views = arrays_of([v for b in streams for v in (*pairs[b], *cot_pairs[b])])
    views = [view[:2] for view in views]
    normed_views = [v for b in streams for v in views[2 * b * n : (2 * b + 1) * n]]
    cot_views = [v for b in streams for v in views[(2 * b + 1) * n : 2 * (b + 1) * n]]
    far = len(arrays)
    if joined:
        arrays[0] = after(arrays[0], second[-1][0], branch[0])
        both = weight_grad(
            at,
            [*arrays, *hidden_cot, *active],
            [(normed_views, by_stream(far)), (by_stream(far + batch), cot_views)],
            shards,
        )
        scattered = [lax.psum_scatter(after(both, cots[0], second_terms[-1][-1]), "fsdp")]
        done = [both]
    else:
        grad_expand = scatter_sum(
            *weight_grad(
                at, [*arrays, *hidden_cot], [(normed_views, by_stream(far))], shards, 1, owned
            ),
            "fsdp",
            shards,
        )
        grad_contract = scatter_sum(
            *weight_grad(at, [*arrays, *active], [(by_stream(far), cot_views)], shards, 1, owned),
            "fsdp",
            shards,
        )
        scattered, done = [grad_expand, grad_contract], []
    for b in streams[1:]:
        second_step(b, *done, cots[b - 1])
    cots[0] = after(cots[0], *done, branch[-1])

    mixed_cot, mixing_sums, tail = [None] * batch, [None] * batch, [None] * batch
    input_grad = None
    near, block_output = None, None
    out_terms = [None] * batch
    first_terms = []
    for b in streams:
        cot = cots[b]
        if b == 0:
            out_near = scatter_near(after(out_parts[b][0], branch[0]), out_parts[b][1], "seq", n)
            cot = after(cot, out_near[0])
            out_terms[b] = scatter_far(*out_near, "seq", n)
        else:
            cot = after(cot, near[0], output_odd)
        mixed_cot[b], odd, even, mixing_sums[b] = attend_backward(
            at, parts[b], lse[b], outs[b], cot, qkv_pieces
        )
        odd = after(odd, out_terms[0][-1], terms[-1] if b else cots[-1])
        near = scatter_near(odd, even, "seq", n)
        terms = scatter_far(*near, "seq", n)
        first_terms.append(terms)
        if b == 0:
            if strips:
                output_odd, output_even = strip_grad(at, [after(came[0], mixed_cot[0]), *came[1:]], branch)
            else:
                product = functools.reduce(
                    jnp.add,
                    [
                        jnp.einsum("kte,td->ked", came[b], branch[b], preferred_element_type=F32)
                        for b in streams
                    ],
                ).reshape(width, n, strip)
                output_odd, output_even = (
                    jnp.stack(
                        [
                            lax.dynamic_index_in_dim(product, s ^ k, 1, keepdims=False).astype(BF)
                            for k in range(first, n, 2)
                        ]
                    )
                    for first in (1, 0)
                )
        if b == batch - 1:
            grad_parts = weight_grad(
                at,
                [after(normed_first[0], near[0]), *normed_first[1:], *mixed_cot],
                [(by_slot(0), by_stream(n))],
                shards,
                1,
                owned,
            )
    for b in streams:
        first_terms[b][0] = after(first_terms[b][0], grad_parts[0])
        input_grad, tail[b] = first_back(
            at, b, first_terms[b], tokens, rescot[b], first_gain, input_grad
        )
    for b in streams[1:]:
        out_near = scatter_near(after(out_parts[b][0], near[0]), out_parts[b][1], "seq", n)
        out_terms[b] = scatter_far(after(out_near[0], terms[-1]), *out_near[1:], "seq", n)
    def over_streams(values):
        return functools.reduce(jnp.add, values)

    mine = jnp.arange(n) == s
    spread_inner = jnp.where(
        mine[None, :, None], over_streams(inner_sums).reshape(shards, 1, piece), 0.0
    )
    spread_mixing = jnp.where(mine[:, None], over_streams(mixing_sums), 0.0)
    peak = jnp.where(mine[:, None], functools.reduce(jnp.maximum, peaks)[None], -jnp.inf)
    top = jnp.pad(peak.reshape(-1), (0, 1024 - n * heads)).reshape(-1, 128)
    vectors = jnp.concatenate(
        [top]
        + [
            v.reshape(-1, 128)
            for v in (over_streams(sums), over_streams(tail), spread_inner, spread_mixing)
        ]
    )
    is_top = jnp.arange(vectors.shape[0])[:, None] < top.shape[0]

    def summed(vectors, axis, size, bits):
        for bit in bits:
            other = swap(vectors, axis, size, bit)
            vectors = jnp.where(is_top, jnp.maximum(vectors, other), vectors + other)
        return vectors

    near_bit, far_bits = bits_of(shards)[0], bits_of(shards)[1:]
    vectors = summed(vectors, "fsdp", shards, far_bits)
    output_near = scatter_near(output_odd, output_even, "seq", n)
    output_terms = scatter_far(*output_near, "seq", n)
    output_terms[-1] = after(output_terms[-1], grad_parts[0])
    output = functools.reduce(jnp.add, [a[0].astype(F32) for a in output_terms])
    order = [*far_bits, near_bit]
    kept, other, left = scatter_half(
        output.reshape(*[2] * len(order), rows, strip), f, "fsdp", shards, order[0],
        bits_of(shards)[::-1],
    )
    held = {}

    def first_step(came):
        came, *held["hidden"] = lax.optimization_barrier((came, *scattered))
        first = summed(after(vectors, came), "fsdp", shards, [near_bit])
        first = summed(first, "seq", n, bits_of(n)[:-1])
        held["vectors"] = first, swap(first, "seq", n, bits_of(n)[-1])
        for b in streams[:-1]:
            out_terms[b][0] = after(out_terms[b][0], came)
        held["output"] = scatter_half(
            kept + after(other, came).astype(F32), f, "fsdp", shards, order[1], left
        )
        return came

    def second_step_over(came):
        came, *held["hidden"] = lax.optimization_barrier((came, *held["hidden"]))
        first, last = held["vectors"]
        last = after(last, came)
        held["vectors"] = jnp.where(is_top, jnp.maximum(first, last), first + last)
        kept, other, left = held["output"]
        held["output"] = kept, after(other, came), left
        out_terms[-1][0] = after(out_terms[-1][0], came)
        return came

    grad_mixing = scatter_sum(*grad_parts, "fsdp", shards, [first_step, second_step_over])
    for b in streams:
        block_output = result_out(
            at, b, batch, out_terms[b], residual[b], contract_bias, block_output
        )
    vectors, (kept, other, left) = held["vectors"], held["output"]
    for bit in order[2:]:
        kept, other, left = scatter_half(
            kept + other.astype(F32), f, "fsdp", shards, bit, left
        )
    grad_output_own = kept + other.astype(F32)
    grad_expand, grad_contract = held["hidden"][0] if joined else held["hidden"]
    back = lax.all_to_all(
        jnp.concatenate(
            [
                grad_expand.astype(BF)
                .reshape(rows, n, ratio * piece)
                .swapaxes(0, 1)
                .reshape(n, cut, strip),
                grad_contract.astype(BF).reshape(piece, n, strip).swapaxes(0, 1),
            ],
            axis=1,
        ),
        "seq",
        0,
        0,
        tiled=True,
    )
    grad_expand_own = (
        back[:, :cut]
        .reshape(n, rows, ratio, piece)
        .transpose(1, 2, 0, 3)
        .reshape(rows, ratio * n * piece)
        .astype(F32)
    )
    grad_contract_own = back[:, cut:].reshape(inner_rows, strip).astype(F32)
    vectors = vectors.reshape(-1)
    ends = [1024]
    for length in [width] * 6 + [n * inner, n * qkv]:
        ends.append(ends[-1] + length)
    (
        second_gain_sum, second_shift_sum, output_sum, contract_sum, first_gain_sum, first_shift_sum,
        inner_sum, mixing_sum,
    ) = (vectors[a:b] for a, b in zip(ends, ends[1:]))

    head_peak = lax.dynamic_slice_in_dim(vectors, s * heads, heads)
    factor = jnp.sqrt(threshold[0] / jnp.maximum(head_peak, threshold[0]))
    multiplier = jnp.broadcast_to(
        jnp.stack([factor, factor, jnp.ones_like(factor)], axis=1)[:, :, None], (heads, 3, HEAD)
    ).reshape(qkv)
    clipped_weight = attention_weight.astype(F32) * multiplier[None, :]
    clipped_bias = mixing_bias * multiplier

    return (
        block_output,
        input_grad,
        first_gain_sum,
        first_shift_sum,
        grad_mixing,
        mixing_sum,
        grad_output_own,
        output_sum,
        second_gain_sum,
        second_shift_sum,
        grad_expand_own,
        inner_sum,
        grad_contract_own,
        contract_sum,
        head_peak,
        clipped_weight,
        clipped_bias,
    )


def solution(mesh):
    grid, both, whole, line = P("fsdp", "seq"), P("fsdp", "seq", None), P(), P("seq")
    return jax.shard_map(
        functools.partial(body, mesh.shape["seq"], mesh.shape["fsdp"]),
        mesh=mesh,
        in_specs=(
            both, whole, whole, grid, whole, grid, whole, whole, whole, grid, whole, grid, whole,
            both, whole,
        ),
        out_specs=(
            both, both, whole, whole, grid, whole, grid, whole, whole, whole, grid, whole, grid,
            whole, line, grid, line,
        ),
        check_vma=False,
    )
```
